32 devices in a mesh: seq: 16 (over z, x, core), head: 2 (over y).
Axes of the slice: x: 2, y: 2, z: 4, core: 2. Of those that a mesh axis runs over, the one named last changes fastest.
Arguments:
- query_rows: bfloat16 [8192, 1024], P(('seq', 'head')), may hold values from -16 to 16
- key_rows: bfloat16 [8192, 1024], P(('seq', 'head')), may hold values from -16 to 16
- value_rows: bfloat16 [8192, 1024], P(('seq', 'head')), may hold values from -6 to 6
- out_grad: bfloat16 [8192, 1024], P(('seq', 'head')), may hold values from -6 to 6
- random_blocks: int32 [128, 2], P('seq'), may hold values from 0 to 127, as said below
- global_blocks: int32 [2], replicated, may hold values from 0 to 127
Outputs:
- attn_out: bfloat16 [8192, 1024], P(('seq', 'head'))
- q_grad: bfloat16 [8192, 1024], P(('seq', 'head'))
- k_grad: bfloat16 [8192, 1024], P(('seq', 'head'))
- v_grad: bfloat16 [8192, 1024], P(('seq', 'head'))
The draws below stay inside these ranges and needn't reach their ends.
Inputs may be any that keep to these rules, and one draw needn't show every extreme that they name: `random_blocks`: the 16 random blocks named by the query blocks of one device belong to 16 different devices along `seq`: at most one of them lies among any one device's 8 blocks.
All inputs are finite; a program needn't handle non-finite values.
Results may differ from the reference program's by a relative error of at most 0.011.
Values may be sent and summed in bfloat16 or wider, within the bound.
A program may use at most 128 MiB of HBM per device.

```python
import jax
import jax.numpy as jnp
from jax import lax

HEADS = 16
HEAD_DIM = 64
BLOCK = 64
RANDOM = 2
GLOBALS = 2
BLK_DEV = 8
SEQLEN = 8192
NBLK = 128
CAP = 1
N_SEQ = 16


def draw_query_rows(key, part):
    noise = jax.random.normal(jax.random.fold_in(key, 11), (SEQLEN, HEADS, HEAD_DIM), jnp.float32)
    values_drawn = jnp.clip(noise, -6.0, 6.0)
    return jnp.clip(values_drawn, -16.0, 16.0).reshape(SEQLEN, HEADS * HEAD_DIM).astype(jnp.bfloat16)


def draw_key_rows(key, part):
    noise = jax.random.normal(jax.random.fold_in(key, 13), (SEQLEN, HEADS, HEAD_DIM), jnp.float32)
    values_drawn = jnp.clip(noise, -6.0, 6.0)
    return jnp.clip(values_drawn, -16.0, 16.0).reshape(SEQLEN, HEADS * HEAD_DIM).astype(jnp.bfloat16)


def draw_random_blocks(key, part):
    slot_total = N_SEQ * CAP
    per_device = RANDOM * BLK_DEV
    device_keys = jax.random.split(jax.random.fold_in(key, 3), N_SEQ)

    def one_device(device_key):
        order = jax.random.permutation(jax.random.fold_in(device_key, 1), slot_total)[:per_device]
        source = order // CAP
        within = jax.random.randint(jax.random.fold_in(device_key, 2), (per_device,), 0, BLK_DEV)
        return (source * BLK_DEV + within).astype(jnp.int32)
    return jax.vmap(one_device)(device_keys).reshape(NBLK, RANDOM).astype(jnp.int32)


def block_levels(key, shape, pieces, smallest, high):
    loudness, own = 1.0, jax.random.fold_in(key, 6)
    for dim, parts in pieces:
        steps = jnp.exp(jax.random.uniform(jax.random.fold_in(own, dim), (parts,), jnp.float32, smallest / len(pieces), high / len(pieces)))
        loudness = loudness * jnp.repeat(steps, shape[dim] // parts).reshape([-1 if axis == dim else 1 for axis in range(len(shape))])
    return loudness


def gaussian(key, dims, width, bound, pieces=(), kind=jnp.bfloat16):
    drawn = width * jax.random.normal(key, dims, jnp.float32)
    if pieces:
        drawn = drawn * block_levels(key, dims, pieces, -0.22, 0.18)
    return jnp.clip(drawn, -bound, bound).astype(kind)


def setup_inputs(seed: int = 0) -> dict:
    streams_of = jax.random.split(jax.random.key(seed), 7)
    query_rows = draw_query_rows(jax.random.fold_in(streams_of[6], 71), 0)
    key_rows = draw_key_rows(jax.random.fold_in(streams_of[6], 71), 0)
    value_rows = gaussian(streams_of[2], (SEQLEN, HEADS * HEAD_DIM), 1.0, 6.0, ((0, 32),))
    out_grad = gaussian(streams_of[3], (SEQLEN, HEADS * HEAD_DIM), 1.0, 6.0, ((0, 32),))
    random_blocks = draw_random_blocks(jax.random.fold_in(streams_of[6], 71), 0)
    global_blocks = jax.random.randint(streams_of[5], (GLOBALS,), 0, NBLK).astype(jnp.int32)
    return dict(query_rows=query_rows, key_rows=key_rows, value_rows=value_rows, out_grad=out_grad, random_blocks=random_blocks, global_blocks=global_blocks)


masked_score = -1e30


def heads_first(matrix):
    return matrix.reshape(matrix.shape[0], HEADS, HEAD_DIM).transpose(1, 0, 2).astype(jnp.float32)


def heads_last(tensor):
    return tensor.transpose(1, 0, 2).reshape(tensor.shape[1], HEADS * HEAD_DIM)


def halfway(tensor):
    return lax.optimization_barrier(tensor.astype(jnp.bfloat16)).astype(jnp.float32)


def reference(query_rows, key_rows, value_rows, out_grad, random_blocks, global_blocks):
    full_width = HEADS * HEAD_DIM
    scale_factor = HEAD_DIM ** -0.5
    part_count = 3 + RANDOM + GLOBALS
    empty_block = jnp.zeros((1, BLOCK, full_width), jnp.bfloat16)
    key_padded = jnp.concatenate([empty_block, key_rows.reshape(NBLK, BLOCK, full_width), empty_block], axis=0)
    value_padded = jnp.concatenate([empty_block, value_rows.reshape(NBLK, BLOCK, full_width), empty_block], axis=0)
    query_blocks = query_rows.reshape(NBLK, BLOCK, full_width)
    grad_blocks = out_grad.reshape(NBLK, BLOCK, full_width)
    part_iota = jnp.arange(part_count, dtype=jnp.int32)
    random_part = (part_iota >= 3) & (part_iota < 3 + RANDOM)

    def one_block(carry, which):
        key_sum, value_sum = carry
        picked_ids = jnp.concatenate([which + jnp.arange(3, dtype=jnp.int32), random_blocks[which].astype(jnp.int32) + 1, global_blocks.astype(jnp.int32) + 1]).astype(jnp.int32)
        part_ok = jnp.ones((part_count,), jnp.bool_).at[0].set(which > 0).at[2].set(which < NBLK - 1)
        key_ok = jnp.repeat(part_ok, BLOCK)
        query_heads = heads_first(query_blocks[which])
        grad_heads = heads_first(grad_blocks[which])
        key_heads = heads_first(key_padded[picked_ids].reshape(part_count * BLOCK, full_width))
        value_heads = heads_first(value_padded[picked_ids].reshape(part_count * BLOCK, full_width))
        scores = jnp.einsum("hqd,hkd->hqk", query_heads, key_heads) * scale_factor
        scores = jnp.where(key_ok[None, None, :], scores, masked_score)
        row_max = jnp.max(scores, axis=-1, keepdims=True)
        weights_raw = jnp.exp(scores - row_max)
        probabilities = weights_raw / jnp.sum(weights_raw, axis=-1, keepdims=True)
        probs_half = halfway(probabilities)
        attended = jnp.einsum("hqk,hkd->hqd", probs_half, value_heads)
        prob_grad = jnp.einsum("hqd,hkd->hqk", grad_heads, value_heads)
        row_delta = jnp.sum(grad_heads * attended, axis=-1, keepdims=True)
        score_grad = halfway(probabilities * (prob_grad - row_delta))
        query_grad = jnp.einsum("hqk,hkd->hqd", score_grad, key_heads) * scale_factor
        key_grad = heads_last(jnp.einsum("hqk,hqd->hkd", score_grad, query_heads) * scale_factor).reshape(part_count, BLOCK, full_width)
        value_grad = heads_last(jnp.einsum("hqk,hqd->hkd", probs_half, grad_heads)).reshape(part_count, BLOCK, full_width)
        key_grad = jnp.where(random_part[:, None, None], halfway(key_grad), key_grad)
        value_grad = jnp.where(random_part[:, None, None], halfway(value_grad), value_grad)
        key_sum = key_sum.at[picked_ids].add(key_grad)
        value_sum = value_sum.at[picked_ids].add(value_grad)
        return (key_sum, value_sum), (heads_last(attended).astype(jnp.bfloat16), heads_last(query_grad).astype(jnp.bfloat16))

    start_sum = jnp.zeros((NBLK + 2, BLOCK, full_width), jnp.float32)
    (key_sum, value_sum), (attended_all, query_all) = lax.scan(one_block, (start_sum, start_sum), jnp.arange(NBLK, dtype=jnp.int32))
    attn_out = attended_all.reshape(SEQLEN, full_width)
    q_grad = query_all.reshape(SEQLEN, full_width)
    k_grad = key_sum[1:NBLK + 1].reshape(SEQLEN, full_width).astype(jnp.bfloat16)
    v_grad = value_sum[1:NBLK + 1].reshape(SEQLEN, full_width).astype(jnp.bfloat16)
    return (attn_out, q_grad, k_grad, v_grad)
```

```python
from functools import partial

import jax
import jax.numpy as jnp
from jax import lax
from jax.experimental import pallas as pl
from jax.experimental.pallas import tpu as pltpu
from jax.sharding import PartitionSpec as P

HEAD_DIM = 64
BLOCK = 64
RANDOM = 2
GLOBALS = 2
PARTS = 3 + RANDOM + GLOBALS
MASKED = -1e30
MESH = pl.DeviceIdType.MESH
VMEM = pl.BlockSpec(memory_space=pltpu.VMEM)
HBM = pl.BlockSpec(memory_space=pltpu.HBM)
SMEM = pl.BlockSpec(memory_space=pltpu.SMEM)


def params(cid):
    return pltpu.CompilerParams(
        collective_id=cid, has_side_effects=True, vmem_limit_bytes=24 * 1024 * 1024
    )


def greet(n, heads):
    s, h = lax.axis_index("seq"), lax.axis_index("head")
    barrier = pltpu.get_barrier_semaphore()
    if n > 0:

        def hello(d, c):
            pl.semaphore_signal(
                barrier, inc=1, device_id={"seq": lax.rem(s + d, n)}, device_id_type=MESH
            )
            return c

        lax.fori_loop(1, n, hello, 0)
    for d in range(1, heads):
        pl.semaphore_signal(
            barrier, inc=1, device_id={"head": lax.rem(h + d, heads)}, device_id_type=MESH
        )
    pl.semaphore_wait(barrier, max(n - 1, 0) + heads - 1)


def cols(index, width, base=0):
    return pl.ds(pl.multiple_of(base + index * width, 128), width)


def rows(index, count):
    return pl.ds(pl.multiple_of(index * count, 16), count)


def each(n, f):
    def step(d, c):
        f(d)
        return c

    lax.fori_loop(1, n, step, 0)


def remote(src, dst, send, recv, **where):
    return pltpu.make_async_remote_copy(
        src_ref=src, dst_ref=dst, send_sem=send, recv_sem=recv, device_id=where,
        device_id_type=MESH,
    )


def exchange(view, heads, send, recv, local, base):
    h = lax.axis_index("head")
    copies = []
    for d in range(1, heads):
        peer = lax.rem(h + d, heads)
        source, target = view(h, peer)
        at = base * heads + d
        copies.append(remote(source, target, send.at[at], recv.at[at], head=peer))
    source, target = view(h, h)
    return copies + [pltpu.make_async_copy(source, target, local.at[base])]


def start(copies):
    for c in copies:
        c.start()


def wait(copies):
    for c in copies:
        c.wait()


def to_heads(src, dst, tokens, width):
    return lambda a, b: (src.at[:, cols(b, width)], dst.at[rows(a, tokens), :])


def piece_in(src, dst, width, offset, size):
    nt = src.shape[0]
    return lambda a, b: (
        src.at[:, :, pl.ds(pl.multiple_of(b * width + offset, 128), size)],
        dst.at[pl.ds(a * nt, nt)],
    )


def to_tokens(src, dst, tokens, width):
    return lambda a, b: (src.at[rows(b, tokens), :], dst.at[:, cols(a, width)])


def piece_out(src, dst, tokens, width, offset, size, base):
    return lambda a, b: (
        src.at[rows(b, tokens), pl.ds(base, size)],
        dst.at[:, pl.ds(pl.multiple_of(a * width + offset, 128), size)],
    )


def kernel_in(n, heads, size, key, ids, pair, ids_all, send, recv, local, isend, irecv):
    s = lax.axis_index("seq")
    greet(n, heads)
    copies = exchange(
        piece_in(key, pair, key.shape[2] // heads, 0, size), heads, send, recv, local, 0
    )

    def idc(d):
        return remote(ids, ids_all.at[s], isend.at[d], irecv.at[d], seq=lax.rem(s + d, n))

    mine = pltpu.make_async_copy(ids, ids_all.at[s], local.at[1])
    start(copies)
    each(n, lambda d: idc(d).start())
    mine.start()
    each(n, lambda d: idc(d).wait())
    mine.wait()
    wait(copies)


def halo(n, low, high, got, send, recv, at=0):
    s = lax.axis_index("seq")
    up, down = 2 * at, 2 * at + 1
    here = pl.ds(at * low.shape[1], low.shape[1])
    return [
        remote(high, got.at[0, :, here], send.at[up], recv.at[up], seq=lax.rem(s + 1, n)),
        remote(low, got.at[1, :, here], send.at[down], recv.at[down], seq=lax.rem(s + n - 1, n)),
    ]


def far_first(n, make):
    def go(i, c):
        make(n // 2 + ((i + 1) // 2) * (2 * lax.rem(i, 2) - 1)).start()
        return c

    lax.fori_loop(0, n - 1, go, 0)


def random_piece(n, c, src_of, dst, size, send, recv):
    s = lax.axis_index("seq")

    def make(d):
        peer = lax.rem(s + d, n)
        return remote(
            src_of(peer), dst.at[s, :, pl.ds(c * size, size)], send.at[c * n + d],
            recv.at[c * n + d], seq=peer,
        )

    return make


class Shared:
    def __init__(self, n, src, here, mine, layer, done, every, sems):
        s = lax.axis_index("seq")
        gs, gr, ls, lr, fs, fr, loc = sems
        self.group = group = src.shape[0]
        self.layers = n // group
        self.me, self.level = lax.rem(s, group), s // group
        self.mine, self.layer, self.done, self.every, self.here = mine, layer, done, every, here
        self.step1 = [pltpu.make_async_copy(src.at[self.me], here.at[self.me], loc.at[0])]
        self.step3 = []
        for j in range(1, group):
            to = lax.rem(self.me + j, group)
            peer = self.level * group + to
            self.step1.append(remote(src.at[to], here.at[self.me], gs.at[j], gr.at[j], seq=peer))
            self.step3.append(remote(done, every.at[self.me], fs.at[j], fr.at[j], seq=peer))
        self.across = lambda j: remote(
            mine, layer.at[self.level], ls.at[j], lr.at[j],
            seq=lax.rem(self.level + j, self.layers) * group + self.me,
        )

    def middle(self, combine):
        wait(self.step1)
        part = combine(self.here)
        self.mine[...] = part
        self.layer[self.level] = part
        each(self.layers, lambda j: self.across(j).start())

    def finish(self, combine):
        each(self.layers, lambda j: self.across(j).wait())
        total = combine(self.layer)
        self.done[...] = total
        self.every[self.me] = total
        start(self.step3)


def kernel_fetch(n, heads, pieces, served, owners, owned_at, query, grad, key, value, first, ready,
                 qh, gh, incoming, halos, gall, *rest):
    landed, rest = (first,) + rest[: pieces - 1], rest[pieces - 1 :]
    outgoing, gsrc, ghere, gmine, glayer, gdone = rest[:6]
    send, recv, local, bs, br, hs, hr, *gsems = rest[6:]
    s = lax.axis_index("seq")
    tokens, width = query.shape[0], query.shape[1] // heads
    size = 2 * width // pieces
    nb = first.shape[0]
    half = pieces // 2
    greet(n, heads)
    moves = [[]]
    for c in range(1, pieces):
        src = key if c < half else value
        moves.append(exchange(
            piece_in(src, landed[c], width, (c % half) * size, size),
            heads, send, recv, local, c,
        ))
    blocks = [
        random_piece(n, c, (lambda p, c=c: (ready.at[p] if c == 0 else outgoing.at[c - 1, p])),
                     incoming, size, bs, br)
        for c in range(pieces)
    ]
    qmove = exchange(to_heads(query, qh, tokens, width), heads, send, recv, local, pieces)
    qmove += exchange(to_heads(grad, gh, tokens, width), heads, send, recv, local, pieces + 1)
    edges = []
    for c in range(pieces):
        edges += halo(n, landed[c].at[0], landed[c].at[nb - 1], halos, hs, hr, c)
    shared = Shared(n, gsrc, ghere, gmine, glayer, gdone, gall, gsems)
    for m in moves:
        start(m)
    far_first(n, blocks[0])
    start(qmove)
    keep = pltpu.make_async_copy(ready.at[s], incoming.at[s, :, pl.ds(0, size)],
                                 local.at[pieces + 2])
    keep.start()
    for c in range(1, pieces):
        wait(moves[c])
        at = pl.ds(c * size, size)

        def gather(i, carry):
            outgoing[c - 1, i] = landed[c][served[i]]
            return carry

        lax.fori_loop(0, n, gather, 0)
        incoming[s, :, at] = landed[c][served[s]]
        if c == pieces - 1:
            group = gsrc.shape[0]
            per = group // GLOBALS
            count = BLOCK // per
            for m in range(group):
                low = (m % per) * count
                for k in range(pieces):
                    gsrc[m, :, pl.ds(k * size, size)] = landed[k][
                        owned_at[m // per], pl.ds(low, count), :
                    ]
            start(shared.step1 + edges)
            mine = owners[shared.me * GLOBALS // group]
            shared.middle(lambda ref: ref[lax.rem(mine, group)])
        far_first(n, blocks[c])
    shared.finish(lambda ref: ref[mine // group])
    keep.wait()
    wait(edges + qmove + shared.step3)
    for c in range(pieces):
        each(n, lambda d: blocks[c](d).wait())


def kernel_return(n, heads, pieces, served, owners, owned_at, att, qg, sending, edge, gsend, wsum,
                  out, qout, kout, vout, returned, halos, gall, summed, ghere, gmine, glayer,
                  gdone, send, recv, local, bs, br, hs, hr, *gsems):
    s = lax.axis_index("seq")
    width = att.shape[1]
    tokens = att.shape[0] // heads
    nb = att.shape[0] // BLOCK
    size = 2 * width // pieces
    half = pieces // 2
    greet(n, heads)
    moves = [
        exchange(
            piece_out(summed, kout if c < half else vout, tokens, width, (c % half) * size, size,
                      c * size),
            heads, send, recv, local, c,
        )
        for c in range(pieces)
    ]
    blocks = [
        random_piece(n, c, lambda p, c=c: sending.at[p, :, pl.ds(c * size, size)], returned, size,
                     bs, br)
        for c in range(pieces)
    ]
    qmove = exchange(to_tokens(att, out, tokens, width), heads, send, recv, local, pieces)
    qmove += exchange(to_tokens(qg, qout, tokens, width), heads, send, recv, local, pieces + 1)
    edges = halo(n, edge.at[0], edge.at[1], halos, hs, hr)
    shared = Shared(n, gsend, ghere, gmine, glayer, gdone, gall, gsems)
    keep = pltpu.make_async_copy(sending.at[s], returned.at[s], local.at[pieces + 2])

    def combine(ref):
        def add(i, acc):
            return acc + ref[i].astype(jnp.float32)

        zero = jnp.zeros(ref.shape[1:], jnp.float32)
        return lax.fori_loop(0, ref.shape[0], add, zero).astype(jnp.bfloat16)

    start(shared.step1 + edges)
    far_first(n, blocks[0])
    start(qmove + [keep])
    shared.middle(combine)
    for c in range(1, pieces):
        far_first(n, blocks[c])
    shared.finish(combine)
    keep.wait()
    wait(edges + shared.step3)
    strip = 16
    per = shared.group // GLOBALS
    count = BLOCK // per

    def weight(cond):
        return jnp.where(cond, 1.0, 0.0).astype(jnp.float32)

    for c in range(pieces):
        each(n, lambda d: blocks[c](d).wait())
        at = pl.ds(c * size, size)

        def one_strip(t, carry):
            low = pl.multiple_of(t * strip, strip)
            here = pl.ds(low, strip)
            acc = [wsum[pl.ds(pl.multiple_of((j + 1) * BLOCK + low, strip), strip), at]
                   for j in range(nb)]
            acc[0] = acc[0] + halos[0, here, at].astype(jnp.float32)
            acc[-1] = acc[-1] + halos[1, here, at].astype(jnp.float32)
            for g in range(GLOBALS):
                inside = pl.ds(pl.multiple_of(lax.rem(low, count), strip), strip)
                extra = gall[g * per + low // count, inside, at].astype(jnp.float32)
                for j in range(nb):
                    hit = (owners[g] == s) & (owned_at[g] == j)
                    acc[j] = acc[j] + weight(hit) * extra

            def add(i, accs):
                x = returned[i, here, at].astype(jnp.float32)
                which = served[i]
                return tuple(accs[j] + weight(which == j) * x for j in range(nb))

            acc = lax.fori_loop(0, n, add, tuple(acc))
            for j in range(nb):
                summed[pl.ds(pl.multiple_of(j * BLOCK + low, strip), strip), at] = acc[j].astype(
                    jnp.bfloat16
                )
            return carry

        lax.fori_loop(0, BLOCK // strip, one_strip, 0)
        start(moves[c])
    wait(qmove)
    for m in moves:
        wait(m)


def dot(a, b, ca, cb):
    return lax.dot_general(a, b, (((ca,), (cb,)), ((), ())), preferred_element_type=jnp.float32)


def kernel_attend(n, lanes, pieces, slots, qh, gh, halos, incoming, gall, *rest):
    landed, rest = rest[:pieces], rest[pieces:]
    att, qg, wsum, edge, sending, gsum, pairs, keys, gacc = rest
    nb = qh.shape[0] // BLOCK
    width = qh.shape[1]
    s = lax.axis_index("seq")
    per = lanes // HEAD_DIM
    scale = jnp.asarray(HEAD_DIM ** (-0.5), jnp.bfloat16)
    pairs[pl.ds(0, BLOCK)] = halos[0]
    size = landed[0].shape[1]
    for c in range(pieces):
        pairs[pl.ds(BLOCK, nb * BLOCK), pl.ds(c * size, size)] = landed[c][...]
    pairs[pl.ds((nb + 1) * BLOCK, BLOCK)] = halos[1]
    keys[pl.ds((3 + RANDOM) * BLOCK, GLOBALS * BLOCK)] = gall[...]
    gacc[...] = jnp.zeros_like(gacc)
    wsum[...] = jnp.zeros_like(wsum)
    if n > RANDOM * nb:
        sending[...] = jnp.zeros_like(sending)
    lane_head = lax.broadcasted_iota(jnp.int32, (BLOCK, lanes), 1) // HEAD_DIM
    part = lax.broadcasted_iota(jnp.int32, (PARTS * BLOCK, 1), 0) // BLOCK

    def stack(x):
        zero = jnp.zeros_like(x)
        return jnp.concatenate([jnp.where(lane_head == j, x, zero) for j in range(per)], axis=0)

    def unstack(x):
        got = x[0:BLOCK]
        for j in range(1, per):
            got = jnp.where(lane_head == j, x[j * BLOCK : (j + 1) * BLOCK], got)
        return got

    def block(b, carry):
        here = pl.ds(pl.multiple_of(b * BLOCK, BLOCK), BLOCK)
        window = pl.ds(pl.multiple_of(b * BLOCK, BLOCK), 3 * BLOCK)
        keys[pl.ds(0, 3 * BLOCK)] = pairs[window]
        for r in range(RANDOM):
            keys[pl.ds((3 + r) * BLOCK, BLOCK)] = incoming[slots[b * RANDOM + r]]
        number = s * nb + b
        bad = ((part == 0) & (number == 0)) | ((part == 2) & (number == n * nb - 1))
        for g in range(width // lanes):
            at = pl.ds(g * lanes, lanes)
            vat = pl.ds(width + g * lanes, lanes)
            q = stack(qh[here, at]) * scale
            do = stack(gh[here, at])
            k = keys[:, at]
            v = keys[:, vat]
            scores = jnp.where(bad, MASKED, dot(k, q, 1, 1))
            raw = jnp.exp(scores - jnp.max(scores, axis=0, keepdims=True))
            probs = raw * (1.0 / jnp.sum(raw, axis=0, keepdims=True))
            half = probs.astype(jnp.bfloat16)
            pgrad = dot(v, do, 1, 1)
            delta = jnp.sum(half.astype(jnp.float32) * pgrad, axis=0, keepdims=True)
            ds = (probs * (pgrad - delta)).astype(jnp.bfloat16)
            att[here, at] = unstack(dot(half, v, 0, 0)).astype(jnp.bfloat16)
            qg[here, at] = (unstack(dot(ds, k, 0, 0)) * HEAD_DIM ** (-0.5)).astype(jnp.bfloat16)
            for x, y, to in ((ds, q, at), (half, do, vat)):
                grad = dot(x, y, 1, 0)
                wsum[window, to] += grad[: 3 * BLOCK]
                for r in range(RANDOM):
                    low = (3 + r) * BLOCK
                    sending[slots[b * RANDOM + r], :, to] = grad[low : low + BLOCK].astype(
                        jnp.bfloat16
                    )
                gacc[:, to] += grad[(3 + RANDOM) * BLOCK :]
        return carry

    lax.fori_loop(0, nb, block, 0, unroll=2)
    edge[0] = wsum[pl.ds(0, BLOCK)].astype(jnp.bfloat16)
    edge[1] = wsum[pl.ds((nb + 1) * BLOCK, BLOCK)].astype(jnp.bfloat16)
    gsum[...] = gacc[...].astype(jnp.bfloat16)


def kernel_store(a, b, c, d, wa, wb, wc, wd, sem):
    copies = [
        pltpu.make_async_copy(x, y, sem.at[i])
        for i, (x, y) in enumerate(((a, wa), (b, wb), (c, wc), (d, wd)))
    ]
    start(copies)
    wait(copies)


def body(n, heads, query_rows, key_rows, value_rows, out_grad, random_blocks, global_blocks):
    bf = jnp.bfloat16
    tokens, full = query_rows.shape
    width = full // heads
    total = tokens * heads
    nb = total // BLOCK
    me = lax.axis_index("seq")
    dma = pltpu.SemaphoreType.DMA
    sds = jax.ShapeDtypeStruct
    requests = RANDOM * nb
    flat = random_blocks.reshape(requests)
    ids = jnp.broadcast_to(jnp.pad(flat, (0, 128 - requests))[None], (8, 128))
    pieces = min(4, 2 * width // 128)
    size = 2 * width // pieces
    blocked = (tokens // BLOCK, BLOCK, full)
    key_blocks, value_blocks = key_rows.reshape(blocked), value_rows.reshape(blocked)
    query_rows, key_blocks, value_blocks, out_grad = (
        pltpu.with_memory_space_constraint(x, pltpu.HBM)
        for x in (query_rows, key_blocks, value_blocks, out_grad)
    )
    first, ids_all = pl.pallas_call(
        partial(kernel_in, n, heads, size),
        out_shape=(sds((nb, BLOCK, size), bf), sds((n, 8, 128), jnp.int32)),
        in_specs=[HBM, VMEM],
        out_specs=(VMEM,) * 2,
        scratch_shapes=[dma((heads,)), dma((heads,)), dma((2,)), dma((n,)), dma((n,))],
        compiler_params=params(0),
        name="head_in",
    )(key_blocks, ids)
    asked = ids_all[:, 0, :requests]
    served = jnp.sum(jnp.where(asked // nb == me, asked % nb, 0), axis=1).astype(jnp.int32)
    owners = global_blocks // nb
    owned_at = global_blocks % nb
    ready = jnp.take(first, served, axis=0, mode="clip")
    group = 4
    layers = n // group
    chunk = GLOBALS * BLOCK // group
    slab = sds((n, BLOCK, 2 * width), bf)
    small = sds((group, chunk, 2 * width), bf)
    wide = (chunk, 2 * width)
    scratch = [
        pltpu.VMEM(small.shape, bf), pltpu.VMEM(wide, bf), pltpu.VMEM((layers,) + wide, bf),
        pltpu.VMEM(wide, bf),
        dma(((pieces + 2) * heads,)), dma(((pieces + 2) * heads,)), dma((pieces + 3,)),
        dma((pieces * n,)), dma((pieces * n,)), dma((2 * pieces,)), dma((2 * pieces,)),
        dma((group,)), dma((group,)), dma((layers,)), dma((layers,)), dma((group,)),
        dma((group,)), dma((1,)),
    ]
    edges = sds((2, BLOCK, 2 * width), bf)
    qh, gh, incoming, halos, gall, *landed = pl.pallas_call(
        partial(kernel_fetch, n, heads, pieces),
        out_shape=(sds((total, width), bf), sds((total, width), bf), slab, edges, small)
        + (sds((nb, BLOCK, size), bf),) * (pieces - 1),
        in_specs=[SMEM] * 3 + [HBM] * 4 + [VMEM] * 2,
        out_specs=(VMEM,) * (4 + pieces),
        scratch_shapes=[pltpu.VMEM((pieces - 1, n, BLOCK, size), bf), pltpu.VMEM(small.shape, bf)]
        + scratch,
        compiler_params=params(1),
        name="fetch",
    )(served, owners, owned_at, query_rows, out_grad, key_blocks, value_blocks, first, ready)
    gwide = (GLOBALS * BLOCK, 2 * width)
    att, qg, wsum, edge, sending, gsum = pl.pallas_call(
        partial(kernel_attend, n, min(256, width), pieces),
        out_shape=(
            sds((total, width), bf), sds((total, width), bf),
            sds(((nb + 2) * BLOCK, 2 * width), jnp.float32), edges, slab, sds(gwide, bf),
        ),
        in_specs=[SMEM] + [VMEM] * (5 + pieces),
        out_specs=(VMEM,) * 6,
        scratch_shapes=[
            pltpu.VMEM(((nb + 2) * BLOCK, 2 * width), bf),
            pltpu.VMEM((PARTS * BLOCK, 2 * width), bf),
            pltpu.VMEM(gwide, jnp.float32),
        ],
        compiler_params=pltpu.CompilerParams(vmem_limit_bytes=24 * 1024 * 1024),
        name="attend",
    )(flat // nb, qh, gh, halos, incoming, gall.reshape(gwide),
      *[x.reshape(total, size) for x in (first, *landed)])
    results = pl.pallas_call(
        partial(kernel_return, n, heads, pieces),
        out_shape=(sds((tokens, full), bf),) * 4,
        in_specs=[SMEM] * 3 + [VMEM] * 6,
        out_specs=(VMEM,) * 4,
        scratch_shapes=[
            pltpu.VMEM(slab.shape, bf), pltpu.VMEM(edges.shape, bf), pltpu.VMEM(small.shape, bf),
            pltpu.VMEM((total, 2 * width), bf),
        ] + scratch,
        compiler_params=params(2),
        name="give_back",
    )(served, owners, owned_at, att, qg, sending, edge, gsum.reshape(group, chunk, 2 * width),
      wsum)
    return pl.pallas_call(
        kernel_store,
        out_shape=(sds((tokens, full), bf),) * 4,
        in_specs=[VMEM] * 4,
        out_specs=(HBM,) * 4,
        scratch_shapes=[dma((4,))],
        compiler_params=pltpu.CompilerParams(vmem_limit_bytes=16 * 1024 * 1024),
        name="store",
    )(*results)


LANES = 128
WIDE = 2 * LANES


class Team:
    def __init__(self, n, heads, groups, tokens):
        self.n, self.heads, self.groups, self.tokens = n, heads, groups, tokens
        self.members = n // groups
        s, self.h = lax.axis_index("seq"), lax.axis_index("head")
        self.g, self.m = s // self.members, lax.rem(s, self.members)
        self.bits = [1 << i for i in reversed(range(self.members.bit_length() - 1))]
        self.places = [(i, d) for i in range(groups) for d in range(heads)]
        self.me = self.slot(self.g, self.h)

    def slot(self, g, h):
        return g * self.heads + h

    def near(self, i):
        total = self.g * 0
        for g in range(self.groups):
            order = sorted(range(self.groups), key=lambda k: (abs(k - g), k))
            total = total + jnp.where(self.g == g, order[i], 0)
        return total

    def place(self, j):
        i, d = self.places[j]
        return (self.near(i) if i else self.g), lax.rem(self.h + d, self.heads)

    def device(self, g, h):
        return {"seq": g * self.members + self.m, "head": h}

    def mate(self, bit):
        return self.m ^ bit

    def mate_device(self, bit):
        return {"seq": self.g * self.members + self.mate(bit)}

    def chunk(self, g, h, m):
        return rows((g * self.members + m) * self.heads + h, self.tokens)

    def columns(self, g, h):
        return pl.ds(pl.multiple_of((h * self.groups + g) * LANES, LANES), LANES)

    def greet(self):
        barrier = pltpu.get_barrier_semaphore()
        for j in range(1, len(self.places)):
            pl.semaphore_signal(
                barrier, inc=1, device_id=self.device(*self.place(j)), device_id_type=MESH
            )
        for bit in self.bits:
            pl.semaphore_signal(
                barrier, inc=1, device_id=self.mate_device(bit), device_id_type=MESH
            )
        pl.semaphore_wait(barrier, len(self.places) - 1 + len(self.bits))


def send_to(src, dst, send, recv, device):
    return pltpu.make_async_remote_copy(
        src_ref=src, dst_ref=dst, send_sem=send, recv_sem=recv, device_id=device,
        device_id_type=MESH,
    )


def kernel_gather(n, heads, groups, key, value, query, grad, ids, kv, qd, ids_all, send, recv,
                  local, fsend, frecv, isend, irecv):
    tokens = query.shape[0]
    t = Team(n, heads, groups, tokens)
    count = len(t.places)
    t.greet()
    kvb = kv.at[pl.ds(BLOCK, kv.shape[0] - 2 * BLOCK)]

    def move(a, j):
        g, h = t.place(j)
        src = (key, value, query, grad)[a].at[:, t.columns(g, h)]
        lanes = pl.ds((a % 2) * LANES, LANES)
        dst = (kvb.at[t.chunk(t.g, t.h, t.m), lanes] if a < 2
               else qd.at[rows(t.me, tokens), lanes])
        if j == 0:
            return pltpu.make_async_copy(src, dst, local.at[a])
        return send_to(src, dst, send.at[a * count + j], recv.at[a * count + t.me],
                       t.device(g, h))

    def arrived(a, j):
        g, h = t.place(j)
        src = (key, value, query, grad)[a].at[:, t.columns(g, h)]
        lanes = pl.ds((a % 2) * LANES, LANES)
        dst = (kvb.at[t.chunk(g, h, t.m), lanes] if a < 2
               else qd.at[rows(t.slot(g, h), tokens), lanes])
        return send_to(src, dst, send.at[a * count + j], recv.at[a * count + t.slot(g, h)],
                       t.device(g, h))

    idm = [send_to(ids, ids_all.at[t.g], isend.at[i], irecv.at[t.g], t.device(t.near(i), t.h))
           for i in range(1, groups)]
    idr = [send_to(ids, ids_all.at[t.near(i)], isend.at[i], irecv.at[t.near(i)],
                   t.device(t.near(i), t.h)) for i in range(1, groups)]
    start(idm)
    for a in (0, 1):
        for j in range(count):
            move(a, j).start()
    for a in (2, 3):
        for j in range(count):
            move(a, j).start()
    mine = pltpu.make_async_copy(ids, ids_all.at[t.g], local.at[4])
    mine.start()
    edge = jnp.zeros((BLOCK, kv.shape[1]), kv.dtype)
    kv[pl.ds(0, BLOCK)] = edge
    kv[pl.ds(kv.shape[0] - BLOCK, BLOCK)] = edge

    def forward(stage, mask, j, mine):
        bit = t.bits[stage]
        g, h = t.place(j)
        owner = t.m ^ mask if mine else t.m ^ bit ^ mask
        ref = kvb.at[t.chunk(g, h, owner)]
        at = (stage * t.members + mask) * count + j
        return send_to(ref, ref, fsend.at[at], frecv.at[at], t.mate_device(bit))

    def masks(stage):
        got = [0]
        for bit in t.bits[:stage]:
            got += [x ^ bit for x in got]
        return got

    lag = 1
    stages = range(len(t.bits))
    for step in range(count + lag * len(t.bits)):
        for stage in reversed(stages):
            j = step - lag * (stage + 1)
            if 0 <= j < count:
                for mask in masks(stage):
                    forward(stage, mask, j, False).wait_recv()
                    for later in range(stage + 1, len(t.bits)):
                        forward(later, mask ^ t.bits[stage], j, True).start()
        if step < count:
            for a in (0, 1):
                if step == 0:
                    move(a, 0).wait()
                else:
                    arrived(a, step).wait_recv()
            for stage in stages:
                forward(stage, 0, step, True).start()
    for stage in stages:
        for mask in masks(stage):
            for j in range(count):
                forward(stage, mask, j, True).wait_send()
    for a in (2, 3):
        move(a, 0).wait()
        for j in range(1, count):
            arrived(a, j).wait_recv()
    for a in range(4):
        for j in range(1, count):
            move(a, j).wait_send()
    mine.wait()
    for c in idr:
        c.wait_recv()
    for c in idm:
        c.wait_send()


def kernel_blocks(n, heads, groups, tokens, picks, owners, kv, qd, od, acc, part, keys, gacc):
    t = Team(n, heads, groups, tokens)
    run = tokens * heads // BLOCK
    total = n * run
    per = LANES // HEAD_DIM
    scale = jnp.asarray(HEAD_DIM ** (-0.5), jnp.bfloat16)
    acc[...] = jnp.zeros_like(acc)
    gacc[...] = jnp.zeros_like(gacc)
    for k in range(GLOBALS):
        keys[pl.ds((3 + RANDOM + k) * BLOCK, BLOCK)] = kv[
            pl.ds(pl.multiple_of((owners[k] + 1) * BLOCK, BLOCK), BLOCK)]
    lane_head = lax.broadcasted_iota(jnp.int32, (BLOCK, LANES), 1) // HEAD_DIM
    where = lax.broadcasted_iota(jnp.int32, (PARTS * BLOCK, 1), 0) // BLOCK
    at, vat = pl.ds(0, LANES), pl.ds(LANES, LANES)

    def stack(x):
        zero = jnp.zeros_like(x)
        return jnp.concatenate([jnp.where(lane_head == j, x, zero) for j in range(per)], axis=0)

    def unstack(x):
        got = x[0:BLOCK]
        for j in range(1, per):
            got = jnp.where(lane_head == j, x[j * BLOCK : (j + 1) * BLOCK], got)
        return got

    def block(b, carry):
        here = pl.ds(pl.multiple_of(b * BLOCK, BLOCK), BLOCK)
        number = ((b // run) * t.members + t.m) * run + lax.rem(b, run)
        window = pl.ds(pl.multiple_of(number * BLOCK, BLOCK), 3 * BLOCK)
        keys[pl.ds(0, 3 * BLOCK)] = kv[window]
        picked = [pl.ds(pl.multiple_of((picks[b * RANDOM + r] + 1) * BLOCK, BLOCK), BLOCK)
                  for r in range(RANDOM)]
        for r in range(RANDOM):
            keys[pl.ds((3 + r) * BLOCK, BLOCK)] = kv[picked[r]]
        bad = ((where == 0) & (number == 0)) | ((where == 2) & (number == total - 1))
        q = stack(qd[here, at]) * scale
        do = stack(qd[here, vat])
        k = keys[:, at]
        v = keys[:, vat]
        scores = jnp.where(bad, MASKED, dot(k, q, 1, 1))
        raw = jnp.exp(scores - jnp.max(scores, axis=0, keepdims=True))
        probs = raw * (1.0 / jnp.sum(raw, axis=0, keepdims=True))
        half = probs.astype(jnp.bfloat16)
        pgrad = dot(v, do, 1, 1)
        delta = jnp.sum(half.astype(jnp.float32) * pgrad, axis=0, keepdims=True)
        ds = (probs * (pgrad - delta)).astype(jnp.bfloat16)
        od[here, at] = unstack(dot(half, v, 0, 0)).astype(jnp.bfloat16)
        od[here, vat] = (unstack(dot(ds, k, 0, 0)) * HEAD_DIM ** (-0.5)).astype(jnp.bfloat16)
        for x, y, to in ((ds, q, at), (half, do, vat)):
            out = dot(x, y, 1, 0)
            acc[window, to] += out[: 3 * BLOCK]
            for r in range(RANDOM):
                low = (3 + r) * BLOCK
                acc[picked[r], to] += out[low : low + BLOCK]
            gacc[:, to] += out[(3 + RANDOM) * BLOCK :]
        return carry

    lax.fori_loop(0, qd.shape[0] // BLOCK, block, 0, unroll=2)
    for k in range(GLOBALS):
        acc[pl.ds(pl.multiple_of((owners[k] + 1) * BLOCK, BLOCK), BLOCK)] += gacc[
            pl.ds(k * BLOCK, BLOCK)]

    def convert(i, carry):
        part[rows(i, BLOCK)] = acc[rows(i + 1, BLOCK)].astype(jnp.bfloat16)
        return carry

    lax.fori_loop(0, total, convert, 0)


def kernel_scatter(n, heads, groups, od, acc, part, out, qout, kout, vout, inbox, sums, final,
                   send, recv, local, fsend, frecv):
    tokens = out.shape[0]
    t = Team(n, heads, groups, tokens)
    count = len(t.places)
    t.greet()
    mine = t.columns(t.g, t.h)
    dests = (out, qout, kout, vout)

    def lanes(a):
        return pl.ds((a % 2) * LANES, LANES)

    def move(a, j):
        g, h = t.place(j)
        base = od if a < 2 else final
        src = base.at[rows(t.slot(g, h) if a < 2 else j, tokens), lanes(a)]
        dst = dests[a].at[:, mine]
        if j == 0:
            return pltpu.make_async_copy(src, dst, local.at[a])
        return send_to(src, dst, send.at[a * count + j], recv.at[a * count + t.me],
                       t.device(g, h))

    def arrived(a, j):
        g, h = t.place(j)
        base = od if a < 2 else final
        src = base.at[rows(t.slot(g, h) if a < 2 else j, tokens), lanes(a)]
        return send_to(src, dests[a].at[:, t.columns(g, h)], send.at[a * count + j],
                       recv.at[a * count + t.slot(g, h)], t.device(g, h))

    order = list(reversed(t.bits))
    owners = []
    held = list(range(t.members))
    for bit in order:
        owners.append([x for x in held if x & bit])
        held = [x for x in held if not x & bit]

    def trade(stage, mask, j, src):
        at = (stage * t.members + mask) * count + j
        return send_to(src, inbox.at[rows(at_box(stage, mask, j), tokens)], fsend.at[at],
                       frecv.at[at], t.mate_device(order[stage]))

    boxes = [(stage, mask) for stage in range(len(order)) for mask in owners[stage]]

    def at_box(stage, mask, j):
        return boxes.index((stage, mask)) * count + j

    def chunk_of(mask, j):
        g, h = t.place(j)
        return t.chunk(g, h, t.m ^ mask)

    def below(ref):
        return pl.ds(BLOCK + ref.start, ref.size)

    js = list(range(1, count)) + [0]
    for j in js:
        for mask in reversed(owners[0]):
            trade(0, mask, j, part.at[chunk_of(mask, j)]).start()
    for a in (0, 1):
        for j in range(count):
            move(a, j).start()

    def total(mask, j, upto):
        x = acc[below(chunk_of(mask, j))]
        for stage in range(upto):
            full = mask ^ order[stage]
            x = x + inbox[rows(at_box(stage, full, j), tokens)].astype(jnp.float32)
        return x.astype(jnp.bfloat16)

    sent = [(0, mask, j, None) for mask in owners[0] for j in js]
    for stage in range(1, len(order)):
        for j in js:
            for mask in owners[stage]:
                for before in range(stage):
                    trade(before, mask ^ order[before], j, inbox.at[rows(0, tokens)]).wait_recv()
                spot = rows((stage - 1) * count + j, tokens)
                sums[spot] = total(mask, j, stage)
                trade(stage, mask, j, sums.at[spot]).start()
    for j in js:
        for stage in range(len(order)):
            trade(stage, order[stage], j, inbox.at[rows(0, tokens)]).wait_recv()
        final[rows(j, tokens)] = total(0, j, len(order))
        for a in (2, 3):
            move(a, j).start()
    for stage in range(len(order)):
        for mask in owners[stage]:
            for j in js:
                trade(stage, mask, j, inbox.at[rows(0, tokens)]).wait_send()
    for a in range(4):
        move(a, 0).wait()
        for j in range(1, count):
            move(a, j).wait_send()
            arrived(a, j).wait_recv()


def grouped(n, heads, groups, query_rows, key_rows, value_rows, out_grad, random_blocks,
            global_blocks):
    bf = jnp.bfloat16
    tokens, full = query_rows.shape
    members = n // groups
    count = groups * heads
    everything = n * heads * tokens
    held = count * tokens
    bits = members.bit_length() - 1
    requests = random_blocks.size
    dma = pltpu.SemaphoreType.DMA
    sds = jax.ShapeDtypeStruct
    ids = jnp.pad(random_blocks.reshape(1, requests), ((0, 7), (0, 128 - requests)))
    query_rows, key_rows, value_rows, out_grad = (
        pltpu.with_memory_space_constraint(x, pltpu.HBM)
        for x in (query_rows, key_rows, value_rows, out_grad)
    )
    kv, qd, ids_all = pl.pallas_call(
        partial(kernel_gather, n, heads, groups),
        out_shape=(sds((everything + 2 * BLOCK, WIDE), bf), sds((held, WIDE), bf),
                   sds((groups, 8, 128), jnp.int32)),
        in_specs=[HBM] * 4 + [VMEM],
        out_specs=(VMEM,) * 3,
        scratch_shapes=[dma((4 * count,)), dma((4 * count,)), dma((5,)),
                        dma((bits * members * count,)), dma((bits * members * count,)),
                        dma((groups,)), dma((groups,))],
        compiler_params=params(0),
        name="gather",
    )(key_rows, value_rows, query_rows, out_grad, ids)
    picks = ids_all[:, 0, :requests].reshape(groups * requests)
    od, acc, part = pl.pallas_call(
        partial(kernel_blocks, n, heads, groups, tokens),
        out_shape=(sds((held, WIDE), bf), sds((everything + 2 * BLOCK, WIDE), jnp.float32),
                   sds((everything, WIDE), bf)),
        in_specs=[SMEM] * 2 + [VMEM] * 2,
        out_specs=(VMEM,) * 3,
        scratch_shapes=[pltpu.VMEM((PARTS * BLOCK, WIDE), bf),
                        pltpu.VMEM((GLOBALS * BLOCK, WIDE), jnp.float32)],
        compiler_params=pltpu.CompilerParams(vmem_limit_bytes=24 * 1024 * 1024),
        name="blocks",
    )(picks, global_blocks, kv, qd)
    results = pl.pallas_call(
        partial(kernel_scatter, n, heads, groups),
        out_shape=(sds((tokens, full), bf),) * 4,
        in_specs=[VMEM] * 3,
        out_specs=(VMEM,) * 4,
        scratch_shapes=[
            pltpu.VMEM(((members - 1) * held, WIDE), bf),
            pltpu.VMEM((max(bits - 1, 1) * held, WIDE), bf), pltpu.VMEM((held, WIDE), bf),
            dma((4 * count,)), dma((4 * count,)), dma((4,)),
            dma((bits * members * count,)), dma((bits * members * count,)),
        ],
        compiler_params=params(1),
        name="scatter",
    )(od, acc, part)
    return pl.pallas_call(
        kernel_store,
        out_shape=(sds((tokens, full), bf),) * 4,
        in_specs=[VMEM] * 4,
        out_specs=(HBM,) * 4,
        scratch_shapes=[dma((4,))],
        compiler_params=pltpu.CompilerParams(vmem_limit_bytes=16 * 1024 * 1024),
        name="store",
    )(*results)


def chosen(n, heads, query_rows, *others):
    tokens, full = query_rows.shape
    groups = full // LANES // heads
    fits = n * heads * tokens * WIDE * 6 <= 24 * 1024 * 1024
    if full % (LANES * heads) == 0 and n % groups == 0 and fits and n // groups in (2, 4):
        return grouped(n, heads, groups, query_rows, *others)
    return body(n, heads, query_rows, *others)


def solution(mesh):
    rows_spec = P(("seq", "head"), None)
    return jax.shard_map(
        partial(chosen, mesh.shape["seq"], mesh.shape["head"]),
        mesh=mesh,
        in_specs=(rows_spec,) * 4 + (P("seq", None), P()),
        out_specs=(rows_spec,) * 4,
        check_vma=False,
    )
```

```python
from functools import partial

import jax
import jax.numpy as jnp
from jax import lax
from jax.experimental import pallas as pl
from jax.experimental.pallas import tpu as pltpu
from jax.sharding import PartitionSpec as P

HEAD_DIM = 64
BLOCK = 64
RANDOM = 2
GLOBALS = 2
PARTS = 3 + RANDOM + GLOBALS
MASKED = -1e30
MESH = pl.DeviceIdType.MESH
VMEM = pl.BlockSpec(memory_space=pltpu.VMEM)
HBM = pl.BlockSpec(memory_space=pltpu.HBM)
SMEM = pl.BlockSpec(memory_space=pltpu.SMEM)


def params(cid):
    return pltpu.CompilerParams(
        collective_id=cid, has_side_effects=True, vmem_limit_bytes=24 * 1024 * 1024
    )


def greet(n, heads):
    s, h = lax.axis_index("seq"), lax.axis_index("head")
    barrier = pltpu.get_barrier_semaphore()
    if n > 0:

        def hello(d, c):
            pl.semaphore_signal(
                barrier, inc=1, device_id={"seq": lax.rem(s + d, n)}, device_id_type=MESH
            )
            return c

        lax.fori_loop(1, n, hello, 0)
    for d in range(1, heads):
        pl.semaphore_signal(
            barrier, inc=1, device_id={"head": lax.rem(h + d, heads)}, device_id_type=MESH
        )
    pl.semaphore_wait(barrier, max(n - 1, 0) + heads - 1)


def cols(index, width, base=0):
    return pl.ds(pl.multiple_of(base + index * width, 128), width)


def rows(index, count):
    return pl.ds(pl.multiple_of(index * count, 16), count)


def each(n, f):
    def step(d, c):
        f(d)
        return c

    lax.fori_loop(1, n, step, 0)


def remote(src, dst, send, recv, **where):
    return pltpu.make_async_remote_copy(
        src_ref=src, dst_ref=dst, send_sem=send, recv_sem=recv, device_id=where,
        device_id_type=MESH,
    )


def exchange(view, heads, send, recv, local, base):
    h = lax.axis_index("head")
    copies = []
    for d in range(1, heads):
        peer = lax.rem(h + d, heads)
        source, target = view(h, peer)
        at = base * heads + d
        copies.append(remote(source, target, send.at[at], recv.at[at], head=peer))
    source, target = view(h, h)
    return copies + [pltpu.make_async_copy(source, target, local.at[base])]


def start(copies):
    for c in copies:
        c.start()


def wait(copies):
    for c in copies:
        c.wait()


def to_heads(src, dst, tokens, width):
    return lambda a, b: (src.at[:, cols(b, width)], dst.at[rows(a, tokens), :])


def piece_in(src, dst, width, offset, size):
    nt = src.shape[0]
    return lambda a, b: (
        src.at[:, :, pl.ds(pl.multiple_of(b * width + offset, 128), size)],
        dst.at[pl.ds(a * nt, nt)],
    )


def to_tokens(src, dst, tokens, width):
    return lambda a, b: (src.at[rows(b, tokens), :], dst.at[:, cols(a, width)])


def piece_out(src, dst, tokens, width, offset, size, base):
    return lambda a, b: (
        src.at[rows(b, tokens), pl.ds(base, size)],
        dst.at[:, pl.ds(pl.multiple_of(a * width + offset, 128), size)],
    )


def kernel_in(n, heads, size, key, ids, pair, ids_all, send, recv, local, isend, irecv):
    s = lax.axis_index("seq")
    greet(n, heads)
    copies = exchange(
        piece_in(key, pair, key.shape[2] // heads, 0, size), heads, send, recv, local, 0
    )

    def idc(d):
        return remote(ids, ids_all.at[s], isend.at[d], irecv.at[d], seq=lax.rem(s + d, n))

    mine = pltpu.make_async_copy(ids, ids_all.at[s], local.at[1])
    start(copies)
    each(n, lambda d: idc(d).start())
    mine.start()
    each(n, lambda d: idc(d).wait())
    mine.wait()
    wait(copies)


def halo(n, low, high, got, send, recv, at=0):
    s = lax.axis_index("seq")
    up, down = 2 * at, 2 * at + 1
    here = pl.ds(at * low.shape[1], low.shape[1])
    return [
        remote(high, got.at[0, :, here], send.at[up], recv.at[up], seq=lax.rem(s + 1, n)),
        remote(low, got.at[1, :, here], send.at[down], recv.at[down], seq=lax.rem(s + n - 1, n)),
    ]


def far_first(n, make):
    def go(i, c):
        make(n // 2 + ((i + 1) // 2) * (2 * lax.rem(i, 2) - 1)).start()
        return c

    lax.fori_loop(0, n - 1, go, 0)


def random_piece(n, c, src_of, dst, size, send, recv):
    s = lax.axis_index("seq")

    def make(d):
        peer = lax.rem(s + d, n)
        return remote(
            src_of(peer), dst.at[s, :, pl.ds(c * size, size)], send.at[c * n + d],
            recv.at[c * n + d], seq=peer,
        )

    return make


class Shared:
    def __init__(self, n, src, here, mine, layer, done, every, sems):
        s = lax.axis_index("seq")
        gs, gr, ls, lr, fs, fr, loc = sems
        self.group = group = src.shape[0]
        self.layers = n // group
        self.me, self.level = lax.rem(s, group), s // group
        self.mine, self.layer, self.done, self.every, self.here = mine, layer, done, every, here
        self.step1 = [pltpu.make_async_copy(src.at[self.me], here.at[self.me], loc.at[0])]
        self.step3 = []
        for j in range(1, group):
            to = lax.rem(self.me + j, group)
            peer = self.level * group + to
            self.step1.append(remote(src.at[to], here.at[self.me], gs.at[j], gr.at[j], seq=peer))
            self.step3.append(remote(done, every.at[self.me], fs.at[j], fr.at[j], seq=peer))
        self.across = lambda j: remote(
            mine, layer.at[self.level], ls.at[j], lr.at[j],
            seq=lax.rem(self.level + j, self.layers) * group + self.me,
        )

    def middle(self, combine):
        wait(self.step1)
        part = combine(self.here)
        self.mine[...] = part
        self.layer[self.level] = part
        each(self.layers, lambda j: self.across(j).start())

    def finish(self, combine):
        each(self.layers, lambda j: self.across(j).wait())
        total = combine(self.layer)
        self.done[...] = total
        self.every[self.me] = total
        start(self.step3)


def kernel_fetch(n, heads, pieces, served, owners, owned_at, query, grad, key, value, first, ready,
                 qh, gh, incoming, halos, gall, *rest):
    landed, rest = (first,) + rest[: pieces - 1], rest[pieces - 1 :]
    outgoing, gsrc, ghere, gmine, glayer, gdone = rest[:6]
    send, recv, local, bs, br, hs, hr, *gsems = rest[6:]
    s = lax.axis_index("seq")
    tokens, width = query.shape[0], query.shape[1] // heads
    size = 2 * width // pieces
    nb = first.shape[0]
    half = pieces // 2
    greet(n, heads)
    moves = [[]]
    for c in range(1, pieces):
        src = key if c < half else value
        moves.append(exchange(
            piece_in(src, landed[c], width, (c % half) * size, size),
            heads, send, recv, local, c,
        ))
    blocks = [
        random_piece(n, c, (lambda p, c=c: (ready.at[p] if c == 0 else outgoing.at[c - 1, p])),
                     incoming, size, bs, br)
        for c in range(pieces)
    ]
    qmove = exchange(to_heads(query, qh, tokens, width), heads, send, recv, local, pieces)
    qmove += exchange(to_heads(grad, gh, tokens, width), heads, send, recv, local, pieces + 1)
    edges = []
    for c in range(pieces):
        edges += halo(n, landed[c].at[0], landed[c].at[nb - 1], halos, hs, hr, c)
    shared = Shared(n, gsrc, ghere, gmine, glayer, gdone, gall, gsems)
    for m in moves:
        start(m)
    far_first(n, blocks[0])
    start(qmove)
    keep = pltpu.make_async_copy(ready.at[s], incoming.at[s, :, pl.ds(0, size)],
                                 local.at[pieces + 2])
    keep.start()
    for c in range(1, pieces):
        wait(moves[c])
        at = pl.ds(c * size, size)

        def gather(i, carry):
            outgoing[c - 1, i] = landed[c][served[i]]
            return carry

        lax.fori_loop(0, n, gather, 0)
        incoming[s, :, at] = landed[c][served[s]]
        if c == pieces - 1:
            group = gsrc.shape[0]
            per = group // GLOBALS
            count = BLOCK // per
            for m in range(group):
                low = (m % per) * count
                for k in range(pieces):
                    gsrc[m, :, pl.ds(k * size, size)] = landed[k][
                        owned_at[m // per], pl.ds(low, count), :
                    ]
            start(shared.step1 + edges)
            mine = owners[shared.me * GLOBALS // group]
            shared.middle(lambda ref: ref[lax.rem(mine, group)])
        far_first(n, blocks[c])
    shared.finish(lambda ref: ref[mine // group])
    keep.wait()
    wait(edges + qmove + shared.step3)
    for c in range(pieces):
        each(n, lambda d: blocks[c](d).wait())


def kernel_return(n, heads, pieces, served, owners, owned_at, att, qg, sending, edge, gsend, wsum,
                  out, qout, kout, vout, returned, halos, gall, summed, ghere, gmine, glayer,
                  gdone, send, recv, local, bs, br, hs, hr, *gsems):
    s = lax.axis_index("seq")
    width = att.shape[1]
    tokens = att.shape[0] // heads
    nb = att.shape[0] // BLOCK
    size = 2 * width // pieces
    half = pieces // 2
    greet(n, heads)
    moves = [
        exchange(
            piece_out(summed, kout if c < half else vout, tokens, width, (c % half) * size, size,
                      c * size),
            heads, send, recv, local, c,
        )
        for c in range(pieces)
    ]
    blocks = [
        random_piece(n, c, lambda p, c=c: sending.at[p, :, pl.ds(c * size, size)], returned, size,
                     bs, br)
        for c in range(pieces)
    ]
    qmove = exchange(to_tokens(att, out, tokens, width), heads, send, recv, local, pieces)
    qmove += exchange(to_tokens(qg, qout, tokens, width), heads, send, recv, local, pieces + 1)
    edges = halo(n, edge.at[0], edge.at[1], halos, hs, hr)
    shared = Shared(n, gsend, ghere, gmine, glayer, gdone, gall, gsems)
    keep = pltpu.make_async_copy(sending.at[s], returned.at[s], local.at[pieces + 2])

    def combine(ref):
        def add(i, acc):
            return acc + ref[i].astype(jnp.float32)

        zero = jnp.zeros(ref.shape[1:], jnp.float32)
        return lax.fori_loop(0, ref.shape[0], add, zero).astype(jnp.bfloat16)

    start(shared.step1 + edges)
    far_first(n, blocks[0])
    start(qmove + [keep])
    shared.middle(combine)
    for c in range(1, pieces):
        far_first(n, blocks[c])
    shared.finish(combine)
    keep.wait()
    wait(edges + shared.step3)
    strip = 16
    per = shared.group // GLOBALS
    count = BLOCK // per

    def weight(cond):
        return jnp.where(cond, 1.0, 0.0).astype(jnp.float32)

    for c in range(pieces):
        each(n, lambda d: blocks[c](d).wait())
        at = pl.ds(c * size, size)

        def one_strip(t, carry):
            low = pl.multiple_of(t * strip, strip)
            here = pl.ds(low, strip)
            acc = [wsum[pl.ds(pl.multiple_of((j + 1) * BLOCK + low, strip), strip), at]
                   for j in range(nb)]
            acc[0] = acc[0] + halos[0, here, at].astype(jnp.float32)
            acc[-1] = acc[-1] + halos[1, here, at].astype(jnp.float32)
            for g in range(GLOBALS):
                inside = pl.ds(pl.multiple_of(lax.rem(low, count), strip), strip)
                extra = gall[g * per + low // count, inside, at].astype(jnp.float32)
                for j in range(nb):
                    hit = (owners[g] == s) & (owned_at[g] == j)
                    acc[j] = acc[j] + weight(hit) * extra

            def add(i, accs):
                x = returned[i, here, at].astype(jnp.float32)
                which = served[i]
                return tuple(accs[j] + weight(which == j) * x for j in range(nb))

            acc = lax.fori_loop(0, n, add, tuple(acc))
            for j in range(nb):
                summed[pl.ds(pl.multiple_of(j * BLOCK + low, strip), strip), at] = acc[j].astype(
                    jnp.bfloat16
                )
            return carry

        lax.fori_loop(0, BLOCK // strip, one_strip, 0)
        start(moves[c])
    wait(qmove)
    for m in moves:
        wait(m)


def dot(a, b, ca, cb):
    return lax.dot_general(a, b, (((ca,), (cb,)), ((), ())), preferred_element_type=jnp.float32)


def kernel_attend(n, lanes, pieces, slots, qh, gh, halos, incoming, gall, *rest):
    landed, rest = rest[:pieces], rest[pieces:]
    att, qg, wsum, edge, sending, gsum, pairs, keys, gacc = rest
    nb = qh.shape[0] // BLOCK
    width = qh.shape[1]
    s = lax.axis_index("seq")
    per = lanes // HEAD_DIM
    scale = jnp.asarray(HEAD_DIM ** (-0.5), jnp.bfloat16)
    pairs[pl.ds(0, BLOCK)] = halos[0]
    size = landed[0].shape[1]
    for c in range(pieces):
        pairs[pl.ds(BLOCK, nb * BLOCK), pl.ds(c * size, size)] = landed[c][...]
    pairs[pl.ds((nb + 1) * BLOCK, BLOCK)] = halos[1]
    keys[pl.ds((3 + RANDOM) * BLOCK, GLOBALS * BLOCK)] = gall[...]
    gacc[...] = jnp.zeros_like(gacc)
    wsum[...] = jnp.zeros_like(wsum)
    if n > RANDOM * nb:
        sending[...] = jnp.zeros_like(sending)
    lane_head = lax.broadcasted_iota(jnp.int32, (BLOCK, lanes), 1) // HEAD_DIM
    part = lax.broadcasted_iota(jnp.int32, (PARTS * BLOCK, 1), 0) // BLOCK

    def stack(x):
        zero = jnp.zeros_like(x)
        return jnp.concatenate([jnp.where(lane_head == j, x, zero) for j in range(per)], axis=0)

    def unstack(x):
        got = x[0:BLOCK]
        for j in range(1, per):
            got = jnp.where(lane_head == j, x[j * BLOCK : (j + 1) * BLOCK], got)
        return got

    def block(b, carry):
        here = pl.ds(pl.multiple_of(b * BLOCK, BLOCK), BLOCK)
        window = pl.ds(pl.multiple_of(b * BLOCK, BLOCK), 3 * BLOCK)
        keys[pl.ds(0, 3 * BLOCK)] = pairs[window]
        for r in range(RANDOM):
            keys[pl.ds((3 + r) * BLOCK, BLOCK)] = incoming[slots[b * RANDOM + r]]
        number = s * nb + b
        bad = ((part == 0) & (number == 0)) | ((part == 2) & (number == n * nb - 1))
        for g in range(width // lanes):
            at = pl.ds(g * lanes, lanes)
            vat = pl.ds(width + g * lanes, lanes)
            q = stack(qh[here, at]) * scale
            do = stack(gh[here, at])
            k = keys[:, at]
            v = keys[:, vat]
            scores = jnp.where(bad, MASKED, dot(k, q, 1, 1))
            raw = jnp.exp(scores - jnp.max(scores, axis=0, keepdims=True))
            probs = raw * (1.0 / jnp.sum(raw, axis=0, keepdims=True))
            half = probs.astype(jnp.bfloat16)
            pgrad = dot(v, do, 1, 1)
            delta = jnp.sum(half.astype(jnp.float32) * pgrad, axis=0, keepdims=True)
            ds = (probs * (pgrad - delta)).astype(jnp.bfloat16)
            att[here, at] = unstack(dot(half, v, 0, 0)).astype(jnp.bfloat16)
            qg[here, at] = (unstack(dot(ds, k, 0, 0)) * HEAD_DIM ** (-0.5)).astype(jnp.bfloat16)
            for x, y, to in ((ds, q, at), (half, do, vat)):
                grad = dot(x, y, 1, 0)
                wsum[window, to] += grad[: 3 * BLOCK]
                for r in range(RANDOM):
                    low = (3 + r) * BLOCK
                    sending[slots[b * RANDOM + r], :, to] = grad[low : low + BLOCK].astype(
                        jnp.bfloat16
                    )
                gacc[:, to] += grad[(3 + RANDOM) * BLOCK :]
        return carry

    lax.fori_loop(0, nb, block, 0, unroll=2)
    edge[0] = wsum[pl.ds(0, BLOCK)].astype(jnp.bfloat16)
    edge[1] = wsum[pl.ds((nb + 1) * BLOCK, BLOCK)].astype(jnp.bfloat16)
    gsum[...] = gacc[...].astype(jnp.bfloat16)


def kernel_store(a, b, c, d, wa, wb, wc, wd, sem):
    copies = [
        pltpu.make_async_copy(x, y, sem.at[i])
        for i, (x, y) in enumerate(((a, wa), (b, wb), (c, wc), (d, wd)))
    ]
    start(copies)
    wait(copies)


def body(n, heads, query_rows, key_rows, value_rows, out_grad, random_blocks, global_blocks):
    bf = jnp.bfloat16
    tokens, full = query_rows.shape
    width = full // heads
    total = tokens * heads
    nb = total // BLOCK
    me = lax.axis_index("seq")
    dma = pltpu.SemaphoreType.DMA
    sds = jax.ShapeDtypeStruct
    requests = RANDOM * nb
    flat = random_blocks.reshape(requests)
    ids = jnp.broadcast_to(jnp.pad(flat, (0, 128 - requests))[None], (8, 128))
    pieces = min(4, 2 * width // 128)
    size = 2 * width // pieces
    blocked = (tokens // BLOCK, BLOCK, full)
    key_blocks, value_blocks = key_rows.reshape(blocked), value_rows.reshape(blocked)
    query_rows, key_blocks, value_blocks, out_grad = (
        pltpu.with_memory_space_constraint(x, pltpu.HBM)
        for x in (query_rows, key_blocks, value_blocks, out_grad)
    )
    first, ids_all = pl.pallas_call(
        partial(kernel_in, n, heads, size),
        out_shape=(sds((nb, BLOCK, size), bf), sds((n, 8, 128), jnp.int32)),
        in_specs=[HBM, VMEM],
        out_specs=(VMEM,) * 2,
        scratch_shapes=[dma((heads,)), dma((heads,)), dma((2,)), dma((n,)), dma((n,))],
        compiler_params=params(0),
        name="head_in",
    )(key_blocks, ids)
    asked = ids_all[:, 0, :requests]
    served = jnp.sum(jnp.where(asked // nb == me, asked % nb, 0), axis=1).astype(jnp.int32)
    owners = global_blocks // nb
    owned_at = global_blocks % nb
    ready = jnp.take(first, served, axis=0, mode="clip")
    group = 4
    layers = n // group
    chunk = GLOBALS * BLOCK // group
    slab = sds((n, BLOCK, 2 * width), bf)
    small = sds((group, chunk, 2 * width), bf)
    wide = (chunk, 2 * width)
    scratch = [
        pltpu.VMEM(small.shape, bf), pltpu.VMEM(wide, bf), pltpu.VMEM((layers,) + wide, bf),
        pltpu.VMEM(wide, bf),
        dma(((pieces + 2) * heads,)), dma(((pieces + 2) * heads,)), dma((pieces + 3,)),
        dma((pieces * n,)), dma((pieces * n,)), dma((2 * pieces,)), dma((2 * pieces,)),
        dma((group,)), dma((group,)), dma((layers,)), dma((layers,)), dma((group,)),
        dma((group,)), dma((1,)),
    ]
    edges = sds((2, BLOCK, 2 * width), bf)
    qh, gh, incoming, halos, gall, *landed = pl.pallas_call(
        partial(kernel_fetch, n, heads, pieces),
        out_shape=(sds((total, width), bf), sds((total, width), bf), slab, edges, small)
        + (sds((nb, BLOCK, size), bf),) * (pieces - 1),
        in_specs=[SMEM] * 3 + [HBM] * 4 + [VMEM] * 2,
        out_specs=(VMEM,) * (4 + pieces),
        scratch_shapes=[pltpu.VMEM((pieces - 1, n, BLOCK, size), bf), pltpu.VMEM(small.shape, bf)]
        + scratch,
        compiler_params=params(1),
        name="fetch",
    )(served, owners, owned_at, query_rows, out_grad, key_blocks, value_blocks, first, ready)
    gwide = (GLOBALS * BLOCK, 2 * width)
    att, qg, wsum, edge, sending, gsum = pl.pallas_call(
        partial(kernel_attend, n, min(256, width), pieces),
        out_shape=(
            sds((total, width), bf), sds((total, width), bf),
            sds(((nb + 2) * BLOCK, 2 * width), jnp.float32), edges, slab, sds(gwide, bf),
        ),
        in_specs=[SMEM] + [VMEM] * (5 + pieces),
        out_specs=(VMEM,) * 6,
        scratch_shapes=[
            pltpu.VMEM(((nb + 2) * BLOCK, 2 * width), bf),
            pltpu.VMEM((PARTS * BLOCK, 2 * width), bf),
            pltpu.VMEM(gwide, jnp.float32),
        ],
        compiler_params=pltpu.CompilerParams(vmem_limit_bytes=24 * 1024 * 1024),
        name="attend",
    )(flat // nb, qh, gh, halos, incoming, gall.reshape(gwide),
      *[x.reshape(total, size) for x in (first, *landed)])
    results = pl.pallas_call(
        partial(kernel_return, n, heads, pieces),
        out_shape=(sds((tokens, full), bf),) * 4,
        in_specs=[SMEM] * 3 + [VMEM] * 6,
        out_specs=(VMEM,) * 4,
        scratch_shapes=[
            pltpu.VMEM(slab.shape, bf), pltpu.VMEM(edges.shape, bf), pltpu.VMEM(small.shape, bf),
            pltpu.VMEM((total, 2 * width), bf),
        ] + scratch,
        compiler_params=params(2),
        name="give_back",
    )(served, owners, owned_at, att, qg, sending, edge, gsum.reshape(group, chunk, 2 * width),
      wsum)
    return pl.pallas_call(
        kernel_store,
        out_shape=(sds((tokens, full), bf),) * 4,
        in_specs=[VMEM] * 4,
        out_specs=(HBM,) * 4,
        scratch_shapes=[dma((4,))],
        compiler_params=pltpu.CompilerParams(vmem_limit_bytes=16 * 1024 * 1024),
        name="store",
    )(*results)


LANES = 128
WIDE = 2 * LANES


class Team:
    def __init__(self, n, heads, groups, tokens):
        self.n, self.heads, self.groups, self.tokens = n, heads, groups, tokens
        self.members = n // groups
        s, self.h = lax.axis_index("seq"), lax.axis_index("head")
        self.g, self.m = s // self.members, lax.rem(s, self.members)
        self.bits = [1 << i for i in reversed(range(self.members.bit_length() - 1))]
        self.places = [(i, d) for i in range(groups) for d in range(heads)]
        self.me = self.slot(self.g, self.h)

    def slot(self, g, h):
        return g * self.heads + h

    def near(self, i):
        total = self.g * 0
        for g in range(self.groups):
            order = sorted(range(self.groups), key=lambda k: (abs(k - g), k))
            total = total + jnp.where(self.g == g, order[i], 0)
        return total

    def place(self, j):
        if isinstance(j, int):
            i, d = self.places[j]
            return (self.near(i) if i else self.g), lax.rem(self.h + d, self.heads)
        g = self.g * 0
        for i in range(self.groups):
            g = g + jnp.where(j // self.heads == i, self.near(i), 0)
        return g, lax.rem(self.h + lax.rem(j, self.heads), self.heads)

    def device(self, g, h):
        return {"seq": g * self.members + self.m, "head": h}

    def mate(self, bit):
        return self.m ^ bit

    def mate_device(self, bit):
        return {"seq": self.g * self.members + self.mate(bit)}

    def chunk(self, g, h, m):
        return rows((g * self.members + m) * self.heads + h, self.tokens)

    def columns(self, g, h):
        return pl.ds(pl.multiple_of((h * self.groups + g) * LANES, LANES), LANES)

    def greet(self):
        barrier = pltpu.get_barrier_semaphore()
        for j in range(1, len(self.places)):
            pl.semaphore_signal(
                barrier, inc=1, device_id=self.device(*self.place(j)), device_id_type=MESH
            )
        for bit in self.bits:
            pl.semaphore_signal(
                barrier, inc=1, device_id=self.mate_device(bit), device_id_type=MESH
            )
        pl.semaphore_wait(barrier, len(self.places) - 1 + len(self.bits))


def send_to(src, dst, send, recv, device):
    return pltpu.make_async_remote_copy(
        src_ref=src, dst_ref=dst, send_sem=send, recv_sem=recv, device_id=device,
        device_id_type=MESH,
    )


def kernel_all(n, heads, groups, owners, key, value, query, grad, ids, out, qout, kout, vout,
               kv, qd, od, acc, extra, keys, ids_all, table, part, inbox, sums, final, send, recv,
               local, fsend, frecv, isend, irecv, bsend, brecv, blocal, tsend, trecv):
    tokens = query.shape[0]
    t = Team(n, heads, groups, tokens)
    count = len(t.places)
    per_chunk = tokens // BLOCK
    run = heads * per_chunk
    requests = RANDOM * run
    t.greet()
    arrays = (key, value, query, grad)
    dests = (out, qout, kout, vout)

    def lanes(a):
        return pl.ds((a % 2) * LANES, LANES)

    def blocks_of(g, h, m):
        return pl.ds(((g * t.members + m) * heads + h) * per_chunk + 1, per_chunk)

    def leaving(a, g, h):
        ref = arrays[a]
        return ref.at[:, :, t.columns(g, h)] if a < 2 else ref.at[:, t.columns(g, h)]

    def landing(a, g, h):
        return (kv.at[blocks_of(g, h, t.m), :, lanes(a)] if a < 2
                else qd.at[rows(t.slot(g, h), tokens), lanes(a)])

    def move(a, j):
        g, h = t.place(j)
        return send_to(leaving(a, g, h), landing(a, t.g, t.h),
                       send.at[a * count + j], recv.at[a * count + t.me], t.device(g, h))

    def keep(a):
        return pltpu.make_async_copy(leaving(a, t.g, t.h), landing(a, t.g, t.h),
                                     local.at[a])

    def arrived(a, j):
        g, h = t.place(j)
        return send_to(leaving(a, g, h), landing(a, g, h),
                       send.at[a * count + j], recv.at[a * count + t.slot(g, h)],
                       t.device(g, h))

    idm = [send_to(ids, ids_all.at[t.g], isend.at[i], irecv.at[t.g], t.device(t.near(i), t.h))
           for i in range(1, groups)]
    idr = [send_to(ids, ids_all.at[t.near(i)], isend.at[i], irecv.at[t.near(i)],
                   t.device(t.near(i), t.h)) for i in range(1, groups)]
    for a in (0, 1):
        keep(a).start()
        for j in range(1, count):
            move(a, j).start()
    start(idm)
    for a in (2, 3):
        keep(a).start()
        for j in range(1, count):
            move(a, j).start()
    own = pltpu.make_async_copy(ids, ids_all.at[t.g], local.at[4])
    own.start()
    edge = jnp.zeros(kv.shape[1:], kv.dtype)
    kv[0] = edge
    kv[kv.shape[0] - 1] = edge
    empty = jnp.zeros((BLOCK, WIDE), jnp.float32)
    for k in range(GLOBALS + 1):
        extra[groups * requests + k] = empty

    def clear(i, carry):
        acc[rows(i, BLOCK)] = empty
        return carry

    lax.fori_loop(0, acc.shape[0] // BLOCK, clear, 0)

    def forward(stage, mask, j, mine):
        bit = t.bits[stage]
        g, h = t.place(j)
        owner = t.m ^ mask if mine else t.m ^ bit ^ mask
        ref = kv.at[blocks_of(g, h, owner)]
        at = (stage * t.members + mask) * count + j
        return send_to(ref, ref, fsend.at[at], frecv.at[at], t.mate_device(bit))

    def masks(stage):
        got = [0]
        for bit in t.bits[:stage]:
            got += [x ^ bit for x in got]
        return got

    stages = range(len(t.bits))
    for step in range(count + len(t.bits)):
        for stage in reversed(stages):
            j = step - stage - 1
            if 0 <= j < count:
                for mask in masks(stage):
                    forward(stage, mask, j, False).wait_recv()
                    for later in range(stage + 1, len(t.bits)):
                        forward(later, mask ^ t.bits[stage], j, True).start()
        if step < count:
            for a in (0, 1):
                if step == 0:
                    keep(a).wait()
                else:
                    arrived(a, step).wait_recv()
            for stage in stages:
                forward(stage, 0, step, True).start()
    own.wait()
    for c in idr:
        c.wait_recv()
    fill = pltpu.make_async_copy(ids_all, table, local.at[5])
    fill.start()
    fill.wait()

    per = LANES // HEAD_DIM
    scale = jnp.asarray(HEAD_DIM ** (-0.5), jnp.bfloat16)
    for k in range(GLOBALS):
        keys[3 + RANDOM + k] = kv[owners[k] + 1]
    lane_head = lax.broadcasted_iota(jnp.int32, (BLOCK, LANES), 1) // HEAD_DIM
    where = lax.broadcasted_iota(jnp.int32, (PARTS * BLOCK, 1), 0) // BLOCK
    at, vat = lanes(0), lanes(1)

    def stack(x):
        zero = jnp.zeros_like(x)
        return jnp.concatenate([jnp.where(lane_head == j, x, zero) for j in range(per)], axis=0)

    def unstack(x):
        got = x[0:BLOCK]
        for j in range(1, per):
            got = jnp.where(lane_head == j, x[j * BLOCK : (j + 1) * BLOCK], got)
        return got

    def chunk(j):
        g, h = t.place(j)
        slot = t.slot(g, h)
        first = ((g * t.members + t.m) * heads + h) * per_chunk

        def block(b, carry):
            here = rows(slot * per_chunk + b, BLOCK)
            number = first + b
            window = pl.ds(pl.multiple_of(number * BLOCK, BLOCK), 3 * BLOCK)
            keys[pl.ds(0, 3)] = kv[pl.ds(number, 3)]
            spot = (h * per_chunk + b) * RANDOM
            for r in range(RANDOM):
                keys[3 + r] = kv[table[g, 0, spot + r] + 1]
            bad = ((where == 0) & (number == 0)) | ((where == 2) & (number == n * run - 1))
            q = stack(qd[here, at]) * scale
            do = stack(qd[here, vat])
            k = keys[:, :, at].reshape(PARTS * BLOCK, LANES)
            v = keys[:, :, vat].reshape(PARTS * BLOCK, LANES)
            scores = jnp.where(bad, MASKED, dot(k, q, 1, 1))
            raw = jnp.exp(scores - jnp.max(scores, axis=0, keepdims=True))
            probs = raw * (1.0 / jnp.sum(raw, axis=0, keepdims=True))
            half = probs.astype(jnp.bfloat16)
            pgrad = dot(v, do, 1, 1)
            delta = jnp.sum(half.astype(jnp.float32) * pgrad, axis=0, keepdims=True)
            ds = (probs * (pgrad - delta)).astype(jnp.bfloat16)
            od[here, at] = unstack(dot(half, v, 0, 0)).astype(jnp.bfloat16)
            od[here, vat] = (unstack(dot(ds, k, 0, 0)) * HEAD_DIM ** (-0.5)).astype(jnp.bfloat16)
            for x, y, to in ((ds, q, at), (half, do, vat)):
                got = dot(x, y, 1, 0)
                acc[window, to] += got[: 3 * BLOCK]
                for r in range(RANDOM):
                    low = (3 + r) * BLOCK
                    extra[g * requests + spot + r, :, to] = got[low : low + BLOCK]
                for k2 in range(GLOBALS):
                    low = (3 + RANDOM + k2) * BLOCK
                    extra[groups * requests + k2, :, to] += got[low : low + BLOCK]
            return carry

        lax.fori_loop(0, per_chunk, block, 0, unroll=2)

    mine = t.columns(t.g, t.h)

    def source(a, j):
        g, h = t.place(j)
        return (od.at[rows(t.slot(g, h), tokens), lanes(a)] if a < 2
                else final.at[rows(j, tokens), lanes(a)])

    def back(a, j):
        g, h = t.place(j)
        return send_to(source(a, j), dests[a].at[:, mine], bsend.at[a * count + j],
                       brecv.at[a * count + t.me], t.device(g, h))

    def back_keep(a):
        return pltpu.make_async_copy(source(a, 0), dests[a].at[:, mine], blocal.at[a])

    def returned(a, j):
        g, h = t.place(j)
        return send_to(source(a, j), dests[a].at[:, t.columns(g, h)], bsend.at[a * count + j],
                       brecv.at[a * count + t.slot(g, h)], t.device(g, h))

    for a in (2, 3):
        keep(a).wait()
    chunk(0)
    for a in (0, 1):
        back_keep(a).start()

    def one(j, carry):
        for a in (2, 3):
            arrived(a, j).wait_recv()
        chunk(j)
        for a in (0, 1):
            back(a, j).start()
        return carry

    lax.fori_loop(1, count, one, 0)

    order = list(reversed(t.bits))
    handed = []
    held = list(range(t.members))
    for bit in order:
        handed.append([x for x in held if x & bit])
        held = [x for x in held if not x & bit]
    boxes = [(stage, mask) for stage in range(len(order)) for mask in handed[stage]]

    def box(stage, mask, j):
        return rows(boxes.index((stage, mask)) * count + j, tokens)

    def trade(stage, mask, j):
        at = (stage * t.members + mask) * count + j
        if stage == 0:
            src = part.at[rows(handed[0].index(mask) * count + j, tokens)]
        else:
            src = sums.at[rows((stage - 1) * count + j, tokens)]
        return send_to(src, inbox.at[box(stage, mask, j)], tsend.at[at], trecv.at[at],
                       t.mate_device(order[stage]))

    def total(ref, base, mask, j, upto):
        g, h = t.place(j)
        lows = [(boxes.index((stage, mask ^ order[stage])) * count + j) * per_chunk
                for stage in range(upto)]
        first = ((g * t.members + (t.m ^ mask)) * heads + h) * per_chunk

        def strip(b, carry):
            x = acc[rows(first + b + 1, BLOCK)]
            for q in range(groups):
                x = x + extra[table[q, 1, first + b]]
            for k in range(GLOBALS):
                x = x + extra[table[0, 2 + k, first + b]]
            for low in lows:
                x = x + inbox[rows(low + b, BLOCK)].astype(jnp.float32)
            ref[rows(base * per_chunk + b, BLOCK)] = x.astype(jnp.bfloat16)
            return carry

        lax.fori_loop(0, per_chunk, strip, 0)

    js = list(range(1, count)) + [0]
    for j in js:
        for mask in reversed(handed[0]):
            total(part, handed[0].index(mask) * count + j, mask, j, 0)
            trade(0, mask, j).start()
    for stage in range(1, len(order)):
        for j in js:
            for mask in handed[stage]:
                for before in range(stage):
                    trade(before, mask ^ order[before], j).wait_recv()
                total(sums, (stage - 1) * count + j, mask, j, stage)
                trade(stage, mask, j).start()
    for j in js:
        for stage in range(len(order)):
            trade(stage, order[stage], j).wait_recv()
        total(final, j, 0, j, len(order))
        for a in (2, 3):
            (back(a, j) if j else back_keep(a)).start()
    for stage in stages:
        for mask in masks(stage):
            for j in range(count):
                forward(stage, mask, j, True).wait_send()
        for mask in handed[stage]:
            for j in js:
                trade(stage, mask, j).wait_send()
    for c in idm:
        c.wait_send()
    for a in range(4):
        back_keep(a).wait()
        for j in range(1, count):
            move(a, j).wait_send()
            back(a, j).wait_send()
            returned(a, j).wait_recv()


def grouped(n, heads, groups, query_rows, key_rows, value_rows, out_grad, random_blocks,
            global_blocks):
    bf = jnp.bfloat16
    tokens, full = query_rows.shape
    members = n // groups
    count = groups * heads
    everything = n * heads * tokens
    held = count * tokens
    bits = members.bit_length() - 1
    run = heads * tokens // BLOCK
    requests = RANDOM * run
    dma = pltpu.SemaphoreType.DMA
    sds = jax.ShapeDtypeStruct
    total = n * run
    blank = groups * requests + GLOBALS
    span = -(-max(total, requests) // 128) * 128
    flat = random_blocks.reshape(requests)
    names = jnp.arange(total, dtype=jnp.int32)
    base = (lax.axis_index("seq") // members) * requests - blank
    slots = base + jnp.arange(requests, dtype=jnp.int32)
    found = jnp.sum(jnp.where(flat[None, :] == names[:, None], slots[None, :], 0), axis=1) + blank
    shared = [jnp.where(global_blocks[k] == names, groups * requests + k, blank)
              for k in range(GLOBALS)]
    lines = [jnp.pad(x.astype(jnp.int32), (0, span - x.shape[0])) for x in [flat, found] + shared]
    ids = jnp.pad(jnp.stack(lines), ((0, 8 - len(lines)), (0, 0)))
    blocked = (tokens // BLOCK, BLOCK, full)
    key_rows, value_rows = key_rows.reshape(blocked), value_rows.reshape(blocked)
    query_rows, key_rows, value_rows, out_grad = (
        pltpu.with_memory_space_constraint(x, pltpu.HBM)
        for x in (query_rows, key_rows, value_rows, out_grad)
    )
    f32 = jnp.float32
    results = pl.pallas_call(
        partial(kernel_all, n, heads, groups),
        out_shape=(sds((tokens, full), bf),) * 4,
        in_specs=[SMEM] + [HBM] * 4 + [VMEM],
        out_specs=(VMEM,) * 4,
        scratch_shapes=[
            pltpu.VMEM((total + 2, BLOCK, WIDE), bf), pltpu.VMEM((held, WIDE), bf),
            pltpu.VMEM((held, WIDE), bf), pltpu.VMEM((everything + 2 * BLOCK, WIDE), f32),
            pltpu.VMEM((groups * requests + GLOBALS + 1, BLOCK, WIDE), f32),
            pltpu.VMEM((PARTS, BLOCK, WIDE), bf), pltpu.VMEM((groups, 8, span), jnp.int32),
            pltpu.SMEM((groups, 8, span), jnp.int32),
            pltpu.VMEM((members // 2 * held, WIDE), bf),
            pltpu.VMEM(((members - 1) * held, WIDE), bf),
            pltpu.VMEM((max(bits - 1, 1) * held, WIDE), bf), pltpu.VMEM((held, WIDE), bf),
            dma((4 * count,)), dma((4 * count,)), dma((6,)),
            dma((bits * members * count,)), dma((bits * members * count,)),
            dma((groups,)), dma((groups,)),
            dma((4 * count,)), dma((4 * count,)), dma((4,)),
            dma((bits * members * count,)), dma((bits * members * count,)),
        ],
        compiler_params=pltpu.CompilerParams(
            collective_id=0, has_side_effects=True, vmem_limit_bytes=44 * 1024 * 1024
        ),
        name="everything",
    )(global_blocks, key_rows, value_rows, query_rows, out_grad, ids)
    return pl.pallas_call(
        kernel_store,
        out_shape=(sds((tokens, full), bf),) * 4,
        in_specs=[VMEM] * 4,
        out_specs=(HBM,) * 4,
        scratch_shapes=[dma((4,))],
        compiler_params=pltpu.CompilerParams(vmem_limit_bytes=16 * 1024 * 1024),
        name="store",
    )(*results)


def chosen(n, heads, query_rows, *others):
    tokens, full = query_rows.shape
    groups = full // LANES // heads
    fits = n * heads * tokens * WIDE * 6 <= 24 * 1024 * 1024
    if full % (LANES * heads) == 0 and n % groups == 0 and fits and n // groups in (2, 4):
        return grouped(n, heads, groups, query_rows, *others)
    return body(n, heads, query_rows, *others)


def solution(mesh):
    rows_spec = P(("seq", "head"), None)
    return jax.shard_map(
        partial(chosen, mesh.shape["seq"], mesh.shape["head"]),
        mesh=mesh,
        in_specs=(rows_spec,) * 4 + (P("seq", None), P()),
        out_specs=(rows_spec,) * 4,
        check_vma=False,
    )
```

```python
from functools import partial

import jax
import jax.numpy as jnp
from jax import lax
from jax.experimental import pallas as pl
from jax.experimental.pallas import tpu as pltpu
from jax.sharding import PartitionSpec as P

HEAD_DIM = 64
BLOCK = 64
RANDOM = 2
GLOBALS = 2
PARTS = 3 + RANDOM + GLOBALS
MASKED = -1e30
MESH = pl.DeviceIdType.MESH
VMEM = pl.BlockSpec(memory_space=pltpu.VMEM)
HBM = pl.BlockSpec(memory_space=pltpu.HBM)
SMEM = pl.BlockSpec(memory_space=pltpu.SMEM)


def params(cid):
    return pltpu.CompilerParams(
        collective_id=cid, has_side_effects=True, vmem_limit_bytes=24 * 1024 * 1024
    )


def greet(n, heads):
    s, h = lax.axis_index("seq"), lax.axis_index("head")
    barrier = pltpu.get_barrier_semaphore()
    if n > 0:

        def hello(d, c):
            pl.semaphore_signal(
                barrier, inc=1, device_id={"seq": lax.rem(s + d, n)}, device_id_type=MESH
            )
            return c

        lax.fori_loop(1, n, hello, 0)
    for d in range(1, heads):
        pl.semaphore_signal(
            barrier, inc=1, device_id={"head": lax.rem(h + d, heads)}, device_id_type=MESH
        )
    pl.semaphore_wait(barrier, max(n - 1, 0) + heads - 1)


def cols(index, width, base=0):
    return pl.ds(pl.multiple_of(base + index * width, 128), width)


def rows(index, count):
    return pl.ds(pl.multiple_of(index * count, 16), count)


def each(n, f):
    def step(d, c):
        f(d)
        return c

    lax.fori_loop(1, n, step, 0)


def remote(src, dst, send, recv, **where):
    return pltpu.make_async_remote_copy(
        src_ref=src, dst_ref=dst, send_sem=send, recv_sem=recv, device_id=where,
        device_id_type=MESH,
    )


def exchange(view, heads, send, recv, local, base):
    h = lax.axis_index("head")
    copies = []
    for d in range(1, heads):
        peer = lax.rem(h + d, heads)
        source, target = view(h, peer)
        at = base * heads + d
        copies.append(remote(source, target, send.at[at], recv.at[at], head=peer))
    source, target = view(h, h)
    return copies + [pltpu.make_async_copy(source, target, local.at[base])]


def start(copies):
    for c in copies:
        c.start()


def wait(copies):
    for c in copies:
        c.wait()


def to_heads(src, dst, tokens, width):
    return lambda a, b: (src.at[:, cols(b, width)], dst.at[rows(a, tokens), :])


def piece_in(src, dst, width, offset, size):
    nt = src.shape[0]
    return lambda a, b: (
        src.at[:, :, pl.ds(pl.multiple_of(b * width + offset, 128), size)],
        dst.at[pl.ds(a * nt, nt)],
    )


def to_tokens(src, dst, tokens, width):
    return lambda a, b: (src.at[rows(b, tokens), :], dst.at[:, cols(a, width)])


def piece_out(src, dst, tokens, width, offset, size, base):
    return lambda a, b: (
        src.at[rows(b, tokens), pl.ds(base, size)],
        dst.at[:, pl.ds(pl.multiple_of(a * width + offset, 128), size)],
    )


def kernel_in(n, heads, size, key, ids, pair, ids_all, send, recv, local, isend, irecv):
    s = lax.axis_index("seq")
    greet(n, heads)
    copies = exchange(
        piece_in(key, pair, key.shape[2] // heads, 0, size), heads, send, recv, local, 0
    )

    def idc(d):
        return remote(ids, ids_all.at[s], isend.at[d], irecv.at[d], seq=lax.rem(s + d, n))

    mine = pltpu.make_async_copy(ids, ids_all.at[s], local.at[1])
    start(copies)
    each(n, lambda d: idc(d).start())
    mine.start()
    each(n, lambda d: idc(d).wait())
    mine.wait()
    wait(copies)


def halo(n, low, high, got, send, recv, at=0):
    s = lax.axis_index("seq")
    up, down = 2 * at, 2 * at + 1
    here = pl.ds(at * low.shape[1], low.shape[1])
    return [
        remote(high, got.at[0, :, here], send.at[up], recv.at[up], seq=lax.rem(s + 1, n)),
        remote(low, got.at[1, :, here], send.at[down], recv.at[down], seq=lax.rem(s + n - 1, n)),
    ]


def far_first(n, make):
    def go(i, c):
        make(n // 2 + ((i + 1) // 2) * (2 * lax.rem(i, 2) - 1)).start()
        return c

    lax.fori_loop(0, n - 1, go, 0)


def random_piece(n, c, src_of, dst, size, send, recv):
    s = lax.axis_index("seq")

    def make(d):
        peer = lax.rem(s + d, n)
        return remote(
            src_of(peer), dst.at[s, :, pl.ds(c * size, size)], send.at[c * n + d],
            recv.at[c * n + d], seq=peer,
        )

    return make


class Shared:
    def __init__(self, n, src, here, mine, layer, done, every, sems):
        s = lax.axis_index("seq")
        gs, gr, ls, lr, fs, fr, loc = sems
        self.group = group = src.shape[0]
        self.layers = n // group
        self.me, self.level = lax.rem(s, group), s // group
        self.mine, self.layer, self.done, self.every, self.here = mine, layer, done, every, here
        self.step1 = [pltpu.make_async_copy(src.at[self.me], here.at[self.me], loc.at[0])]
        self.step3 = []
        for j in range(1, group):
            to = lax.rem(self.me + j, group)
            peer = self.level * group + to
            self.step1.append(remote(src.at[to], here.at[self.me], gs.at[j], gr.at[j], seq=peer))
            self.step3.append(remote(done, every.at[self.me], fs.at[j], fr.at[j], seq=peer))
        self.across = lambda j: remote(
            mine, layer.at[self.level], ls.at[j], lr.at[j],
            seq=lax.rem(self.level + j, self.layers) * group + self.me,
        )

    def middle(self, combine):
        wait(self.step1)
        part = combine(self.here)
        self.mine[...] = part
        self.layer[self.level] = part
        each(self.layers, lambda j: self.across(j).start())

    def finish(self, combine):
        each(self.layers, lambda j: self.across(j).wait())
        total = combine(self.layer)
        self.done[...] = total
        self.every[self.me] = total
        start(self.step3)


def kernel_fetch(n, heads, pieces, served, owners, owned_at, query, grad, key, value, first, ready,
                 qh, gh, incoming, halos, gall, *rest):
    landed, rest = (first,) + rest[: pieces - 1], rest[pieces - 1 :]
    outgoing, gsrc, ghere, gmine, glayer, gdone = rest[:6]
    send, recv, local, bs, br, hs, hr, *gsems = rest[6:]
    s = lax.axis_index("seq")
    tokens, width = query.shape[0], query.shape[1] // heads
    size = 2 * width // pieces
    nb = first.shape[0]
    half = pieces // 2
    greet(n, heads)
    moves = [[]]
    for c in range(1, pieces):
        src = key if c < half else value
        moves.append(exchange(
            piece_in(src, landed[c], width, (c % half) * size, size),
            heads, send, recv, local, c,
        ))
    blocks = [
        random_piece(n, c, (lambda p, c=c: (ready.at[p] if c == 0 else outgoing.at[c - 1, p])),
                     incoming, size, bs, br)
        for c in range(pieces)
    ]
    qmove = exchange(to_heads(query, qh, tokens, width), heads, send, recv, local, pieces)
    qmove += exchange(to_heads(grad, gh, tokens, width), heads, send, recv, local, pieces + 1)
    edges = []
    for c in range(pieces):
        edges += halo(n, landed[c].at[0], landed[c].at[nb - 1], halos, hs, hr, c)
    shared = Shared(n, gsrc, ghere, gmine, glayer, gdone, gall, gsems)
    for m in moves:
        start(m)
    far_first(n, blocks[0])
    start(qmove)
    keep = pltpu.make_async_copy(ready.at[s], incoming.at[s, :, pl.ds(0, size)],
                                 local.at[pieces + 2])
    keep.start()
    for c in range(1, pieces):
        wait(moves[c])
        at = pl.ds(c * size, size)

        def gather(i, carry):
            outgoing[c - 1, i] = landed[c][served[i]]
            return carry

        lax.fori_loop(0, n, gather, 0)
        incoming[s, :, at] = landed[c][served[s]]
        if c == pieces - 1:
            group = gsrc.shape[0]
            per = group // GLOBALS
            count = BLOCK // per
            for m in range(group):
                low = (m % per) * count
                for k in range(pieces):
                    gsrc[m, :, pl.ds(k * size, size)] = landed[k][
                        owned_at[m // per], pl.ds(low, count), :
                    ]
            start(shared.step1 + edges)
            mine = owners[shared.me * GLOBALS // group]
            shared.middle(lambda ref: ref[lax.rem(mine, group)])
        far_first(n, blocks[c])
    shared.finish(lambda ref: ref[mine // group])
    keep.wait()
    wait(edges + qmove + shared.step3)
    for c in range(pieces):
        each(n, lambda d: blocks[c](d).wait())


def kernel_return(n, heads, pieces, served, owners, owned_at, att, qg, sending, edge, gsend, wsum,
                  out, qout, kout, vout, returned, halos, gall, summed, ghere, gmine, glayer,
                  gdone, send, recv, local, bs, br, hs, hr, *gsems):
    s = lax.axis_index("seq")
    width = att.shape[1]
    tokens = att.shape[0] // heads
    nb = att.shape[0] // BLOCK
    size = 2 * width // pieces
    half = pieces // 2
    greet(n, heads)
    moves = [
        exchange(
            piece_out(summed, kout if c < half else vout, tokens, width, (c % half) * size, size,
                      c * size),
            heads, send, recv, local, c,
        )
        for c in range(pieces)
    ]
    blocks = [
        random_piece(n, c, lambda p, c=c: sending.at[p, :, pl.ds(c * size, size)], returned, size,
                     bs, br)
        for c in range(pieces)
    ]
    qmove = exchange(to_tokens(att, out, tokens, width), heads, send, recv, local, pieces)
    qmove += exchange(to_tokens(qg, qout, tokens, width), heads, send, recv, local, pieces + 1)
    edges = halo(n, edge.at[0], edge.at[1], halos, hs, hr)
    shared = Shared(n, gsend, ghere, gmine, glayer, gdone, gall, gsems)
    keep = pltpu.make_async_copy(sending.at[s], returned.at[s], local.at[pieces + 2])

    def combine(ref):
        def add(i, acc):
            return acc + ref[i].astype(jnp.float32)

        zero = jnp.zeros(ref.shape[1:], jnp.float32)
        return lax.fori_loop(0, ref.shape[0], add, zero).astype(jnp.bfloat16)

    start(shared.step1 + edges)
    far_first(n, blocks[0])
    start(qmove + [keep])
    shared.middle(combine)
    for c in range(1, pieces):
        far_first(n, blocks[c])
    shared.finish(combine)
    keep.wait()
    wait(edges + shared.step3)
    strip = 16
    per = shared.group // GLOBALS
    count = BLOCK // per

    def weight(cond):
        return jnp.where(cond, 1.0, 0.0).astype(jnp.float32)

    for c in range(pieces):
        each(n, lambda d: blocks[c](d).wait())
        at = pl.ds(c * size, size)

        def one_strip(t, carry):
            low = pl.multiple_of(t * strip, strip)
            here = pl.ds(low, strip)
            acc = [wsum[pl.ds(pl.multiple_of((j + 1) * BLOCK + low, strip), strip), at]
                   for j in range(nb)]
            acc[0] = acc[0] + halos[0, here, at].astype(jnp.float32)
            acc[-1] = acc[-1] + halos[1, here, at].astype(jnp.float32)
            for g in range(GLOBALS):
                inside = pl.ds(pl.multiple_of(lax.rem(low, count), strip), strip)
                extra = gall[g * per + low // count, inside, at].astype(jnp.float32)
                for j in range(nb):
                    hit = (owners[g] == s) & (owned_at[g] == j)
                    acc[j] = acc[j] + weight(hit) * extra

            def add(i, accs):
                x = returned[i, here, at].astype(jnp.float32)
                which = served[i]
                return tuple(accs[j] + weight(which == j) * x for j in range(nb))

            acc = lax.fori_loop(0, n, add, tuple(acc))
            for j in range(nb):
                summed[pl.ds(pl.multiple_of(j * BLOCK + low, strip), strip), at] = acc[j].astype(
                    jnp.bfloat16
                )
            return carry

        lax.fori_loop(0, BLOCK // strip, one_strip, 0)
        start(moves[c])
    wait(qmove)
    for m in moves:
        wait(m)


def dot(a, b, ca, cb):
    return lax.dot_general(a, b, (((ca,), (cb,)), ((), ())), preferred_element_type=jnp.float32)


def kernel_attend(n, lanes, pieces, slots, qh, gh, halos, incoming, gall, *rest):
    landed, rest = rest[:pieces], rest[pieces:]
    att, qg, wsum, edge, sending, gsum, pairs, keys, gacc = rest
    nb = qh.shape[0] // BLOCK
    width = qh.shape[1]
    s = lax.axis_index("seq")
    per = lanes // HEAD_DIM
    scale = jnp.asarray(HEAD_DIM ** (-0.5), jnp.bfloat16)
    pairs[pl.ds(0, BLOCK)] = halos[0]
    size = landed[0].shape[1]
    for c in range(pieces):
        pairs[pl.ds(BLOCK, nb * BLOCK), pl.ds(c * size, size)] = landed[c][...]
    pairs[pl.ds((nb + 1) * BLOCK, BLOCK)] = halos[1]
    keys[pl.ds((3 + RANDOM) * BLOCK, GLOBALS * BLOCK)] = gall[...]
    gacc[...] = jnp.zeros_like(gacc)
    wsum[...] = jnp.zeros_like(wsum)
    if n > RANDOM * nb:
        sending[...] = jnp.zeros_like(sending)
    lane_head = lax.broadcasted_iota(jnp.int32, (BLOCK, lanes), 1) // HEAD_DIM
    part = lax.broadcasted_iota(jnp.int32, (PARTS * BLOCK, 1), 0) // BLOCK

    def stack(x):
        zero = jnp.zeros_like(x)
        return jnp.concatenate([jnp.where(lane_head == j, x, zero) for j in range(per)], axis=0)

    def unstack(x):
        got = x[0:BLOCK]
        for j in range(1, per):
            got = jnp.where(lane_head == j, x[j * BLOCK : (j + 1) * BLOCK], got)
        return got

    def block(b, carry):
        here = pl.ds(pl.multiple_of(b * BLOCK, BLOCK), BLOCK)
        window = pl.ds(pl.multiple_of(b * BLOCK, BLOCK), 3 * BLOCK)
        keys[pl.ds(0, 3 * BLOCK)] = pairs[window]
        for r in range(RANDOM):
            keys[pl.ds((3 + r) * BLOCK, BLOCK)] = incoming[slots[b * RANDOM + r]]
        number = s * nb + b
        bad = ((part == 0) & (number == 0)) | ((part == 2) & (number == n * nb - 1))
        for g in range(width // lanes):
            at = pl.ds(g * lanes, lanes)
            vat = pl.ds(width + g * lanes, lanes)
            q = stack(qh[here, at]) * scale
            do = stack(gh[here, at])
            k = keys[:, at]
            v = keys[:, vat]
            scores = jnp.where(bad, MASKED, dot(k, q, 1, 1))
            raw = jnp.exp(scores - jnp.max(scores, axis=0, keepdims=True))
            probs = raw * (1.0 / jnp.sum(raw, axis=0, keepdims=True))
            half = probs.astype(jnp.bfloat16)
            pgrad = dot(v, do, 1, 1)
            delta = jnp.sum(half.astype(jnp.float32) * pgrad, axis=0, keepdims=True)
            ds = (probs * (pgrad - delta)).astype(jnp.bfloat16)
            att[here, at] = unstack(dot(half, v, 0, 0)).astype(jnp.bfloat16)
            qg[here, at] = (unstack(dot(ds, k, 0, 0)) * HEAD_DIM ** (-0.5)).astype(jnp.bfloat16)
            for x, y, to in ((ds, q, at), (half, do, vat)):
                grad = dot(x, y, 1, 0)
                wsum[window, to] += grad[: 3 * BLOCK]
                for r in range(RANDOM):
                    low = (3 + r) * BLOCK
                    sending[slots[b * RANDOM + r], :, to] = grad[low : low + BLOCK].astype(
                        jnp.bfloat16
                    )
                gacc[:, to] += grad[(3 + RANDOM) * BLOCK :]
        return carry

    lax.fori_loop(0, nb, block, 0, unroll=2)
    edge[0] = wsum[pl.ds(0, BLOCK)].astype(jnp.bfloat16)
    edge[1] = wsum[pl.ds((nb + 1) * BLOCK, BLOCK)].astype(jnp.bfloat16)
    gsum[...] = gacc[...].astype(jnp.bfloat16)


def kernel_store(a, b, c, d, wa, wb, wc, wd, sem):
    copies = [
        pltpu.make_async_copy(x, y, sem.at[i])
        for i, (x, y) in enumerate(((a, wa), (b, wb), (c, wc), (d, wd)))
    ]
    start(copies)
    wait(copies)


def body(n, heads, query_rows, key_rows, value_rows, out_grad, random_blocks, global_blocks):
    bf = jnp.bfloat16
    tokens, full = query_rows.shape
    width = full // heads
    total = tokens * heads
    nb = total // BLOCK
    me = lax.axis_index("seq")
    dma = pltpu.SemaphoreType.DMA
    sds = jax.ShapeDtypeStruct
    requests = RANDOM * nb
    flat = random_blocks.reshape(requests)
    ids = jnp.broadcast_to(jnp.pad(flat, (0, 128 - requests))[None], (8, 128))
    pieces = min(4, 2 * width // 128)
    size = 2 * width // pieces
    blocked = (tokens // BLOCK, BLOCK, full)
    key_blocks, value_blocks = key_rows.reshape(blocked), value_rows.reshape(blocked)
    query_rows, key_blocks, value_blocks, out_grad = (
        pltpu.with_memory_space_constraint(x, pltpu.HBM)
        for x in (query_rows, key_blocks, value_blocks, out_grad)
    )
    first, ids_all = pl.pallas_call(
        partial(kernel_in, n, heads, size),
        out_shape=(sds((nb, BLOCK, size), bf), sds((n, 8, 128), jnp.int32)),
        in_specs=[HBM, VMEM],
        out_specs=(VMEM,) * 2,
        scratch_shapes=[dma((heads,)), dma((heads,)), dma((2,)), dma((n,)), dma((n,))],
        compiler_params=params(0),
        name="head_in",
    )(key_blocks, ids)
    asked = ids_all[:, 0, :requests]
    served = jnp.sum(jnp.where(asked // nb == me, asked % nb, 0), axis=1).astype(jnp.int32)
    owners = global_blocks // nb
    owned_at = global_blocks % nb
    ready = jnp.take(first, served, axis=0, mode="clip")
    group = 4
    layers = n // group
    chunk = GLOBALS * BLOCK // group
    slab = sds((n, BLOCK, 2 * width), bf)
    small = sds((group, chunk, 2 * width), bf)
    wide = (chunk, 2 * width)
    scratch = [
        pltpu.VMEM(small.shape, bf), pltpu.VMEM(wide, bf), pltpu.VMEM((layers,) + wide, bf),
        pltpu.VMEM(wide, bf),
        dma(((pieces + 2) * heads,)), dma(((pieces + 2) * heads,)), dma((pieces + 3,)),
        dma((pieces * n,)), dma((pieces * n,)), dma((2 * pieces,)), dma((2 * pieces,)),
        dma((group,)), dma((group,)), dma((layers,)), dma((layers,)), dma((group,)),
        dma((group,)), dma((1,)),
    ]
    edges = sds((2, BLOCK, 2 * width), bf)
    qh, gh, incoming, halos, gall, *landed = pl.pallas_call(
        partial(kernel_fetch, n, heads, pieces),
        out_shape=(sds((total, width), bf), sds((total, width), bf), slab, edges, small)
        + (sds((nb, BLOCK, size), bf),) * (pieces - 1),
        in_specs=[SMEM] * 3 + [HBM] * 4 + [VMEM] * 2,
        out_specs=(VMEM,) * (4 + pieces),
        scratch_shapes=[pltpu.VMEM((pieces - 1, n, BLOCK, size), bf), pltpu.VMEM(small.shape, bf)]
        + scratch,
        compiler_params=params(1),
        name="fetch",
    )(served, owners, owned_at, query_rows, out_grad, key_blocks, value_blocks, first, ready)
    gwide = (GLOBALS * BLOCK, 2 * width)
    att, qg, wsum, edge, sending, gsum = pl.pallas_call(
        partial(kernel_attend, n, min(256, width), pieces),
        out_shape=(
            sds((total, width), bf), sds((total, width), bf),
            sds(((nb + 2) * BLOCK, 2 * width), jnp.float32), edges, slab, sds(gwide, bf),
        ),
        in_specs=[SMEM] + [VMEM] * (5 + pieces),
        out_specs=(VMEM,) * 6,
        scratch_shapes=[
            pltpu.VMEM(((nb + 2) * BLOCK, 2 * width), bf),
            pltpu.VMEM((PARTS * BLOCK, 2 * width), bf),
            pltpu.VMEM(gwide, jnp.float32),
        ],
        compiler_params=pltpu.CompilerParams(vmem_limit_bytes=24 * 1024 * 1024),
        name="attend",
    )(flat // nb, qh, gh, halos, incoming, gall.reshape(gwide),
      *[x.reshape(total, size) for x in (first, *landed)])
    results = pl.pallas_call(
        partial(kernel_return, n, heads, pieces),
        out_shape=(sds((tokens, full), bf),) * 4,
        in_specs=[SMEM] * 3 + [VMEM] * 6,
        out_specs=(VMEM,) * 4,
        scratch_shapes=[
            pltpu.VMEM(slab.shape, bf), pltpu.VMEM(edges.shape, bf), pltpu.VMEM(small.shape, bf),
            pltpu.VMEM((total, 2 * width), bf),
        ] + scratch,
        compiler_params=params(2),
        name="give_back",
    )(served, owners, owned_at, att, qg, sending, edge, gsum.reshape(group, chunk, 2 * width),
      wsum)
    return pl.pallas_call(
        kernel_store,
        out_shape=(sds((tokens, full), bf),) * 4,
        in_specs=[VMEM] * 4,
        out_specs=(HBM,) * 4,
        scratch_shapes=[dma((4,))],
        compiler_params=pltpu.CompilerParams(vmem_limit_bytes=16 * 1024 * 1024),
        name="store",
    )(*results)


LANES = 128
WIDE = 2 * LANES


class Team:
    def __init__(self, n, heads, groups, tokens):
        self.n, self.heads, self.groups, self.tokens = n, heads, groups, tokens
        self.members = n // groups
        s, self.h = lax.axis_index("seq"), lax.axis_index("head")
        self.g, self.m = s // self.members, lax.rem(s, self.members)
        self.bits = [1 << i for i in reversed(range(self.members.bit_length() - 1))]
        self.places = [(i, d) for i in range(groups) for d in range(heads)]
        self.me = self.slot(self.g, self.h)

    def slot(self, g, h):
        return g * self.heads + h

    def near(self, i):
        total = self.g * 0
        for g in range(self.groups):
            order = sorted(range(self.groups), key=lambda k: (k != g, -abs(k - g), k))
            total = total + jnp.where(self.g == g, order[i], 0)
        return total

    def place(self, j):
        if isinstance(j, int):
            i, d = self.places[j]
            return (self.near(i) if i else self.g), lax.rem(self.h + d, self.heads)
        g = self.g * 0
        for i in range(self.groups):
            g = g + jnp.where(j // self.heads == i, self.near(i), 0)
        return g, lax.rem(self.h + lax.rem(j, self.heads), self.heads)

    def device(self, g, h):
        return {"seq": g * self.members + self.m, "head": h}

    def mate(self, bit):
        return self.m ^ bit

    def mate_device(self, bit):
        return {"seq": self.g * self.members + self.mate(bit)}

    def chunk(self, g, h, m):
        return rows((g * self.members + m) * self.heads + h, self.tokens)

    def columns(self, g, h):
        return pl.ds(pl.multiple_of((h * self.groups + g) * LANES, LANES), LANES)

    def greet(self):
        barrier = pltpu.get_barrier_semaphore()
        for j in range(1, len(self.places)):
            pl.semaphore_signal(
                barrier, inc=1, device_id=self.device(*self.place(j)), device_id_type=MESH
            )
        for bit in self.bits:
            pl.semaphore_signal(
                barrier, inc=1, device_id=self.mate_device(bit), device_id_type=MESH
            )
        pl.semaphore_wait(barrier, len(self.places) - 1 + len(self.bits))


def send_to(src, dst, send, recv, device):
    return pltpu.make_async_remote_copy(
        src_ref=src, dst_ref=dst, send_sem=send, recv_sem=recv, device_id=device,
        device_id_type=MESH,
    )


def kernel_all(n, heads, groups, named, owners, key, value, query, grad, out, qout, kout, vout,
               kv, qd, od, acc, extra, keys, ids, ids_all, table, part, inbox, sums, final, send, recv,
               local, fsend, frecv, isend, irecv, bsend, brecv, blocal, tsend, trecv):
    tokens = query.shape[0]
    t = Team(n, heads, groups, tokens)
    count = len(t.places)
    per_chunk = tokens // BLOCK
    run = heads * per_chunk
    requests = RANDOM * run
    blank = groups * requests + GLOBALS
    lane = lax.broadcasted_iota(jnp.int32, ids.shape, 1)
    row = lax.broadcasted_iota(jnp.int32, ids.shape, 0)
    entry = jnp.where(row == 0, 0, blank)
    for r in range(requests):
        name = named[r // RANDOM, r % RANDOM]
        entry = jnp.where((row == 0) & (lane == r), name, entry)
        entry = jnp.where((row == 1) & (lane == name), t.g * requests + r, entry)
    for k in range(GLOBALS):
        entry = jnp.where((row == 2 + k) & (lane == owners[k]), groups * requests + k, entry)
    ids[...] = entry
    t.greet()
    arrays = (key, value, query, grad)
    dests = (out, qout, kout, vout)

    def lanes(a):
        return pl.ds((a % 2) * LANES, LANES)

    def blocks_of(g, h, m):
        return pl.ds(((g * t.members + m) * heads + h) * per_chunk + 1, per_chunk)

    def leaving(a, g, h):
        ref = arrays[a]
        return ref.at[:, :, t.columns(g, h)] if a < 2 else ref.at[:, t.columns(g, h)]

    def landing(a, g, h):
        return (kv.at[blocks_of(g, h, t.m), :, lanes(a)] if a < 2
                else qd.at[rows(t.slot(g, h), tokens), lanes(a)])

    def move(a, j):
        g, h = t.place(j)
        return send_to(leaving(a, g, h), landing(a, t.g, t.h),
                       send.at[a * count + j], recv.at[a * count + t.me], t.device(g, h))

    def keep(a):
        return pltpu.make_async_copy(leaving(a, t.g, t.h), landing(a, t.g, t.h),
                                     local.at[a])

    def arrived(a, j):
        g, h = t.place(j)
        return send_to(leaving(a, g, h), landing(a, g, h),
                       send.at[a * count + j], recv.at[a * count + t.slot(g, h)],
                       t.device(g, h))

    idm = [send_to(ids, ids_all.at[t.g], isend.at[i], irecv.at[t.g], t.device(t.near(i), t.h))
           for i in range(1, groups)]
    idr = [send_to(ids, ids_all.at[t.near(i)], isend.at[i], irecv.at[t.near(i)],
                   t.device(t.near(i), t.h)) for i in range(1, groups)]
    for a in (0, 1):
        keep(a).start()
    for j in range(1, count):
        for a in (0, 1):
            move(a, j).start()
    start(idm)
    for a in (2, 3):
        keep(a).start()
    for j in range(1, count):
        for a in (2, 3):
            move(a, j).start()
    own = pltpu.make_async_copy(ids, ids_all.at[t.g], local.at[4])
    own.start()
    edge = jnp.zeros(kv.shape[1:], kv.dtype)
    kv[0] = edge
    kv[kv.shape[0] - 1] = edge
    empty = jnp.zeros((BLOCK, WIDE), jnp.float32)
    for k in range(GLOBALS + 1):
        extra[groups * requests + k] = empty

    def clear(i, carry):
        acc[rows(i, BLOCK)] = empty
        return carry

    lax.fori_loop(0, acc.shape[0] // BLOCK, clear, 0)

    def forward(stage, mask, p, mine):
        bit = t.bits[stage]
        g, h = t.place(p // 2)
        owner = t.m ^ mask if mine else t.m ^ bit ^ mask
        ref = kv.at[blocks_of(g, h, owner), :, lanes(p)]
        at = (stage * t.members + mask) * 2 * count + p
        return send_to(ref, ref, fsend.at[at], frecv.at[at], t.mate_device(bit))

    def masks(stage):
        got = [0]
        for bit in t.bits[:stage]:
            got += [x ^ bit for x in got]
        return got

    stages = range(len(t.bits))
    pieces = 2 * count
    for step in range(pieces + 4 * len(t.bits)):
        for stage in reversed(stages):
            p = step - 4 * (stage + 1)
            if 0 <= p < pieces:
                for mask in masks(stage):
                    forward(stage, mask, p, False).wait_recv()
                    for later in range(stage + 1, len(t.bits)):
                        forward(later, mask ^ t.bits[stage], p, True).start()
        if step < pieces:
            if step < 2:
                keep(step).wait()
            else:
                arrived(step % 2, step // 2).wait_recv()
            for stage in stages:
                forward(stage, 0, step, True).start()
    own.wait()
    for c in idr:
        c.wait_recv()
    fill = pltpu.make_async_copy(ids_all, table, local.at[5])
    fill.start()
    fill.wait()

    per = LANES // HEAD_DIM
    scale = jnp.asarray(HEAD_DIM ** (-0.5), jnp.bfloat16)
    for k in range(GLOBALS):
        keys[3 + RANDOM + k] = kv[owners[k] + 1]
    lane_head = lax.broadcasted_iota(jnp.int32, (BLOCK, LANES), 1) // HEAD_DIM
    where = lax.broadcasted_iota(jnp.int32, (PARTS * BLOCK, 1), 0) // BLOCK
    at, vat = lanes(0), lanes(1)

    def stack(x):
        zero = jnp.zeros_like(x)
        return jnp.concatenate([jnp.where(lane_head == j, x, zero) for j in range(per)], axis=0)

    def unstack(x):
        got = x[0:BLOCK]
        for j in range(1, per):
            got = jnp.where(lane_head == j, x[j * BLOCK : (j + 1) * BLOCK], got)
        return got

    def chunk(j):
        g, h = t.place(j)
        slot = t.slot(g, h)
        first = ((g * t.members + t.m) * heads + h) * per_chunk

        def block(b, carry):
            here = rows(slot * per_chunk + b, BLOCK)
            number = first + b
            window = pl.ds(pl.multiple_of(number * BLOCK, BLOCK), 3 * BLOCK)
            keys[pl.ds(0, 3)] = kv[pl.ds(number, 3)]
            spot = (h * per_chunk + b) * RANDOM
            for r in range(RANDOM):
                keys[3 + r] = kv[table[g, 0, spot + r] + 1]
            bad = ((where == 0) & (number == 0)) | ((where == 2) & (number == n * run - 1))
            q = stack(qd[here, at]) * scale
            do = stack(qd[here, vat])
            k = keys[:, :, at].reshape(PARTS * BLOCK, LANES)
            v = keys[:, :, vat].reshape(PARTS * BLOCK, LANES)
            scores = jnp.where(bad, MASKED, dot(k, q, 1, 1))
            raw = jnp.exp(scores - jnp.max(scores, axis=0, keepdims=True))
            probs = raw * (1.0 / jnp.sum(raw, axis=0, keepdims=True))
            half = probs.astype(jnp.bfloat16)
            pgrad = dot(v, do, 1, 1)
            delta = jnp.sum(half.astype(jnp.float32) * pgrad, axis=0, keepdims=True)
            ds = (probs * (pgrad - delta)).astype(jnp.bfloat16)
            od[here, at] = unstack(dot(half, v, 0, 0)).astype(jnp.bfloat16)
            od[here, vat] = (unstack(dot(ds, k, 0, 0)) * HEAD_DIM ** (-0.5)).astype(jnp.bfloat16)
            for x, y, to in ((ds, q, at), (half, do, vat)):
                got = dot(x, y, 1, 0)
                acc[window, to] += got[: 3 * BLOCK]
                for r in range(RANDOM):
                    low = (3 + r) * BLOCK
                    extra[g * requests + spot + r, :, to] = got[low : low + BLOCK]
                for k2 in range(GLOBALS):
                    low = (3 + RANDOM + k2) * BLOCK
                    extra[groups * requests + k2, :, to] += got[low : low + BLOCK]
            return carry

        lax.fori_loop(0, per_chunk, block, 0, unroll=2)

    mine = t.columns(t.g, t.h)

    def source(a, j):
        g, h = t.place(j)
        return (od.at[rows(t.slot(g, h), tokens), lanes(a)] if a < 2
                else final.at[rows(j, tokens), lanes(a)])

    def back(a, j):
        g, h = t.place(j)
        return send_to(source(a, j), dests[a].at[:, mine], bsend.at[a * count + j],
                       brecv.at[a * count + t.me], t.device(g, h))

    def back_keep(a):
        return pltpu.make_async_copy(source(a, 0), dests[a].at[:, mine], blocal.at[a])

    def returned(a, j):
        g, h = t.place(j)
        return send_to(source(a, j), dests[a].at[:, t.columns(g, h)], bsend.at[a * count + j],
                       brecv.at[a * count + t.slot(g, h)], t.device(g, h))

    for a in (2, 3):
        keep(a).wait()
    chunk(0)
    for a in (0, 1):
        back_keep(a).start()

    def one(j, carry):
        for a in (2, 3):
            arrived(a, j).wait_recv()
        chunk(j)
        for a in (0, 1):
            back(a, j).start()
        return carry

    lax.fori_loop(1, count, one, 0)

    order = list(reversed(t.bits))
    handed = []
    held = list(range(t.members))
    for bit in order:
        handed.append([x for x in held if x & bit])
        held = [x for x in held if not x & bit]
    boxes = [(stage, mask) for stage in range(len(order)) for mask in handed[stage]]

    def box(stage, mask, j):
        return rows(boxes.index((stage, mask)) * count + j, tokens)

    def trade(stage, mask, j):
        at = (stage * t.members + mask) * count + j
        if stage == 0:
            src = part.at[rows(handed[0].index(mask) * count + j, tokens)]
        else:
            src = sums.at[rows((stage - 1) * count + j, tokens)]
        return send_to(src, inbox.at[box(stage, mask, j)], tsend.at[at], trecv.at[at],
                       t.mate_device(order[stage]))

    def total(ref, base, mask, j, upto):
        g, h = t.place(j)
        lows = [(boxes.index((stage, mask ^ order[stage])) * count + j) * per_chunk
                for stage in range(upto)]
        first = ((g * t.members + (t.m ^ mask)) * heads + h) * per_chunk

        def strip(b, carry):
            x = acc[rows(first + b + 1, BLOCK)]
            for q in range(groups):
                x = x + extra[table[q, 1, first + b]]
            for k in range(GLOBALS):
                x = x + extra[table[0, 2 + k, first + b]]
            for low in lows:
                x = x + inbox[rows(low + b, BLOCK)].astype(jnp.float32)
            ref[rows(base * per_chunk + b, BLOCK)] = x.astype(jnp.bfloat16)
            return carry

        lax.fori_loop(0, per_chunk, strip, 0)

    js = list(range(1, count)) + [0]
    for j in js:
        for mask in reversed(handed[0]):
            total(part, handed[0].index(mask) * count + j, mask, j, 0)
            trade(0, mask, j).start()
    for stage in range(1, len(order)):
        for j in js:
            for mask in handed[stage]:
                for before in range(stage):
                    trade(before, mask ^ order[before], j).wait_recv()
                total(sums, (stage - 1) * count + j, mask, j, stage)
                trade(stage, mask, j).start()
    for j in js:
        for stage in range(len(order)):
            trade(stage, order[stage], j).wait_recv()
        total(final, j, 0, j, len(order))
        for a in (2, 3):
            (back(a, j) if j else back_keep(a)).start()
    for stage in stages:
        for mask in masks(stage):
            for p in range(2 * count):
                forward(stage, mask, p, True).wait_send()
        for mask in handed[stage]:
            for j in js:
                trade(stage, mask, j).wait_send()
    for c in idm:
        c.wait_send()
    for a in range(4):
        back_keep(a).wait()
        for j in range(1, count):
            move(a, j).wait_send()
            back(a, j).wait_send()
            returned(a, j).wait_recv()


def grouped(n, heads, groups, query_rows, key_rows, value_rows, out_grad, random_blocks,
            global_blocks):
    bf = jnp.bfloat16
    tokens, full = query_rows.shape
    members = n // groups
    count = groups * heads
    everything = n * heads * tokens
    held = count * tokens
    bits = members.bit_length() - 1
    run = heads * tokens // BLOCK
    requests = RANDOM * run
    dma = pltpu.SemaphoreType.DMA
    sds = jax.ShapeDtypeStruct
    total = n * run
    span = -(-max(total, requests) // 128) * 128
    blocked = (tokens // BLOCK, BLOCK, full)
    key_rows, value_rows = key_rows.reshape(blocked), value_rows.reshape(blocked)
    query_rows, key_rows, value_rows, out_grad = (
        pltpu.with_memory_space_constraint(x, pltpu.HBM)
        for x in (query_rows, key_rows, value_rows, out_grad)
    )
    f32 = jnp.float32
    results = pl.pallas_call(
        partial(kernel_all, n, heads, groups),
        out_shape=(sds((tokens, full), bf),) * 4,
        in_specs=[SMEM] * 2 + [HBM] * 4,
        out_specs=(VMEM,) * 4,
        scratch_shapes=[
            pltpu.VMEM((total + 2, BLOCK, WIDE), bf), pltpu.VMEM((held, WIDE), bf),
            pltpu.VMEM((held, WIDE), bf), pltpu.VMEM((everything + 2 * BLOCK, WIDE), f32),
            pltpu.VMEM((groups * requests + GLOBALS + 1, BLOCK, WIDE), f32),
            pltpu.VMEM((PARTS, BLOCK, WIDE), bf), pltpu.VMEM((8, span), jnp.int32),
            pltpu.VMEM((groups, 8, span), jnp.int32),
            pltpu.SMEM((groups, 8, span), jnp.int32),
            pltpu.VMEM((members // 2 * held, WIDE), bf),
            pltpu.VMEM(((members - 1) * held, WIDE), bf),
            pltpu.VMEM((max(bits - 1, 1) * held, WIDE), bf), pltpu.VMEM((held, WIDE), bf),
            dma((4 * count,)), dma((4 * count,)), dma((6,)),
            dma((2 * bits * members * count,)), dma((2 * bits * members * count,)),
            dma((groups,)), dma((groups,)),
            dma((4 * count,)), dma((4 * count,)), dma((4,)),
            dma((bits * members * count,)), dma((bits * members * count,)),
        ],
        compiler_params=pltpu.CompilerParams(
            collective_id=0, has_side_effects=True, vmem_limit_bytes=44 * 1024 * 1024
        ),
        name="everything",
    )(random_blocks, global_blocks, key_rows, value_rows, query_rows, out_grad)
    return pl.pallas_call(
        kernel_store,
        out_shape=(sds((tokens, full), bf),) * 4,
        in_specs=[VMEM] * 4,
        out_specs=(HBM,) * 4,
        scratch_shapes=[dma((4,))],
        compiler_params=pltpu.CompilerParams(vmem_limit_bytes=16 * 1024 * 1024),
        name="store",
    )(*results)


def chosen(n, heads, query_rows, *others):
    tokens, full = query_rows.shape
    groups = full // LANES // heads
    fits = n * heads * tokens * WIDE * 6 <= 24 * 1024 * 1024
    if full % (LANES * heads) == 0 and n % groups == 0 and fits and n // groups in (2, 4):
        return grouped(n, heads, groups, query_rows, *others)
    return body(n, heads, query_rows, *others)


def solution(mesh):
    rows_spec = P(("seq", "head"), None)
    return jax.shard_map(
        partial(chosen, mesh.shape["seq"], mesh.shape["head"]),
        mesh=mesh,
        in_specs=(rows_spec,) * 4 + (P("seq", None), P()),
        out_specs=(rows_spec,) * 4,
        check_vma=False,
    )
```

```python
from functools import partial

import jax
import jax.numpy as jnp
from jax import lax
from jax.experimental import pallas as pl
from jax.experimental.pallas import tpu as pltpu
from jax.sharding import PartitionSpec as P

HEAD_DIM = 64
BLOCK = 64
RANDOM = 2
GLOBALS = 2
PARTS = 3 + RANDOM + GLOBALS
MASKED = -1e30
MESH = pl.DeviceIdType.MESH
VMEM = pl.BlockSpec(memory_space=pltpu.VMEM)
HBM = pl.BlockSpec(memory_space=pltpu.HBM)
SMEM = pl.BlockSpec(memory_space=pltpu.SMEM)


def params(cid):
    return pltpu.CompilerParams(
        collective_id=cid, has_side_effects=True, vmem_limit_bytes=24 * 1024 * 1024
    )


def greet(n, heads):
    s, h = lax.axis_index("seq"), lax.axis_index("head")
    barrier = pltpu.get_barrier_semaphore()
    if n > 0:

        def hello(d, c):
            pl.semaphore_signal(
                barrier, inc=1, device_id={"seq": lax.rem(s + d, n)}, device_id_type=MESH
            )
            return c

        lax.fori_loop(1, n, hello, 0)
    for d in range(1, heads):
        pl.semaphore_signal(
            barrier, inc=1, device_id={"head": lax.rem(h + d, heads)}, device_id_type=MESH
        )
    pl.semaphore_wait(barrier, max(n - 1, 0) + heads - 1)


def cols(index, width, base=0):
    return pl.ds(pl.multiple_of(base + index * width, 128), width)


def rows(index, count):
    return pl.ds(pl.multiple_of(index * count, 16), count)


def each(n, f):
    def step(d, c):
        f(d)
        return c

    lax.fori_loop(1, n, step, 0)


def remote(src, dst, send, recv, **where):
    return pltpu.make_async_remote_copy(
        src_ref=src, dst_ref=dst, send_sem=send, recv_sem=recv, device_id=where,
        device_id_type=MESH,
    )


def exchange(view, heads, send, recv, local, base):
    h = lax.axis_index("head")
    copies = []
    for d in range(1, heads):
        peer = lax.rem(h + d, heads)
        source, target = view(h, peer)
        at = base * heads + d
        copies.append(remote(source, target, send.at[at], recv.at[at], head=peer))
    source, target = view(h, h)
    return copies + [pltpu.make_async_copy(source, target, local.at[base])]


def start(copies):
    for c in copies:
        c.start()


def wait(copies):
    for c in copies:
        c.wait()


def to_heads(src, dst, tokens, width):
    return lambda a, b: (src.at[:, cols(b, width)], dst.at[rows(a, tokens), :])


def piece_in(src, dst, width, offset, size):
    nt = src.shape[0]
    return lambda a, b: (
        src.at[:, :, pl.ds(pl.multiple_of(b * width + offset, 128), size)],
        dst.at[pl.ds(a * nt, nt)],
    )


def to_tokens(src, dst, tokens, width):
    return lambda a, b: (src.at[rows(b, tokens), :], dst.at[:, cols(a, width)])


def piece_out(src, dst, tokens, width, offset, size, base):
    return lambda a, b: (
        src.at[rows(b, tokens), pl.ds(base, size)],
        dst.at[:, pl.ds(pl.multiple_of(a * width + offset, 128), size)],
    )


def kernel_in(n, heads, size, key, ids, pair, ids_all, send, recv, local, isend, irecv):
    s = lax.axis_index("seq")
    greet(n, heads)
    copies = exchange(
        piece_in(key, pair, key.shape[2] // heads, 0, size), heads, send, recv, local, 0
    )

    def idc(d):
        return remote(ids, ids_all.at[s], isend.at[d], irecv.at[d], seq=lax.rem(s + d, n))

    mine = pltpu.make_async_copy(ids, ids_all.at[s], local.at[1])
    start(copies)
    each(n, lambda d: idc(d).start())
    mine.start()
    each(n, lambda d: idc(d).wait())
    mine.wait()
    wait(copies)


def halo(n, low, high, got, send, recv, at=0):
    s = lax.axis_index("seq")
    up, down = 2 * at, 2 * at + 1
    here = pl.ds(at * low.shape[1], low.shape[1])
    return [
        remote(high, got.at[0, :, here], send.at[up], recv.at[up], seq=lax.rem(s + 1, n)),
        remote(low, got.at[1, :, here], send.at[down], recv.at[down], seq=lax.rem(s + n - 1, n)),
    ]


def far_first(n, make):
    def go(i, c):
        make(n // 2 + ((i + 1) // 2) * (2 * lax.rem(i, 2) - 1)).start()
        return c

    lax.fori_loop(0, n - 1, go, 0)


def random_piece(n, c, src_of, dst, size, send, recv):
    s = lax.axis_index("seq")

    def make(d):
        peer = lax.rem(s + d, n)
        return remote(
            src_of(peer), dst.at[s, :, pl.ds(c * size, size)], send.at[c * n + d],
            recv.at[c * n + d], seq=peer,
        )

    return make


class Shared:
    def __init__(self, n, src, here, mine, layer, done, every, sems):
        s = lax.axis_index("seq")
        gs, gr, ls, lr, fs, fr, loc = sems
        self.group = group = src.shape[0]
        self.layers = n // group
        self.me, self.level = lax.rem(s, group), s // group
        self.mine, self.layer, self.done, self.every, self.here = mine, layer, done, every, here
        self.step1 = [pltpu.make_async_copy(src.at[self.me], here.at[self.me], loc.at[0])]
        self.step3 = []
        for j in range(1, group):
            to = lax.rem(self.me + j, group)
            peer = self.level * group + to
            self.step1.append(remote(src.at[to], here.at[self.me], gs.at[j], gr.at[j], seq=peer))
            self.step3.append(remote(done, every.at[self.me], fs.at[j], fr.at[j], seq=peer))
        self.across = lambda j: remote(
            mine, layer.at[self.level], ls.at[j], lr.at[j],
            seq=lax.rem(self.level + j, self.layers) * group + self.me,
        )

    def middle(self, combine):
        wait(self.step1)
        part = combine(self.here)
        self.mine[...] = part
        self.layer[self.level] = part
        each(self.layers, lambda j: self.across(j).start())

    def finish(self, combine):
        each(self.layers, lambda j: self.across(j).wait())
        total = combine(self.layer)
        self.done[...] = total
        self.every[self.me] = total
        start(self.step3)


def kernel_fetch(n, heads, pieces, served, owners, owned_at, query, grad, key, value, first, ready,
                 qh, gh, incoming, halos, gall, *rest):
    landed, rest = (first,) + rest[: pieces - 1], rest[pieces - 1 :]
    outgoing, gsrc, ghere, gmine, glayer, gdone = rest[:6]
    send, recv, local, bs, br, hs, hr, *gsems = rest[6:]
    s = lax.axis_index("seq")
    tokens, width = query.shape[0], query.shape[1] // heads
    size = 2 * width // pieces
    nb = first.shape[0]
    half = pieces // 2
    greet(n, heads)
    moves = [[]]
    for c in range(1, pieces):
        src = key if c < half else value
        moves.append(exchange(
            piece_in(src, landed[c], width, (c % half) * size, size),
            heads, send, recv, local, c,
        ))
    blocks = [
        random_piece(n, c, (lambda p, c=c: (ready.at[p] if c == 0 else outgoing.at[c - 1, p])),
                     incoming, size, bs, br)
        for c in range(pieces)
    ]
    qmove = exchange(to_heads(query, qh, tokens, width), heads, send, recv, local, pieces)
    qmove += exchange(to_heads(grad, gh, tokens, width), heads, send, recv, local, pieces + 1)
    edges = []
    for c in range(pieces):
        edges += halo(n, landed[c].at[0], landed[c].at[nb - 1], halos, hs, hr, c)
    shared = Shared(n, gsrc, ghere, gmine, glayer, gdone, gall, gsems)
    for m in moves:
        start(m)
    far_first(n, blocks[0])
    start(qmove)
    keep = pltpu.make_async_copy(ready.at[s], incoming.at[s, :, pl.ds(0, size)],
                                 local.at[pieces + 2])
    keep.start()
    for c in range(1, pieces):
        wait(moves[c])
        at = pl.ds(c * size, size)

        def gather(i, carry):
            outgoing[c - 1, i] = landed[c][served[i]]
            return carry

        lax.fori_loop(0, n, gather, 0)
        incoming[s, :, at] = landed[c][served[s]]
        if c == pieces - 1:
            group = gsrc.shape[0]
            per = group // GLOBALS
            count = BLOCK // per
            for m in range(group):
                low = (m % per) * count
                for k in range(pieces):
                    gsrc[m, :, pl.ds(k * size, size)] = landed[k][
                        owned_at[m // per], pl.ds(low, count), :
                    ]
            start(shared.step1 + edges)
            mine = owners[shared.me * GLOBALS // group]
            shared.middle(lambda ref: ref[lax.rem(mine, group)])
        far_first(n, blocks[c])
    shared.finish(lambda ref: ref[mine // group])
    keep.wait()
    wait(edges + qmove + shared.step3)
    for c in range(pieces):
        each(n, lambda d: blocks[c](d).wait())


def kernel_return(n, heads, pieces, served, owners, owned_at, att, qg, sending, edge, gsend, wsum,
                  out, qout, kout, vout, returned, halos, gall, summed, ghere, gmine, glayer,
                  gdone, send, recv, local, bs, br, hs, hr, *gsems):
    s = lax.axis_index("seq")
    width = att.shape[1]
    tokens = att.shape[0] // heads
    nb = att.shape[0] // BLOCK
    size = 2 * width // pieces
    half = pieces // 2
    greet(n, heads)
    moves = [
        exchange(
            piece_out(summed, kout if c < half else vout, tokens, width, (c % half) * size, size,
                      c * size),
            heads, send, recv, local, c,
        )
        for c in range(pieces)
    ]
    blocks = [
        random_piece(n, c, lambda p, c=c: sending.at[p, :, pl.ds(c * size, size)], returned, size,
                     bs, br)
        for c in range(pieces)
    ]
    qmove = exchange(to_tokens(att, out, tokens, width), heads, send, recv, local, pieces)
    qmove += exchange(to_tokens(qg, qout, tokens, width), heads, send, recv, local, pieces + 1)
    edges = halo(n, edge.at[0], edge.at[1], halos, hs, hr)
    shared = Shared(n, gsend, ghere, gmine, glayer, gdone, gall, gsems)
    keep = pltpu.make_async_copy(sending.at[s], returned.at[s], local.at[pieces + 2])

    def combine(ref):
        def add(i, acc):
            return acc + ref[i].astype(jnp.float32)

        zero = jnp.zeros(ref.shape[1:], jnp.float32)
        return lax.fori_loop(0, ref.shape[0], add, zero).astype(jnp.bfloat16)

    start(shared.step1 + edges)
    far_first(n, blocks[0])
    start(qmove + [keep])
    shared.middle(combine)
    for c in range(1, pieces):
        far_first(n, blocks[c])
    shared.finish(combine)
    keep.wait()
    wait(edges + shared.step3)
    strip = 16
    per = shared.group // GLOBALS
    count = BLOCK // per

    def weight(cond):
        return jnp.where(cond, 1.0, 0.0).astype(jnp.float32)

    for c in range(pieces):
        each(n, lambda d: blocks[c](d).wait())
        at = pl.ds(c * size, size)

        def one_strip(t, carry):
            low = pl.multiple_of(t * strip, strip)
            here = pl.ds(low, strip)
            acc = [wsum[pl.ds(pl.multiple_of((j + 1) * BLOCK + low, strip), strip), at]
                   for j in range(nb)]
            acc[0] = acc[0] + halos[0, here, at].astype(jnp.float32)
            acc[-1] = acc[-1] + halos[1, here, at].astype(jnp.float32)
            for g in range(GLOBALS):
                inside = pl.ds(pl.multiple_of(lax.rem(low, count), strip), strip)
                extra = gall[g * per + low // count, inside, at].astype(jnp.float32)
                for j in range(nb):
                    hit = (owners[g] == s) & (owned_at[g] == j)
                    acc[j] = acc[j] + weight(hit) * extra

            def add(i, accs):
                x = returned[i, here, at].astype(jnp.float32)
                which = served[i]
                return tuple(accs[j] + weight(which == j) * x for j in range(nb))

            acc = lax.fori_loop(0, n, add, tuple(acc))
            for j in range(nb):
                summed[pl.ds(pl.multiple_of(j * BLOCK + low, strip), strip), at] = acc[j].astype(
                    jnp.bfloat16
                )
            return carry

        lax.fori_loop(0, BLOCK // strip, one_strip, 0)
        start(moves[c])
    wait(qmove)
    for m in moves:
        wait(m)


def dot(a, b, ca, cb):
    return lax.dot_general(a, b, (((ca,), (cb,)), ((), ())), preferred_element_type=jnp.float32)


def kernel_attend(n, lanes, pieces, slots, qh, gh, halos, incoming, gall, *rest):
    landed, rest = rest[:pieces], rest[pieces:]
    att, qg, wsum, edge, sending, gsum, pairs, keys, gacc = rest
    nb = qh.shape[0] // BLOCK
    width = qh.shape[1]
    s = lax.axis_index("seq")
    per = lanes // HEAD_DIM
    scale = jnp.asarray(HEAD_DIM ** (-0.5), jnp.bfloat16)
    pairs[pl.ds(0, BLOCK)] = halos[0]
    size = landed[0].shape[1]
    for c in range(pieces):
        pairs[pl.ds(BLOCK, nb * BLOCK), pl.ds(c * size, size)] = landed[c][...]
    pairs[pl.ds((nb + 1) * BLOCK, BLOCK)] = halos[1]
    keys[pl.ds((3 + RANDOM) * BLOCK, GLOBALS * BLOCK)] = gall[...]
    gacc[...] = jnp.zeros_like(gacc)
    wsum[...] = jnp.zeros_like(wsum)
    if n > RANDOM * nb:
        sending[...] = jnp.zeros_like(sending)
    lane_head = lax.broadcasted_iota(jnp.int32, (BLOCK, lanes), 1) // HEAD_DIM
    part = lax.broadcasted_iota(jnp.int32, (PARTS * BLOCK, 1), 0) // BLOCK

    def stack(x):
        zero = jnp.zeros_like(x)
        return jnp.concatenate([jnp.where(lane_head == j, x, zero) for j in range(per)], axis=0)

    def unstack(x):
        got = x[0:BLOCK]
        for j in range(1, per):
            got = jnp.where(lane_head == j, x[j * BLOCK : (j + 1) * BLOCK], got)
        return got

    def block(b, carry):
        here = pl.ds(pl.multiple_of(b * BLOCK, BLOCK), BLOCK)
        window = pl.ds(pl.multiple_of(b * BLOCK, BLOCK), 3 * BLOCK)
        keys[pl.ds(0, 3 * BLOCK)] = pairs[window]
        for r in range(RANDOM):
            keys[pl.ds((3 + r) * BLOCK, BLOCK)] = incoming[slots[b * RANDOM + r]]
        number = s * nb + b
        bad = ((part == 0) & (number == 0)) | ((part == 2) & (number == n * nb - 1))
        for g in range(width // lanes):
            at = pl.ds(g * lanes, lanes)
            vat = pl.ds(width + g * lanes, lanes)
            q = stack(qh[here, at]) * scale
            do = stack(gh[here, at])
            k = keys[:, at]
            v = keys[:, vat]
            scores = jnp.where(bad, MASKED, dot(k, q, 1, 1))
            raw = jnp.exp(scores - jnp.max(scores, axis=0, keepdims=True))
            probs = raw * (1.0 / jnp.sum(raw, axis=0, keepdims=True))
            half = probs.astype(jnp.bfloat16)
            pgrad = dot(v, do, 1, 1)
            delta = jnp.sum(half.astype(jnp.float32) * pgrad, axis=0, keepdims=True)
            ds = (probs * (pgrad - delta)).astype(jnp.bfloat16)
            att[here, at] = unstack(dot(half, v, 0, 0)).astype(jnp.bfloat16)
            qg[here, at] = (unstack(dot(ds, k, 0, 0)) * HEAD_DIM ** (-0.5)).astype(jnp.bfloat16)
            for x, y, to in ((ds, q, at), (half, do, vat)):
                grad = dot(x, y, 1, 0)
                wsum[window, to] += grad[: 3 * BLOCK]
                for r in range(RANDOM):
                    low = (3 + r) * BLOCK
                    sending[slots[b * RANDOM + r], :, to] = grad[low : low + BLOCK].astype(
                        jnp.bfloat16
                    )
                gacc[:, to] += grad[(3 + RANDOM) * BLOCK :]
        return carry

    lax.fori_loop(0, nb, block, 0, unroll=2)
    edge[0] = wsum[pl.ds(0, BLOCK)].astype(jnp.bfloat16)
    edge[1] = wsum[pl.ds((nb + 1) * BLOCK, BLOCK)].astype(jnp.bfloat16)
    gsum[...] = gacc[...].astype(jnp.bfloat16)


def kernel_store(a, b, c, d, wa, wb, wc, wd, sem):
    copies = [
        pltpu.make_async_copy(x, y, sem.at[i])
        for i, (x, y) in enumerate(((a, wa), (b, wb), (c, wc), (d, wd)))
    ]
    start(copies)
    wait(copies)


def body(n, heads, query_rows, key_rows, value_rows, out_grad, random_blocks, global_blocks):
    bf = jnp.bfloat16
    tokens, full = query_rows.shape
    width = full // heads
    total = tokens * heads
    nb = total // BLOCK
    me = lax.axis_index("seq")
    dma = pltpu.SemaphoreType.DMA
    sds = jax.ShapeDtypeStruct
    requests = RANDOM * nb
    flat = random_blocks.reshape(requests)
    ids = jnp.broadcast_to(jnp.pad(flat, (0, 128 - requests))[None], (8, 128))
    pieces = min(4, 2 * width // 128)
    size = 2 * width // pieces
    blocked = (tokens // BLOCK, BLOCK, full)
    key_blocks, value_blocks = key_rows.reshape(blocked), value_rows.reshape(blocked)
    query_rows, key_blocks, value_blocks, out_grad = (
        pltpu.with_memory_space_constraint(x, pltpu.HBM)
        for x in (query_rows, key_blocks, value_blocks, out_grad)
    )
    first, ids_all = pl.pallas_call(
        partial(kernel_in, n, heads, size),
        out_shape=(sds((nb, BLOCK, size), bf), sds((n, 8, 128), jnp.int32)),
        in_specs=[HBM, VMEM],
        out_specs=(VMEM,) * 2,
        scratch_shapes=[dma((heads,)), dma((heads,)), dma((2,)), dma((n,)), dma((n,))],
        compiler_params=params(0),
        name="head_in",
    )(key_blocks, ids)
    asked = ids_all[:, 0, :requests]
    served = jnp.sum(jnp.where(asked // nb == me, asked % nb, 0), axis=1).astype(jnp.int32)
    owners = global_blocks // nb
    owned_at = global_blocks % nb
    ready = jnp.take(first, served, axis=0, mode="clip")
    group = 4
    layers = n // group
    chunk = GLOBALS * BLOCK // group
    slab = sds((n, BLOCK, 2 * width), bf)
    small = sds((group, chunk, 2 * width), bf)
    wide = (chunk, 2 * width)
    scratch = [
        pltpu.VMEM(small.shape, bf), pltpu.VMEM(wide, bf), pltpu.VMEM((layers,) + wide, bf),
        pltpu.VMEM(wide, bf),
        dma(((pieces + 2) * heads,)), dma(((pieces + 2) * heads,)), dma((pieces + 3,)),
        dma((pieces * n,)), dma((pieces * n,)), dma((2 * pieces,)), dma((2 * pieces,)),
        dma((group,)), dma((group,)), dma((layers,)), dma((layers,)), dma((group,)),
        dma((group,)), dma((1,)),
    ]
    edges = sds((2, BLOCK, 2 * width), bf)
    qh, gh, incoming, halos, gall, *landed = pl.pallas_call(
        partial(kernel_fetch, n, heads, pieces),
        out_shape=(sds((total, width), bf), sds((total, width), bf), slab, edges, small)
        + (sds((nb, BLOCK, size), bf),) * (pieces - 1),
        in_specs=[SMEM] * 3 + [HBM] * 4 + [VMEM] * 2,
        out_specs=(VMEM,) * (4 + pieces),
        scratch_shapes=[pltpu.VMEM((pieces - 1, n, BLOCK, size), bf), pltpu.VMEM(small.shape, bf)]
        + scratch,
        compiler_params=params(1),
        name="fetch",
    )(served, owners, owned_at, query_rows, out_grad, key_blocks, value_blocks, first, ready)
    gwide = (GLOBALS * BLOCK, 2 * width)
    att, qg, wsum, edge, sending, gsum = pl.pallas_call(
        partial(kernel_attend, n, min(256, width), pieces),
        out_shape=(
            sds((total, width), bf), sds((total, width), bf),
            sds(((nb + 2) * BLOCK, 2 * width), jnp.float32), edges, slab, sds(gwide, bf),
        ),
        in_specs=[SMEM] + [VMEM] * (5 + pieces),
        out_specs=(VMEM,) * 6,
        scratch_shapes=[
            pltpu.VMEM(((nb + 2) * BLOCK, 2 * width), bf),
            pltpu.VMEM((PARTS * BLOCK, 2 * width), bf),
            pltpu.VMEM(gwide, jnp.float32),
        ],
        compiler_params=pltpu.CompilerParams(vmem_limit_bytes=24 * 1024 * 1024),
        name="attend",
    )(flat // nb, qh, gh, halos, incoming, gall.reshape(gwide),
      *[x.reshape(total, size) for x in (first, *landed)])
    results = pl.pallas_call(
        partial(kernel_return, n, heads, pieces),
        out_shape=(sds((tokens, full), bf),) * 4,
        in_specs=[SMEM] * 3 + [VMEM] * 6,
        out_specs=(VMEM,) * 4,
        scratch_shapes=[
            pltpu.VMEM(slab.shape, bf), pltpu.VMEM(edges.shape, bf), pltpu.VMEM(small.shape, bf),
            pltpu.VMEM((total, 2 * width), bf),
        ] + scratch,
        compiler_params=params(2),
        name="give_back",
    )(served, owners, owned_at, att, qg, sending, edge, gsum.reshape(group, chunk, 2 * width),
      wsum)
    return pl.pallas_call(
        kernel_store,
        out_shape=(sds((tokens, full), bf),) * 4,
        in_specs=[VMEM] * 4,
        out_specs=(HBM,) * 4,
        scratch_shapes=[dma((4,))],
        compiler_params=pltpu.CompilerParams(vmem_limit_bytes=16 * 1024 * 1024),
        name="store",
    )(*results)


LANES = 128
WIDE = 2 * LANES


class Team:
    def __init__(self, n, heads, groups, tokens):
        self.n, self.heads, self.groups, self.tokens = n, heads, groups, tokens
        self.members = n // groups
        s, self.h = lax.axis_index("seq"), lax.axis_index("head")
        self.g, self.m = s // self.members, lax.rem(s, self.members)
        self.bits = [1 << i for i in reversed(range(self.members.bit_length() - 1))]
        self.places = [(i, d) for i in range(groups) for d in range(heads)]
        self.me = self.slot(self.g, self.h)

    def slot(self, g, h):
        return g * self.heads + h

    def near(self, i):
        total = self.g * 0
        for g in range(self.groups):
            order = sorted(range(self.groups), key=lambda k: (k != g, -abs(k - g), k))
            total = total + jnp.where(self.g == g, order[i], 0)
        return total

    def place(self, j):
        if isinstance(j, int):
            i, d = self.places[j]
            return (self.near(i) if i else self.g), lax.rem(self.h + d, self.heads)
        g = self.g * 0
        for i in range(self.groups):
            g = g + jnp.where(j // self.heads == i, self.near(i), 0)
        return g, lax.rem(self.h + lax.rem(j, self.heads), self.heads)

    def device(self, g, h):
        return {"seq": g * self.members + self.m, "head": h}

    def mate(self, bit):
        return self.m ^ bit

    def mate_device(self, bit):
        return {"seq": self.g * self.members + self.mate(bit)}

    def chunk(self, g, h, m):
        return rows((g * self.members + m) * self.heads + h, self.tokens)

    def columns(self, g, h):
        return pl.ds(pl.multiple_of((h * self.groups + g) * LANES, LANES), LANES)

    def greet(self):
        barrier = pltpu.get_barrier_semaphore()
        for j in range(1, len(self.places)):
            pl.semaphore_signal(
                barrier, inc=1, device_id=self.device(*self.place(j)), device_id_type=MESH
            )
        for bit in self.bits:
            pl.semaphore_signal(
                barrier, inc=1, device_id=self.mate_device(bit), device_id_type=MESH
            )
        pl.semaphore_wait(barrier, len(self.places) - 1 + len(self.bits))


def send_to(src, dst, send, recv, device):
    return pltpu.make_async_remote_copy(
        src_ref=src, dst_ref=dst, send_sem=send, recv_sem=recv, device_id=device,
        device_id_type=MESH,
    )


def kernel_all(n, heads, groups, named_in, owners_in, key, value, query, grad, out, qout, kout, vout,
               kv, qd, od, acc, extra, keys, ids, ids_all, table, named, owners, part, inbox, sums, final, send, recv,
               local, fsend, frecv, isend, irecv, bsend, brecv, blocal, tsend, trecv):
    tokens = query.shape[0]
    t = Team(n, heads, groups, tokens)
    count = len(t.places)
    per_chunk = tokens // BLOCK
    run = heads * per_chunk
    requests = RANDOM * run
    blank = groups * requests + GLOBALS
    asks = [pltpu.make_async_copy(named_in, named, local.at[6]),
            pltpu.make_async_copy(owners_in, owners, local.at[7])]
    start(asks)
    t.greet()
    arrays = (key, value, query, grad)
    dests = (out, qout, kout, vout)

    def lanes(a):
        return pl.ds((a % 2) * LANES, LANES)

    def blocks_of(g, h, m):
        return pl.ds(((g * t.members + m) * heads + h) * per_chunk + 1, per_chunk)

    def leaving(a, g, h):
        ref = arrays[a]
        return ref.at[:, :, t.columns(g, h)] if a < 2 else ref.at[:, t.columns(g, h)]

    def landing(a, g, h):
        return (kv.at[blocks_of(g, h, t.m), :, lanes(a)] if a < 2
                else qd.at[rows(t.slot(g, h), tokens), lanes(a)])

    def move(a, j):
        g, h = t.place(j)
        return send_to(leaving(a, g, h), landing(a, t.g, t.h),
                       send.at[a * count + j], recv.at[a * count + t.me], t.device(g, h))

    def keep(a):
        return pltpu.make_async_copy(leaving(a, t.g, t.h), landing(a, t.g, t.h),
                                     local.at[a])

    def arrived(a, j):
        g, h = t.place(j)
        return send_to(leaving(a, g, h), landing(a, g, h),
                       send.at[a * count + j], recv.at[a * count + t.slot(g, h)],
                       t.device(g, h))

    idm = [send_to(ids, ids_all.at[t.g], isend.at[i], irecv.at[t.g], t.device(t.near(i), t.h))
           for i in range(1, groups)]
    idr = [send_to(ids, ids_all.at[t.near(i)], isend.at[i], irecv.at[t.near(i)],
                   t.device(t.near(i), t.h)) for i in range(1, groups)]
    for a in (0, 1):
        keep(a).start()
    for j in range(1, count):
        for a in (0, 1):
            move(a, j).start()
    wait(asks)
    lane = lax.broadcasted_iota(jnp.int32, ids.shape, 1)
    row = lax.broadcasted_iota(jnp.int32, ids.shape, 0)
    entry = jnp.where(row == 0, 0, blank)
    for r in range(requests):
        name = named[r % RANDOM, r // RANDOM]
        entry = jnp.where((row == 0) & (lane == r), name, entry)
        entry = jnp.where((row == 1) & (lane == name), t.g * requests + r, entry)
    for k in range(GLOBALS):
        entry = jnp.where((row == 2 + k) & (lane == owners[k]), groups * requests + k, entry)
    ids[...] = entry
    edge = jnp.zeros(kv.shape[1:], kv.dtype)
    kv[0] = edge
    kv[kv.shape[0] - 1] = edge
    empty = jnp.zeros((BLOCK, WIDE), jnp.float32)
    for k in range(GLOBALS + 1):
        extra[groups * requests + k] = empty

    def clear(i, carry):
        acc[rows(i, BLOCK)] = empty
        return carry

    lax.fori_loop(0, acc.shape[0] // BLOCK, clear, 0)
    start(idm)
    for a in (2, 3):
        keep(a).start()
    for j in range(1, count):
        for a in (2, 3):
            move(a, j).start()
    own = pltpu.make_async_copy(ids, ids_all.at[t.g], local.at[4])
    own.start()

    def forward(stage, mask, p, mine):
        bit = t.bits[stage]
        g, h = t.place(p // 2)
        owner = t.m ^ mask if mine else t.m ^ bit ^ mask
        ref = kv.at[blocks_of(g, h, owner), :, lanes(p)]
        at = (stage * t.members + mask) * 2 * count + p
        return send_to(ref, ref, fsend.at[at], frecv.at[at], t.mate_device(bit))

    def masks(stage):
        got = [0]
        for bit in t.bits[:stage]:
            got += [x ^ bit for x in got]
        return got

    stages = range(len(t.bits))
    pieces = 2 * count
    for step in range(pieces + 4 * len(t.bits)):
        for stage in reversed(stages):
            p = step - 4 * (stage + 1)
            if 0 <= p < pieces:
                for mask in masks(stage):
                    forward(stage, mask, p, False).wait_recv()
                    for later in range(stage + 1, len(t.bits)):
                        forward(later, mask ^ t.bits[stage], p, True).start()
        if step < pieces:
            if step < 2:
                keep(step).wait()
            else:
                arrived(step % 2, step // 2).wait_recv()
            for stage in stages:
                forward(stage, 0, step, True).start()
    own.wait()
    for c in idr:
        c.wait_recv()
    fill = pltpu.make_async_copy(ids_all, table, local.at[5])
    fill.start()
    fill.wait()

    per = LANES // HEAD_DIM
    scale = jnp.asarray(HEAD_DIM ** (-0.5), jnp.bfloat16)
    for k in range(GLOBALS):
        keys[3 + RANDOM + k] = kv[owners[k] + 1]
    lane_head = lax.broadcasted_iota(jnp.int32, (BLOCK, LANES), 1) // HEAD_DIM
    where = lax.broadcasted_iota(jnp.int32, (PARTS * BLOCK, 1), 0) // BLOCK
    at, vat = lanes(0), lanes(1)

    def stack(x):
        zero = jnp.zeros_like(x)
        return jnp.concatenate([jnp.where(lane_head == j, x, zero) for j in range(per)], axis=0)

    def unstack(x):
        got = x[0:BLOCK]
        for j in range(1, per):
            got = jnp.where(lane_head == j, x[j * BLOCK : (j + 1) * BLOCK], got)
        return got

    def chunk(j):
        g, h = t.place(j)
        slot = t.slot(g, h)
        first = ((g * t.members + t.m) * heads + h) * per_chunk

        def block(b, carry):
            here = rows(slot * per_chunk + b, BLOCK)
            number = first + b
            window = pl.ds(pl.multiple_of(number * BLOCK, BLOCK), 3 * BLOCK)
            keys[pl.ds(0, 3)] = kv[pl.ds(number, 3)]
            spot = (h * per_chunk + b) * RANDOM
            for r in range(RANDOM):
                keys[3 + r] = kv[table[g, 0, spot + r] + 1]
            bad = ((where == 0) & (number == 0)) | ((where == 2) & (number == n * run - 1))
            q = stack(qd[here, at]) * scale
            do = stack(qd[here, vat])
            k = keys[:, :, at].reshape(PARTS * BLOCK, LANES)
            v = keys[:, :, vat].reshape(PARTS * BLOCK, LANES)
            scores = jnp.where(bad, MASKED, dot(k, q, 1, 1))
            raw = jnp.exp(scores - jnp.max(scores, axis=0, keepdims=True))
            probs = raw * (1.0 / jnp.sum(raw, axis=0, keepdims=True))
            half = probs.astype(jnp.bfloat16)
            pgrad = dot(v, do, 1, 1)
            delta = jnp.sum(half.astype(jnp.float32) * pgrad, axis=0, keepdims=True)
            ds = (probs * (pgrad - delta)).astype(jnp.bfloat16)
            od[here, at] = unstack(dot(half, v, 0, 0)).astype(jnp.bfloat16)
            od[here, vat] = (unstack(dot(ds, k, 0, 0)) * HEAD_DIM ** (-0.5)).astype(jnp.bfloat16)
            for x, y, to in ((ds, q, at), (half, do, vat)):
                got = dot(x, y, 1, 0)
                acc[window, to] += got[: 3 * BLOCK]
                for r in range(RANDOM):
                    low = (3 + r) * BLOCK
                    extra[g * requests + spot + r, :, to] = got[low : low + BLOCK]
                for k2 in range(GLOBALS):
                    low = (3 + RANDOM + k2) * BLOCK
                    extra[groups * requests + k2, :, to] += got[low : low + BLOCK]
            return carry

        lax.fori_loop(0, per_chunk, block, 0, unroll=2)

    mine = t.columns(t.g, t.h)

    def source(a, j):
        g, h = t.place(j)
        return (od.at[rows(t.slot(g, h), tokens), lanes(a)] if a < 2
                else final.at[rows(j, tokens), lanes(a)])

    def back(a, j):
        g, h = t.place(j)
        return send_to(source(a, j), dests[a].at[:, mine], bsend.at[a * count + j],
                       brecv.at[a * count + t.me], t.device(g, h))

    def back_keep(a):
        return pltpu.make_async_copy(source(a, 0), dests[a].at[:, mine], blocal.at[a])

    def returned(a, j):
        g, h = t.place(j)
        return send_to(source(a, j), dests[a].at[:, t.columns(g, h)], bsend.at[a * count + j],
                       brecv.at[a * count + t.slot(g, h)], t.device(g, h))

    for a in (2, 3):
        keep(a).wait()
    chunk(0)
    for a in (0, 1):
        back_keep(a).start()

    def one(j, carry):
        for a in (2, 3):
            arrived(a, j).wait_recv()
        chunk(j)
        for a in (0, 1):
            back(a, j).start()
        return carry

    lax.fori_loop(1, count, one, 0)

    order = list(reversed(t.bits))
    handed = []
    held = list(range(t.members))
    for bit in order:
        handed.append([x for x in held if x & bit])
        held = [x for x in held if not x & bit]
    boxes = [(stage, mask) for stage in range(len(order)) for mask in handed[stage]]

    def box(stage, mask, j):
        return rows(boxes.index((stage, mask)) * count + j, tokens)

    def trade(stage, mask, j):
        at = (stage * t.members + mask) * count + j
        if stage == 0:
            src = part.at[rows(handed[0].index(mask) * count + j, tokens)]
        else:
            src = sums.at[rows((stage - 1) * count + j, tokens)]
        return send_to(src, inbox.at[box(stage, mask, j)], tsend.at[at], trecv.at[at],
                       t.mate_device(order[stage]))

    def total(ref, base, mask, j, upto):
        g, h = t.place(j)
        lows = [(boxes.index((stage, mask ^ order[stage])) * count + j) * per_chunk
                for stage in range(upto)]
        first = ((g * t.members + (t.m ^ mask)) * heads + h) * per_chunk

        def strip(b, carry):
            x = acc[rows(first + b + 1, BLOCK)]
            for q in range(groups):
                x = x + extra[table[q, 1, first + b]]
            for k in range(GLOBALS):
                x = x + extra[table[0, 2 + k, first + b]]
            for low in lows:
                x = x + inbox[rows(low + b, BLOCK)].astype(jnp.float32)
            ref[rows(base * per_chunk + b, BLOCK)] = x.astype(jnp.bfloat16)
            return carry

        lax.fori_loop(0, per_chunk, strip, 0)

    js = list(range(1, count)) + [0]
    for j in js:
        for mask in reversed(handed[0]):
            total(part, handed[0].index(mask) * count + j, mask, j, 0)
            trade(0, mask, j).start()
    for stage in range(1, len(order)):
        for j in js:
            for mask in handed[stage]:
                for before in range(stage):
                    trade(before, mask ^ order[before], j).wait_recv()
                total(sums, (stage - 1) * count + j, mask, j, stage)
                trade(stage, mask, j).start()
    for j in js:
        for stage in range(len(order)):
            trade(stage, order[stage], j).wait_recv()
        total(final, j, 0, j, len(order))
        for a in (2, 3):
            (back(a, j) if j else back_keep(a)).start()
    for stage in stages:
        for mask in masks(stage):
            for p in range(2 * count):
                forward(stage, mask, p, True).wait_send()
        for mask in handed[stage]:
            for j in js:
                trade(stage, mask, j).wait_send()
    for c in idm:
        c.wait_send()
    for a in range(4):
        back_keep(a).wait()
        for j in range(1, count):
            move(a, j).wait_send()
            back(a, j).wait_send()
            returned(a, j).wait_recv()


def grouped(n, heads, groups, query_rows, key_rows, value_rows, out_grad, random_blocks,
            global_blocks):
    bf = jnp.bfloat16
    tokens, full = query_rows.shape
    members = n // groups
    count = groups * heads
    everything = n * heads * tokens
    held = count * tokens
    bits = members.bit_length() - 1
    run = heads * tokens // BLOCK
    requests = RANDOM * run
    dma = pltpu.SemaphoreType.DMA
    sds = jax.ShapeDtypeStruct
    total = n * run
    span = -(-max(total, requests) // 128) * 128
    picked = pltpu.with_memory_space_constraint(random_blocks.T, pltpu.HBM)
    shared = pltpu.with_memory_space_constraint(global_blocks, pltpu.HBM)
    blocked = (tokens // BLOCK, BLOCK, full)
    key_rows, value_rows = key_rows.reshape(blocked), value_rows.reshape(blocked)
    query_rows, key_rows, value_rows, out_grad = (
        pltpu.with_memory_space_constraint(x, pltpu.HBM)
        for x in (query_rows, key_rows, value_rows, out_grad)
    )
    f32 = jnp.float32
    results = pl.pallas_call(
        partial(kernel_all, n, heads, groups),
        out_shape=(sds((tokens, full), bf),) * 4,
        in_specs=[HBM] * 6,
        out_specs=(VMEM,) * 4,
        scratch_shapes=[
            pltpu.VMEM((total + 2, BLOCK, WIDE), bf), pltpu.VMEM((held, WIDE), bf),
            pltpu.VMEM((held, WIDE), bf), pltpu.VMEM((everything + 2 * BLOCK, WIDE), f32),
            pltpu.VMEM((groups * requests + GLOBALS + 1, BLOCK, WIDE), f32),
            pltpu.VMEM((PARTS, BLOCK, WIDE), bf), pltpu.VMEM((8, span), jnp.int32),
            pltpu.VMEM((groups, 8, span), jnp.int32),
            pltpu.SMEM((groups, 8, span), jnp.int32),
            pltpu.SMEM((RANDOM, run), jnp.int32), pltpu.SMEM((GLOBALS,), jnp.int32),
            pltpu.VMEM((members // 2 * held, WIDE), bf),
            pltpu.VMEM(((members - 1) * held, WIDE), bf),
            pltpu.VMEM((max(bits - 1, 1) * held, WIDE), bf), pltpu.VMEM((held, WIDE), bf),
            dma((4 * count,)), dma((4 * count,)), dma((8,)),
            dma((2 * bits * members * count,)), dma((2 * bits * members * count,)),
            dma((groups,)), dma((groups,)),
            dma((4 * count,)), dma((4 * count,)), dma((4,)),
            dma((bits * members * count,)), dma((bits * members * count,)),
        ],
        compiler_params=pltpu.CompilerParams(
            collective_id=0, has_side_effects=True, vmem_limit_bytes=44 * 1024 * 1024
        ),
        name="everything",
    )(picked, shared, key_rows, value_rows, query_rows, out_grad)
    return pl.pallas_call(
        kernel_store,
        out_shape=(sds((tokens, full), bf),) * 4,
        in_specs=[VMEM] * 4,
        out_specs=(HBM,) * 4,
        scratch_shapes=[dma((4,))],
        compiler_params=pltpu.CompilerParams(vmem_limit_bytes=16 * 1024 * 1024),
        name="store",
    )(*results)


def chosen(n, heads, query_rows, *others):
    tokens, full = query_rows.shape
    groups = full // LANES // heads
    fits = n * heads * tokens * WIDE * 6 <= 24 * 1024 * 1024
    if full % (LANES * heads) == 0 and n % groups == 0 and fits and n // groups in (2, 4):
        return grouped(n, heads, groups, query_rows, *others)
    return body(n, heads, query_rows, *others)


def solution(mesh):
    rows_spec = P(("seq", "head"), None)
    return jax.shard_map(
        partial(chosen, mesh.shape["seq"], mesh.shape["head"]),
        mesh=mesh,
        in_specs=(rows_spec,) * 4 + (P("seq", None), P()),
        out_specs=(rows_spec,) * 4,
        check_vma=False,
    )
```

```python
from functools import partial

import jax
import jax.numpy as jnp
from jax import lax
from jax.experimental import pallas as pl
from jax.experimental.pallas import tpu as pltpu
from jax.sharding import PartitionSpec as P

HEAD_DIM = 64
BLOCK = 64
RANDOM = 2
GLOBALS = 2
PARTS = 3 + RANDOM + GLOBALS
MASKED = -1e30
MESH = pl.DeviceIdType.MESH
VMEM = pl.BlockSpec(memory_space=pltpu.VMEM)
HBM = pl.BlockSpec(memory_space=pltpu.HBM)
SMEM = pl.BlockSpec(memory_space=pltpu.SMEM)


def params(cid):
    return pltpu.CompilerParams(
        collective_id=cid, has_side_effects=True, vmem_limit_bytes=24 * 1024 * 1024
    )


def greet(n, heads):
    s, h = lax.axis_index("seq"), lax.axis_index("head")
    barrier = pltpu.get_barrier_semaphore()
    if n > 0:

        def hello(d, c):
            pl.semaphore_signal(
                barrier, inc=1, device_id={"seq": lax.rem(s + d, n)}, device_id_type=MESH
            )
            return c

        lax.fori_loop(1, n, hello, 0)
    for d in range(1, heads):
        pl.semaphore_signal(
            barrier, inc=1, device_id={"head": lax.rem(h + d, heads)}, device_id_type=MESH
        )
    pl.semaphore_wait(barrier, max(n - 1, 0) + heads - 1)


def cols(index, width, base=0):
    return pl.ds(pl.multiple_of(base + index * width, 128), width)


def rows(index, count):
    return pl.ds(pl.multiple_of(index * count, 16), count)


def each(n, f):
    def step(d, c):
        f(d)
        return c

    lax.fori_loop(1, n, step, 0)


def remote(src, dst, send, recv, **where):
    return pltpu.make_async_remote_copy(
        src_ref=src, dst_ref=dst, send_sem=send, recv_sem=recv, device_id=where,
        device_id_type=MESH,
    )


def exchange(view, heads, send, recv, local, base):
    h = lax.axis_index("head")
    copies = []
    for d in range(1, heads):
        peer = lax.rem(h + d, heads)
        source, target = view(h, peer)
        at = base * heads + d
        copies.append(remote(source, target, send.at[at], recv.at[at], head=peer))
    source, target = view(h, h)
    return copies + [pltpu.make_async_copy(source, target, local.at[base])]


def start(copies):
    for c in copies:
        c.start()


def wait(copies):
    for c in copies:
        c.wait()


def to_heads(src, dst, tokens, width):
    return lambda a, b: (src.at[:, cols(b, width)], dst.at[rows(a, tokens), :])


def piece_in(src, dst, width, offset, size):
    nt = src.shape[0]
    return lambda a, b: (
        src.at[:, :, pl.ds(pl.multiple_of(b * width + offset, 128), size)],
        dst.at[pl.ds(a * nt, nt)],
    )


def to_tokens(src, dst, tokens, width):
    return lambda a, b: (src.at[rows(b, tokens), :], dst.at[:, cols(a, width)])


def piece_out(src, dst, tokens, width, offset, size, base):
    return lambda a, b: (
        src.at[rows(b, tokens), pl.ds(base, size)],
        dst.at[:, pl.ds(pl.multiple_of(a * width + offset, 128), size)],
    )


def kernel_in(n, heads, size, key, ids, pair, ids_all, send, recv, local, isend, irecv):
    s = lax.axis_index("seq")
    greet(n, heads)
    copies = exchange(
        piece_in(key, pair, key.shape[2] // heads, 0, size), heads, send, recv, local, 0
    )

    def idc(d):
        return remote(ids, ids_all.at[s], isend.at[d], irecv.at[d], seq=lax.rem(s + d, n))

    mine = pltpu.make_async_copy(ids, ids_all.at[s], local.at[1])
    start(copies)
    each(n, lambda d: idc(d).start())
    mine.start()
    each(n, lambda d: idc(d).wait())
    mine.wait()
    wait(copies)


def halo(n, low, high, got, send, recv, at=0):
    s = lax.axis_index("seq")
    up, down = 2 * at, 2 * at + 1
    here = pl.ds(at * low.shape[1], low.shape[1])
    return [
        remote(high, got.at[0, :, here], send.at[up], recv.at[up], seq=lax.rem(s + 1, n)),
        remote(low, got.at[1, :, here], send.at[down], recv.at[down], seq=lax.rem(s + n - 1, n)),
    ]


def far_first(n, make):
    def go(i, c):
        make(n // 2 + ((i + 1) // 2) * (2 * lax.rem(i, 2) - 1)).start()
        return c

    lax.fori_loop(0, n - 1, go, 0)


def random_piece(n, c, src_of, dst, size, send, recv):
    s = lax.axis_index("seq")

    def make(d):
        peer = lax.rem(s + d, n)
        return remote(
            src_of(peer), dst.at[s, :, pl.ds(c * size, size)], send.at[c * n + d],
            recv.at[c * n + d], seq=peer,
        )

    return make


class Shared:
    def __init__(self, n, src, here, mine, layer, done, every, sems):
        s = lax.axis_index("seq")
        gs, gr, ls, lr, fs, fr, loc = sems
        self.group = group = src.shape[0]
        self.layers = n // group
        self.me, self.level = lax.rem(s, group), s // group
        self.mine, self.layer, self.done, self.every, self.here = mine, layer, done, every, here
        self.step1 = [pltpu.make_async_copy(src.at[self.me], here.at[self.me], loc.at[0])]
        self.step3 = []
        for j in range(1, group):
            to = lax.rem(self.me + j, group)
            peer = self.level * group + to
            self.step1.append(remote(src.at[to], here.at[self.me], gs.at[j], gr.at[j], seq=peer))
            self.step3.append(remote(done, every.at[self.me], fs.at[j], fr.at[j], seq=peer))
        self.across = lambda j: remote(
            mine, layer.at[self.level], ls.at[j], lr.at[j],
            seq=lax.rem(self.level + j, self.layers) * group + self.me,
        )

    def middle(self, combine):
        wait(self.step1)
        part = combine(self.here)
        self.mine[...] = part
        self.layer[self.level] = part
        each(self.layers, lambda j: self.across(j).start())

    def finish(self, combine):
        each(self.layers, lambda j: self.across(j).wait())
        total = combine(self.layer)
        self.done[...] = total
        self.every[self.me] = total
        start(self.step3)


def kernel_fetch(n, heads, pieces, served, owners, owned_at, query, grad, key, value, first, ready,
                 qh, gh, incoming, halos, gall, *rest):
    landed, rest = (first,) + rest[: pieces - 1], rest[pieces - 1 :]
    outgoing, gsrc, ghere, gmine, glayer, gdone = rest[:6]
    send, recv, local, bs, br, hs, hr, *gsems = rest[6:]
    s = lax.axis_index("seq")
    tokens, width = query.shape[0], query.shape[1] // heads
    size = 2 * width // pieces
    nb = first.shape[0]
    half = pieces // 2
    greet(n, heads)
    moves = [[]]
    for c in range(1, pieces):
        src = key if c < half else value
        moves.append(exchange(
            piece_in(src, landed[c], width, (c % half) * size, size),
            heads, send, recv, local, c,
        ))
    blocks = [
        random_piece(n, c, (lambda p, c=c: (ready.at[p] if c == 0 else outgoing.at[c - 1, p])),
                     incoming, size, bs, br)
        for c in range(pieces)
    ]
    qmove = exchange(to_heads(query, qh, tokens, width), heads, send, recv, local, pieces)
    qmove += exchange(to_heads(grad, gh, tokens, width), heads, send, recv, local, pieces + 1)
    edges = []
    for c in range(pieces):
        edges += halo(n, landed[c].at[0], landed[c].at[nb - 1], halos, hs, hr, c)
    shared = Shared(n, gsrc, ghere, gmine, glayer, gdone, gall, gsems)
    for m in moves:
        start(m)
    far_first(n, blocks[0])
    start(qmove)
    keep = pltpu.make_async_copy(ready.at[s], incoming.at[s, :, pl.ds(0, size)],
                                 local.at[pieces + 2])
    keep.start()
    for c in range(1, pieces):
        wait(moves[c])
        at = pl.ds(c * size, size)

        def gather(i, carry):
            outgoing[c - 1, i] = landed[c][served[i]]
            return carry

        lax.fori_loop(0, n, gather, 0)
        incoming[s, :, at] = landed[c][served[s]]
        if c == pieces - 1:
            group = gsrc.shape[0]
            per = group // GLOBALS
            count = BLOCK // per
            for m in range(group):
                low = (m % per) * count
                for k in range(pieces):
                    gsrc[m, :, pl.ds(k * size, size)] = landed[k][
                        owned_at[m // per], pl.ds(low, count), :
                    ]
            start(shared.step1 + edges)
            mine = owners[shared.me * GLOBALS // group]
            shared.middle(lambda ref: ref[lax.rem(mine, group)])
        far_first(n, blocks[c])
    shared.finish(lambda ref: ref[mine // group])
    keep.wait()
    wait(edges + qmove + shared.step3)
    for c in range(pieces):
        each(n, lambda d: blocks[c](d).wait())


def kernel_return(n, heads, pieces, served, owners, owned_at, att, qg, sending, edge, gsend, wsum,
                  out, qout, kout, vout, returned, halos, gall, summed, ghere, gmine, glayer,
                  gdone, send, recv, local, bs, br, hs, hr, *gsems):
    s = lax.axis_index("seq")
    width = att.shape[1]
    tokens = att.shape[0] // heads
    nb = att.shape[0] // BLOCK
    size = 2 * width // pieces
    half = pieces // 2
    greet(n, heads)
    moves = [
        exchange(
            piece_out(summed, kout if c < half else vout, tokens, width, (c % half) * size, size,
                      c * size),
            heads, send, recv, local, c,
        )
        for c in range(pieces)
    ]
    blocks = [
        random_piece(n, c, lambda p, c=c: sending.at[p, :, pl.ds(c * size, size)], returned, size,
                     bs, br)
        for c in range(pieces)
    ]
    qmove = exchange(to_tokens(att, out, tokens, width), heads, send, recv, local, pieces)
    qmove += exchange(to_tokens(qg, qout, tokens, width), heads, send, recv, local, pieces + 1)
    edges = halo(n, edge.at[0], edge.at[1], halos, hs, hr)
    shared = Shared(n, gsend, ghere, gmine, glayer, gdone, gall, gsems)
    keep = pltpu.make_async_copy(sending.at[s], returned.at[s], local.at[pieces + 2])

    def combine(ref):
        def add(i, acc):
            return acc + ref[i].astype(jnp.float32)

        zero = jnp.zeros(ref.shape[1:], jnp.float32)
        return lax.fori_loop(0, ref.shape[0], add, zero).astype(jnp.bfloat16)

    start(shared.step1 + edges)
    far_first(n, blocks[0])
    start(qmove + [keep])
    shared.middle(combine)
    for c in range(1, pieces):
        far_first(n, blocks[c])
    shared.finish(combine)
    keep.wait()
    wait(edges + shared.step3)
    strip = 16
    per = shared.group // GLOBALS
    count = BLOCK // per

    def weight(cond):
        return jnp.where(cond, 1.0, 0.0).astype(jnp.float32)

    for c in range(pieces):
        each(n, lambda d: blocks[c](d).wait())
        at = pl.ds(c * size, size)

        def one_strip(t, carry):
            low = pl.multiple_of(t * strip, strip)
            here = pl.ds(low, strip)
            acc = [wsum[pl.ds(pl.multiple_of((j + 1) * BLOCK + low, strip), strip), at]
                   for j in range(nb)]
            acc[0] = acc[0] + halos[0, here, at].astype(jnp.float32)
            acc[-1] = acc[-1] + halos[1, here, at].astype(jnp.float32)
            for g in range(GLOBALS):
                inside = pl.ds(pl.multiple_of(lax.rem(low, count), strip), strip)
                extra = gall[g * per + low // count, inside, at].astype(jnp.float32)
                for j in range(nb):
                    hit = (owners[g] == s) & (owned_at[g] == j)
                    acc[j] = acc[j] + weight(hit) * extra

            def add(i, accs):
                x = returned[i, here, at].astype(jnp.float32)
                which = served[i]
                return tuple(accs[j] + weight(which == j) * x for j in range(nb))

            acc = lax.fori_loop(0, n, add, tuple(acc))
            for j in range(nb):
                summed[pl.ds(pl.multiple_of(j * BLOCK + low, strip), strip), at] = acc[j].astype(
                    jnp.bfloat16
                )
            return carry

        lax.fori_loop(0, BLOCK // strip, one_strip, 0)
        start(moves[c])
    wait(qmove)
    for m in moves:
        wait(m)


def dot(a, b, ca, cb):
    return lax.dot_general(a, b, (((ca,), (cb,)), ((), ())), preferred_element_type=jnp.float32)


def kernel_attend(n, lanes, pieces, slots, qh, gh, halos, incoming, gall, *rest):
    landed, rest = rest[:pieces], rest[pieces:]
    att, qg, wsum, edge, sending, gsum, pairs, keys, gacc = rest
    nb = qh.shape[0] // BLOCK
    width = qh.shape[1]
    s = lax.axis_index("seq")
    per = lanes // HEAD_DIM
    scale = jnp.asarray(HEAD_DIM ** (-0.5), jnp.bfloat16)
    pairs[pl.ds(0, BLOCK)] = halos[0]
    size = landed[0].shape[1]
    for c in range(pieces):
        pairs[pl.ds(BLOCK, nb * BLOCK), pl.ds(c * size, size)] = landed[c][...]
    pairs[pl.ds((nb + 1) * BLOCK, BLOCK)] = halos[1]
    keys[pl.ds((3 + RANDOM) * BLOCK, GLOBALS * BLOCK)] = gall[...]
    gacc[...] = jnp.zeros_like(gacc)
    wsum[...] = jnp.zeros_like(wsum)
    if n > RANDOM * nb:
        sending[...] = jnp.zeros_like(sending)
    lane_head = lax.broadcasted_iota(jnp.int32, (BLOCK, lanes), 1) // HEAD_DIM
    part = lax.broadcasted_iota(jnp.int32, (PARTS * BLOCK, 1), 0) // BLOCK

    def stack(x):
        zero = jnp.zeros_like(x)
        return jnp.concatenate([jnp.where(lane_head == j, x, zero) for j in range(per)], axis=0)

    def unstack(x):
        got = x[0:BLOCK]
        for j in range(1, per):
            got = jnp.where(lane_head == j, x[j * BLOCK : (j + 1) * BLOCK], got)
        return got

    def block(b, carry):
        here = pl.ds(pl.multiple_of(b * BLOCK, BLOCK), BLOCK)
        window = pl.ds(pl.multiple_of(b * BLOCK, BLOCK), 3 * BLOCK)
        keys[pl.ds(0, 3 * BLOCK)] = pairs[window]
        for r in range(RANDOM):
            keys[pl.ds((3 + r) * BLOCK, BLOCK)] = incoming[slots[b * RANDOM + r]]
        number = s * nb + b
        bad = ((part == 0) & (number == 0)) | ((part == 2) & (number == n * nb - 1))
        for g in range(width // lanes):
            at = pl.ds(g * lanes, lanes)
            vat = pl.ds(width + g * lanes, lanes)
            q = stack(qh[here, at]) * scale
            do = stack(gh[here, at])
            k = keys[:, at]
            v = keys[:, vat]
            scores = jnp.where(bad, MASKED, dot(k, q, 1, 1))
            raw = jnp.exp(scores - jnp.max(scores, axis=0, keepdims=True))
            probs = raw * (1.0 / jnp.sum(raw, axis=0, keepdims=True))
            half = probs.astype(jnp.bfloat16)
            pgrad = dot(v, do, 1, 1)
            delta = jnp.sum(half.astype(jnp.float32) * pgrad, axis=0, keepdims=True)
            ds = (probs * (pgrad - delta)).astype(jnp.bfloat16)
            att[here, at] = unstack(dot(half, v, 0, 0)).astype(jnp.bfloat16)
            qg[here, at] = (unstack(dot(ds, k, 0, 0)) * HEAD_DIM ** (-0.5)).astype(jnp.bfloat16)
            for x, y, to in ((ds, q, at), (half, do, vat)):
                grad = dot(x, y, 1, 0)
                wsum[window, to] += grad[: 3 * BLOCK]
                for r in range(RANDOM):
                    low = (3 + r) * BLOCK
                    sending[slots[b * RANDOM + r], :, to] = grad[low : low + BLOCK].astype(
                        jnp.bfloat16
                    )
                gacc[:, to] += grad[(3 + RANDOM) * BLOCK :]
        return carry

    lax.fori_loop(0, nb, block, 0, unroll=2)
    edge[0] = wsum[pl.ds(0, BLOCK)].astype(jnp.bfloat16)
    edge[1] = wsum[pl.ds((nb + 1) * BLOCK, BLOCK)].astype(jnp.bfloat16)
    gsum[...] = gacc[...].astype(jnp.bfloat16)


def kernel_store(a, b, c, d, wa, wb, wc, wd, sem):
    copies = [
        pltpu.make_async_copy(x, y, sem.at[i])
        for i, (x, y) in enumerate(((a, wa), (b, wb), (c, wc), (d, wd)))
    ]
    start(copies)
    wait(copies)


def body(n, heads, query_rows, key_rows, value_rows, out_grad, random_blocks, global_blocks):
    bf = jnp.bfloat16
    tokens, full = query_rows.shape
    width = full // heads
    total = tokens * heads
    nb = total // BLOCK
    me = lax.axis_index("seq")
    dma = pltpu.SemaphoreType.DMA
    sds = jax.ShapeDtypeStruct
    requests = RANDOM * nb
    flat = random_blocks.reshape(requests)
    ids = jnp.broadcast_to(jnp.pad(flat, (0, 128 - requests))[None], (8, 128))
    pieces = min(4, 2 * width // 128)
    size = 2 * width // pieces
    blocked = (tokens // BLOCK, BLOCK, full)
    key_blocks, value_blocks = key_rows.reshape(blocked), value_rows.reshape(blocked)
    query_rows, key_blocks, value_blocks, out_grad = (
        pltpu.with_memory_space_constraint(x, pltpu.HBM)
        for x in (query_rows, key_blocks, value_blocks, out_grad)
    )
    first, ids_all = pl.pallas_call(
        partial(kernel_in, n, heads, size),
        out_shape=(sds((nb, BLOCK, size), bf), sds((n, 8, 128), jnp.int32)),
        in_specs=[HBM, VMEM],
        out_specs=(VMEM,) * 2,
        scratch_shapes=[dma((heads,)), dma((heads,)), dma((2,)), dma((n,)), dma((n,))],
        compiler_params=params(0),
        name="head_in",
    )(key_blocks, ids)
    asked = ids_all[:, 0, :requests]
    served = jnp.sum(jnp.where(asked // nb == me, asked % nb, 0), axis=1).astype(jnp.int32)
    owners = global_blocks // nb
    owned_at = global_blocks % nb
    ready = jnp.take(first, served, axis=0, mode="clip")
    group = 4
    layers = n // group
    chunk = GLOBALS * BLOCK // group
    slab = sds((n, BLOCK, 2 * width), bf)
    small = sds((group, chunk, 2 * width), bf)
    wide = (chunk, 2 * width)
    scratch = [
        pltpu.VMEM(small.shape, bf), pltpu.VMEM(wide, bf), pltpu.VMEM((layers,) + wide, bf),
        pltpu.VMEM(wide, bf),
        dma(((pieces + 2) * heads,)), dma(((pieces + 2) * heads,)), dma((pieces + 3,)),
        dma((pieces * n,)), dma((pieces * n,)), dma((2 * pieces,)), dma((2 * pieces,)),
        dma((group,)), dma((group,)), dma((layers,)), dma((layers,)), dma((group,)),
        dma((group,)), dma((1,)),
    ]
    edges = sds((2, BLOCK, 2 * width), bf)
    qh, gh, incoming, halos, gall, *landed = pl.pallas_call(
        partial(kernel_fetch, n, heads, pieces),
        out_shape=(sds((total, width), bf), sds((total, width), bf), slab, edges, small)
        + (sds((nb, BLOCK, size), bf),) * (pieces - 1),
        in_specs=[SMEM] * 3 + [HBM] * 4 + [VMEM] * 2,
        out_specs=(VMEM,) * (4 + pieces),
        scratch_shapes=[pltpu.VMEM((pieces - 1, n, BLOCK, size), bf), pltpu.VMEM(small.shape, bf)]
        + scratch,
        compiler_params=params(1),
        name="fetch",
    )(served, owners, owned_at, query_rows, out_grad, key_blocks, value_blocks, first, ready)
    gwide = (GLOBALS * BLOCK, 2 * width)
    att, qg, wsum, edge, sending, gsum = pl.pallas_call(
        partial(kernel_attend, n, min(256, width), pieces),
        out_shape=(
            sds((total, width), bf), sds((total, width), bf),
            sds(((nb + 2) * BLOCK, 2 * width), jnp.float32), edges, slab, sds(gwide, bf),
        ),
        in_specs=[SMEM] + [VMEM] * (5 + pieces),
        out_specs=(VMEM,) * 6,
        scratch_shapes=[
            pltpu.VMEM(((nb + 2) * BLOCK, 2 * width), bf),
            pltpu.VMEM((PARTS * BLOCK, 2 * width), bf),
            pltpu.VMEM(gwide, jnp.float32),
        ],
        compiler_params=pltpu.CompilerParams(vmem_limit_bytes=24 * 1024 * 1024),
        name="attend",
    )(flat // nb, qh, gh, halos, incoming, gall.reshape(gwide),
      *[x.reshape(total, size) for x in (first, *landed)])
    results = pl.pallas_call(
        partial(kernel_return, n, heads, pieces),
        out_shape=(sds((tokens, full), bf),) * 4,
        in_specs=[SMEM] * 3 + [VMEM] * 6,
        out_specs=(VMEM,) * 4,
        scratch_shapes=[
            pltpu.VMEM(slab.shape, bf), pltpu.VMEM(edges.shape, bf), pltpu.VMEM(small.shape, bf),
            pltpu.VMEM((total, 2 * width), bf),
        ] + scratch,
        compiler_params=params(2),
        name="give_back",
    )(served, owners, owned_at, att, qg, sending, edge, gsum.reshape(group, chunk, 2 * width),
      wsum)
    return pl.pallas_call(
        kernel_store,
        out_shape=(sds((tokens, full), bf),) * 4,
        in_specs=[VMEM] * 4,
        out_specs=(HBM,) * 4,
        scratch_shapes=[dma((4,))],
        compiler_params=pltpu.CompilerParams(vmem_limit_bytes=16 * 1024 * 1024),
        name="store",
    )(*results)


LANES = 128
WIDE = 2 * LANES


class Team:
    def __init__(self, n, heads, groups, tokens):
        self.n, self.heads, self.groups, self.tokens = n, heads, groups, tokens
        self.members = n // groups
        s, self.h = lax.axis_index("seq"), lax.axis_index("head")
        self.g, self.m = s // self.members, lax.rem(s, self.members)
        self.bits = [1 << i for i in reversed(range(self.members.bit_length() - 1))]
        self.places = [(i, d) for i in range(groups) for d in range(heads)]
        self.me = self.slot(self.g, self.h)

    def slot(self, g, h):
        return g * self.heads + h

    def near(self, i):
        total = self.g * 0
        for g in range(self.groups):
            order = sorted(range(self.groups), key=lambda k: (k != g, -abs(k - g), -abs(2 * k + 1 - self.groups)))
            total = total + jnp.where(self.g == g, order[i], 0)
        return total

    def place(self, j):
        if isinstance(j, int):
            i, d = self.places[j]
            return (self.near(i) if i else self.g), lax.rem(self.h + d, self.heads)
        g = self.g * 0
        for i in range(self.groups):
            g = g + jnp.where(j // self.heads == i, self.near(i), 0)
        return g, lax.rem(self.h + lax.rem(j, self.heads), self.heads)

    def device(self, g, h):
        return {"seq": g * self.members + self.m, "head": h}

    def mate(self, bit):
        return self.m ^ bit

    def mate_device(self, bit):
        return {"seq": self.g * self.members + self.mate(bit)}

    def chunk(self, g, h, m):
        return rows((g * self.members + m) * self.heads + h, self.tokens)

    def columns(self, g, h):
        return pl.ds(pl.multiple_of((h * self.groups + g) * LANES, LANES), LANES)

    def greet(self):
        barrier = pltpu.get_barrier_semaphore()
        for j in range(1, len(self.places)):
            pl.semaphore_signal(
                barrier, inc=1, device_id=self.device(*self.place(j)), device_id_type=MESH
            )
        for bit in self.bits:
            pl.semaphore_signal(
                barrier, inc=1, device_id=self.mate_device(bit), device_id_type=MESH
            )
        pl.semaphore_wait(barrier, len(self.places) - 1 + len(self.bits))


def send_to(src, dst, send, recv, device):
    return pltpu.make_async_remote_copy(
        src_ref=src, dst_ref=dst, send_sem=send, recv_sem=recv, device_id=device,
        device_id_type=MESH,
    )


def kernel_all(n, heads, groups, named_in, owners_in, key, value, query, grad, out, qout, kout, vout,
               kv, qd, od, acc, extra, keys, ids, ids_all, table, named, owners, part, inbox, sums, final, send, recv,
               local, fsend, frecv, isend, irecv, bsend, brecv, blocal, tsend, trecv):
    tokens = query.shape[0]
    t = Team(n, heads, groups, tokens)
    count = len(t.places)
    per_chunk = tokens // BLOCK
    run = heads * per_chunk
    requests = RANDOM * run
    blank = groups * requests + GLOBALS
    asks = [pltpu.make_async_copy(named_in, named, local.at[6]),
            pltpu.make_async_copy(owners_in, owners, local.at[7])]
    start(asks)
    t.greet()
    arrays = (key, value, query, grad)
    dests = (out, qout, kout, vout)

    def lanes(a):
        return pl.ds((a % 2) * LANES, LANES)

    def blocks_of(g, h, m):
        return pl.ds(((g * t.members + m) * heads + h) * per_chunk + 1, per_chunk)

    def leaving(a, g, h):
        ref = arrays[a]
        return ref.at[:, :, t.columns(g, h)] if a < 2 else ref.at[:, t.columns(g, h)]

    def landing(a, g, h):
        return (kv.at[blocks_of(g, h, t.m), :, lanes(a)] if a < 2
                else qd.at[rows(t.slot(g, h), tokens), lanes(a)])

    def move(a, j):
        g, h = t.place(j)
        return send_to(leaving(a, g, h), landing(a, t.g, t.h),
                       send.at[a * count + j], recv.at[a * count + t.me], t.device(g, h))

    def keep(a):
        return pltpu.make_async_copy(leaving(a, t.g, t.h), landing(a, t.g, t.h),
                                     local.at[a])

    def arrived(a, j):
        g, h = t.place(j)
        return send_to(leaving(a, g, h), landing(a, g, h),
                       send.at[a * count + j], recv.at[a * count + t.slot(g, h)],
                       t.device(g, h))

    idm = [send_to(ids, ids_all.at[t.g], isend.at[i], irecv.at[t.g], t.device(t.near(i), t.h))
           for i in range(1, groups)]
    idr = [send_to(ids, ids_all.at[t.near(i)], isend.at[i], irecv.at[t.near(i)],
                   t.device(t.near(i), t.h)) for i in range(1, groups)]
    for a in (0, 1):
        keep(a).start()
    for j in range(1, count):
        for a in (0, 1):
            move(a, j).start()
    wait(asks)
    lane = lax.broadcasted_iota(jnp.int32, ids.shape, 1)
    row = lax.broadcasted_iota(jnp.int32, ids.shape, 0)
    entry = jnp.where(row == 0, 0, blank)
    for r in range(requests):
        name = named[r % RANDOM, r // RANDOM]
        entry = jnp.where((row == 0) & (lane == r), name, entry)
        entry = jnp.where((row == 1) & (lane == name), t.g * requests + r, entry)
    for k in range(GLOBALS):
        entry = jnp.where((row == 2 + k) & (lane == owners[k]), groups * requests + k, entry)
    ids[...] = entry
    edge = jnp.zeros(kv.shape[1:], kv.dtype)
    kv[0] = edge
    kv[kv.shape[0] - 1] = edge
    empty = jnp.zeros((BLOCK, WIDE), jnp.float32)
    for k in range(GLOBALS + 1):
        extra[groups * requests + k] = empty

    def clear(i, carry):
        acc[rows(i, BLOCK)] = empty
        return carry

    lax.fori_loop(0, acc.shape[0] // BLOCK, clear, 0)
    start(idm)
    for a in (2, 3):
        keep(a).start()
    for j in range(1, count):
        for a in (2, 3):
            move(a, j).start()
    own = pltpu.make_async_copy(ids, ids_all.at[t.g], local.at[4])
    own.start()

    def forward(stage, mask, p, mine):
        bit = t.bits[stage]
        g, h = t.place(p // 2)
        owner = t.m ^ mask if mine else t.m ^ bit ^ mask
        ref = kv.at[blocks_of(g, h, owner), :, lanes(p)]
        at = (stage * t.members + mask) * 2 * count + p
        return send_to(ref, ref, fsend.at[at], frecv.at[at], t.mate_device(bit))

    def masks(stage):
        got = [0]
        for bit in t.bits[:stage]:
            got += [x ^ bit for x in got]
        return got

    stages = range(len(t.bits))
    pieces = 2 * count
    for step in range(pieces + 4 * len(t.bits)):
        for stage in reversed(stages):
            p = step - 4 * (stage + 1)
            if 0 <= p < pieces:
                for mask in masks(stage):
                    forward(stage, mask, p, False).wait_recv()
                    for later in range(stage + 1, len(t.bits)):
                        forward(later, mask ^ t.bits[stage], p, True).start()
        if step < pieces:
            if step < 2:
                keep(step).wait()
            else:
                arrived(step % 2, step // 2).wait_recv()
            for stage in stages:
                forward(stage, 0, step, True).start()
    own.wait()
    for c in idr:
        c.wait_recv()
    fill = pltpu.make_async_copy(ids_all, table, local.at[5])
    fill.start()
    fill.wait()

    per = LANES // HEAD_DIM
    scale = jnp.asarray(HEAD_DIM ** (-0.5), jnp.bfloat16)
    for k in range(GLOBALS):
        keys[3 + RANDOM + k] = kv[owners[k] + 1]
    lane_head = lax.broadcasted_iota(jnp.int32, (BLOCK, LANES), 1) // HEAD_DIM
    where = lax.broadcasted_iota(jnp.int32, (PARTS * BLOCK, 1), 0) // BLOCK
    at, vat = lanes(0), lanes(1)

    def stack(x):
        zero = jnp.zeros_like(x)
        return jnp.concatenate([jnp.where(lane_head == j, x, zero) for j in range(per)], axis=0)

    def unstack(x):
        got = x[0:BLOCK]
        for j in range(1, per):
            got = jnp.where(lane_head == j, x[j * BLOCK : (j + 1) * BLOCK], got)
        return got

    def chunk(j):
        g, h = t.place(j)
        slot = t.slot(g, h)
        first = ((g * t.members + t.m) * heads + h) * per_chunk

        def block(b, carry):
            here = rows(slot * per_chunk + b, BLOCK)
            number = first + b
            window = pl.ds(pl.multiple_of(number * BLOCK, BLOCK), 3 * BLOCK)
            keys[pl.ds(0, 3)] = kv[pl.ds(number, 3)]
            spot = (h * per_chunk + b) * RANDOM
            for r in range(RANDOM):
                keys[3 + r] = kv[table[g, 0, spot + r] + 1]
            bad = ((where == 0) & (number == 0)) | ((where == 2) & (number == n * run - 1))
            q = stack(qd[here, at]) * scale
            do = stack(qd[here, vat])
            k = keys[:, :, at].reshape(PARTS * BLOCK, LANES)
            v = keys[:, :, vat].reshape(PARTS * BLOCK, LANES)
            scores = jnp.where(bad, MASKED, dot(k, q, 1, 1))
            raw = jnp.exp(scores - jnp.max(scores, axis=0, keepdims=True))
            probs = raw * (1.0 / jnp.sum(raw, axis=0, keepdims=True))
            half = probs.astype(jnp.bfloat16)
            pgrad = dot(v, do, 1, 1)
            delta = jnp.sum(half.astype(jnp.float32) * pgrad, axis=0, keepdims=True)
            ds = (probs * (pgrad - delta)).astype(jnp.bfloat16)
            od[here, at] = unstack(dot(half, v, 0, 0)).astype(jnp.bfloat16)
            od[here, vat] = (unstack(dot(ds, k, 0, 0)) * HEAD_DIM ** (-0.5)).astype(jnp.bfloat16)
            for x, y, to in ((ds, q, at), (half, do, vat)):
                got = dot(x, y, 1, 0)
                acc[window, to] += got[: 3 * BLOCK]
                for r in range(RANDOM):
                    low = (3 + r) * BLOCK
                    extra[g * requests + spot + r, :, to] = got[low : low + BLOCK]
                for k2 in range(GLOBALS):
                    low = (3 + RANDOM + k2) * BLOCK
                    extra[groups * requests + k2, :, to] += got[low : low + BLOCK]
            return carry

        lax.fori_loop(0, per_chunk, block, 0, unroll=2)

    mine = t.columns(t.g, t.h)

    def source(a, j):
        g, h = t.place(j)
        return (od.at[rows(t.slot(g, h), tokens), lanes(a)] if a < 2
                else final.at[rows(j, tokens), lanes(a)])

    def back(a, j):
        g, h = t.place(j)
        return send_to(source(a, j), dests[a].at[:, mine], bsend.at[a * count + j],
                       brecv.at[a * count + t.me], t.device(g, h))

    def back_keep(a):
        return pltpu.make_async_copy(source(a, 0), dests[a].at[:, mine], blocal.at[a])

    def returned(a, j):
        g, h = t.place(j)
        return send_to(source(a, j), dests[a].at[:, t.columns(g, h)], bsend.at[a * count + j],
                       brecv.at[a * count + t.slot(g, h)], t.device(g, h))

    for a in (2, 3):
        keep(a).wait()
    chunk(0)
    for a in (0, 1):
        back_keep(a).start()

    def one(j, carry):
        for a in (2, 3):
            arrived(a, j).wait_recv()
        chunk(j)
        for a in (0, 1):
            back(a, j).start()
        return carry

    lax.fori_loop(1, count, one, 0)

    order = list(reversed(t.bits))
    handed = []
    held = list(range(t.members))
    for bit in order:
        handed.append([x for x in held if x & bit])
        held = [x for x in held if not x & bit]
    boxes = [(stage, mask) for stage in range(len(order)) for mask in handed[stage]]

    def box(stage, mask, j):
        return rows(boxes.index((stage, mask)) * count + j, tokens)

    def trade(stage, mask, j):
        at = (stage * t.members + mask) * count + j
        if stage == 0:
            src = part.at[rows(handed[0].index(mask) * count + j, tokens)]
        else:
            src = sums.at[rows((stage - 1) * count + j, tokens)]
        return send_to(src, inbox.at[box(stage, mask, j)], tsend.at[at], trecv.at[at],
                       t.mate_device(order[stage]))

    def total(ref, base, mask, j, upto):
        g, h = t.place(j)
        lows = [(boxes.index((stage, mask ^ order[stage])) * count + j) * per_chunk
                for stage in range(upto)]
        first = ((g * t.members + (t.m ^ mask)) * heads + h) * per_chunk

        def strip(b, carry):
            x = acc[rows(first + b + 1, BLOCK)]
            for q in range(groups):
                x = x + extra[table[q, 1, first + b]]
            for k in range(GLOBALS):
                x = x + extra[table[0, 2 + k, first + b]]
            for low in lows:
                x = x + inbox[rows(low + b, BLOCK)].astype(jnp.float32)
            ref[rows(base * per_chunk + b, BLOCK)] = x.astype(jnp.bfloat16)
            return carry

        lax.fori_loop(0, per_chunk, strip, 0)

    js = list(range(1, count)) + [0]
    def hand(mask, j):
        total(part, handed[0].index(mask) * count + j, mask, j, 0)
        trade(0, mask, j).start()

    def relay(stage, j):
        for mask in handed[stage]:
            for before in range(stage):
                trade(before, mask ^ order[before], j).wait_recv()
            total(sums, (stage - 1) * count + j, mask, j, stage)
            trade(stage, mask, j).start()

    early = [x for x in handed[0] if x & ~order[0]]
    late = [x for x in handed[0] if not x & ~order[0]]
    for i in range(count + 2):
        if i < count:
            for mask in early:
                hand(mask, js[i])
        if i >= 2:
            for stage in range(1, len(order)):
                relay(stage, js[i - 2])
            for mask in late:
                hand(mask, js[i - 2])
    for j in js:
        for stage in range(len(order)):
            trade(stage, order[stage], j).wait_recv()
        total(final, j, 0, j, len(order))
        for a in (2, 3):
            (back(a, j) if j else back_keep(a)).start()
    for stage in stages:
        for mask in masks(stage):
            for p in range(2 * count):
                forward(stage, mask, p, True).wait_send()
        for mask in handed[stage]:
            for j in js:
                trade(stage, mask, j).wait_send()
    for c in idm:
        c.wait_send()
    for a in range(4):
        back_keep(a).wait()
        for j in range(1, count):
            move(a, j).wait_send()
            back(a, j).wait_send()
            returned(a, j).wait_recv()


def grouped(n, heads, groups, query_rows, key_rows, value_rows, out_grad, random_blocks,
            global_blocks):
    bf = jnp.bfloat16
    tokens, full = query_rows.shape
    members = n // groups
    count = groups * heads
    everything = n * heads * tokens
    held = count * tokens
    bits = members.bit_length() - 1
    run = heads * tokens // BLOCK
    requests = RANDOM * run
    dma = pltpu.SemaphoreType.DMA
    sds = jax.ShapeDtypeStruct
    total = n * run
    span = -(-max(total, requests) // 128) * 128
    picked = pltpu.with_memory_space_constraint(random_blocks.T, pltpu.HBM)
    shared = pltpu.with_memory_space_constraint(global_blocks, pltpu.HBM)
    blocked = (tokens // BLOCK, BLOCK, full)
    key_rows, value_rows = key_rows.reshape(blocked), value_rows.reshape(blocked)
    query_rows, key_rows, value_rows, out_grad = (
        pltpu.with_memory_space_constraint(x, pltpu.HBM)
        for x in (query_rows, key_rows, value_rows, out_grad)
    )
    f32 = jnp.float32
    results = pl.pallas_call(
        partial(kernel_all, n, heads, groups),
        out_shape=(sds((tokens, full), bf),) * 4,
        in_specs=[HBM] * 6,
        out_specs=(VMEM,) * 4,
        scratch_shapes=[
            pltpu.VMEM((total + 2, BLOCK, WIDE), bf), pltpu.VMEM((held, WIDE), bf),
            pltpu.VMEM((held, WIDE), bf), pltpu.VMEM((everything + 2 * BLOCK, WIDE), f32),
            pltpu.VMEM((groups * requests + GLOBALS + 1, BLOCK, WIDE), f32),
            pltpu.VMEM((PARTS, BLOCK, WIDE), bf), pltpu.VMEM((8, span), jnp.int32),
            pltpu.VMEM((groups, 8, span), jnp.int32),
            pltpu.SMEM((groups, 8, span), jnp.int32),
            pltpu.SMEM((RANDOM, run), jnp.int32), pltpu.SMEM((GLOBALS,), jnp.int32),
            pltpu.VMEM((members // 2 * held, WIDE), bf),
            pltpu.VMEM(((members - 1) * held, WIDE), bf),
            pltpu.VMEM((max(bits - 1, 1) * held, WIDE), bf), pltpu.VMEM((held, WIDE), bf),
            dma((4 * count,)), dma((4 * count,)), dma((8,)),
            dma((2 * bits * members * count,)), dma((2 * bits * members * count,)),
            dma((groups,)), dma((groups,)),
            dma((4 * count,)), dma((4 * count,)), dma((4,)),
            dma((bits * members * count,)), dma((bits * members * count,)),
        ],
        compiler_params=pltpu.CompilerParams(
            collective_id=0, has_side_effects=True, vmem_limit_bytes=44 * 1024 * 1024
        ),
        name="everything",
    )(picked, shared, key_rows, value_rows, query_rows, out_grad)
    return pl.pallas_call(
        kernel_store,
        out_shape=(sds((tokens, full), bf),) * 4,
        in_specs=[VMEM] * 4,
        out_specs=(HBM,) * 4,
        scratch_shapes=[dma((4,))],
        compiler_params=pltpu.CompilerParams(vmem_limit_bytes=16 * 1024 * 1024),
        name="store",
    )(*results)


def chosen(n, heads, query_rows, *others):
    tokens, full = query_rows.shape
    groups = full // LANES // heads
    fits = n * heads * tokens * WIDE * 6 <= 24 * 1024 * 1024
    if full % (LANES * heads) == 0 and n % groups == 0 and fits and n // groups in (2, 4):
        return grouped(n, heads, groups, query_rows, *others)
    return body(n, heads, query_rows, *others)


def solution(mesh):
    rows_spec = P(("seq", "head"), None)
    return jax.shard_map(
        partial(chosen, mesh.shape["seq"], mesh.shape["head"]),
        mesh=mesh,
        in_specs=(rows_spec,) * 4 + (P("seq", None), P()),
        out_specs=(rows_spec,) * 4,
        check_vma=False,
    )
```
